32 devices in a mesh: fsdp: 8 (over z, x), tp: 4 (over y, core).
Axes of the slice: x: 2, y: 2, z: 4, core: 2. Of those that a mesh axis runs over, the one named last changes fastest.
Arguments:
- block_in: bfloat16 [3, 4096, 2048], P(None, ('fsdp', 'tp')), may hold values from -6 to 6
- span_start: int32 [3, 8], P(None, 'fsdp'), may hold values from 0 to 256
- w_query: bfloat16 [2048, 2048], P('fsdp', 'tp'), may hold values from -0.25 to 0.25
- w_key: bfloat16 [2048, 256], P('fsdp', 'tp'), may hold values from -0.125 to 0.125
- w_value: bfloat16 [2048, 256], P('fsdp', 'tp'), may hold values from -0.125 to 0.125
- w_out: bfloat16 [2048, 2048], P('tp', 'fsdp'), may hold values from -1.5 to 1.5
- w_gate: bfloat16 [2048, 5632], P('fsdp', 'tp'), may hold values from -0.125 to 0.125
- w_up: bfloat16 [2048, 5632], P('fsdp', 'tp'), may hold values from -0.125 to 0.125
- w_down: bfloat16 [5632, 2048], P('tp', 'fsdp'), may hold values from -0.078125 to 0.078125
- gain_attn: bfloat16 [2048], P('fsdp'), may hold values from 0.099609375 to 1.8984375
- gain_mlp: bfloat16 [2048], P('fsdp'), may hold values from 0.099609375 to 1.8984375
- cotangent: bfloat16 [3, 4096, 2048], P(None, ('fsdp', 'tp')), may hold values from -6 to 6
Outputs:
- block_out: float32 [3, 4096, 2048], P(None, ('fsdp', 'tp'))
- grad_in: float32 [3, 4096, 2048], P(None, ('fsdp', 'tp'))
- grad_query: float32 [2048, 2048], P('fsdp', 'tp')
- grad_key: float32 [2048, 256], P('fsdp', 'tp')
- grad_value: float32 [2048, 256], P('fsdp', 'tp')
- grad_out: float32 [2048, 2048], P('tp', 'fsdp')
- grad_gate: float32 [2048, 5632], P('fsdp', 'tp')
- grad_up: float32 [2048, 5632], P('fsdp', 'tp')
- grad_down: float32 [5632, 2048], P('tp', 'fsdp')
- grad_gain_attn: float32 [2048], P('fsdp')
- grad_gain_mlp: float32 [2048], P('fsdp')
The draws below stay inside these ranges and needn't reach their ends.
Inputs may be any that keep to these rules, and one draw needn't show every extreme that they name: A sequence's image span covers positions span_start to span_start + 255.
All inputs are finite; a program needn't handle non-finite values.
Results may differ from the reference program's by a relative error of at most 0.018.
Values may be sent and summed in bfloat16 or wider, within the bound.
No kernel may reach another device: no remote copies, remote signals or barrier semaphores. Data moves between devices by JAX's collectives and lax.ppermute only.
A program may use at most 256 MiB of HBM per device.

```python
import math
import jax
import jax.numpy as jnp
from jax import lax

D = 2048
H = 32
KVH = 4
HD = 64
FF = 5632
SEQ = 512
SPAN = 256
MICRO = 3
TOK = 4096
N_FSDP = 8


def set_ends(entries, key, smallest, high):
    place = [jax.random.randint(jax.random.fold_in(key, axis), (), 0, length) for axis, length in enumerate(entries.shape)]
    main_axis = entries.shape.index(max(entries.shape))
    beside = place[:main_axis] + [(place[main_axis] + 1) % entries.shape[main_axis]] + place[main_axis + 1:]
    return entries.at[tuple(place)].set(smallest).at[tuple(beside)].set(high)


def block_levels(stream_key, extent, cuts, low, high):
    factor_of = 1.0
    for axis_at, parts in cuts:
        heights = jax.random.uniform(jax.random.fold_in(jax.random.fold_in(stream_key, 6), axis_at), (parts,), jnp.float32, low / len(cuts), high / len(cuts))
        factor_of = factor_of * jnp.repeat(jnp.exp(heights), extent[axis_at] // parts).reshape((-1,) + (1,) * (len(extent) - 1 - axis_at))
    return factor_of


def scatter_about(stream_key, dims, deviation, reach, cuts=(), held_as=jnp.bfloat16):
    gain = block_levels(stream_key, dims, cuts, -0.22, 0.18) if cuts else 1.0
    entries = jax.random.normal(stream_key, dims, jnp.float32) * deviation * gain
    return jnp.minimum(jnp.maximum(entries, -reach), reach).astype(held_as)


def setup_inputs(seed: int = 0) -> dict:
    key_of = jax.random.split(jax.random.key(seed), 13)
    return {
        "block_in": scatter_about(key_of[0], (MICRO, TOK, D), 1.0, 6.0, ((1, 32),)),
        "span_start": set_ends(jax.random.randint(key_of[1], (MICRO, N_FSDP), 0, SEQ - SPAN + 1), jax.random.fold_in(key_of[1], 1), 0, SEQ - SPAN).astype(jnp.int32),
        "w_query": scatter_about(key_of[2], (D, H * HD), (D // 4) ** -0.5, 0.25, ((0, 8), (1, 4))),
        "w_key": scatter_about(key_of[3], (D, KVH * HD), D ** -0.5, 0.125, ((0, 8), (1, 4))),
        "w_value": scatter_about(key_of[4], (D, KVH * HD), D ** -0.5, 0.125, ((0, 8), (1, 4))),
        "w_out": scatter_about(key_of[5], (H * HD, D), 16 ** -0.5, 1.5, ((0, 4), (1, 8))),
        "w_gate": scatter_about(key_of[6], (D, FF), D ** -0.5, 0.125, ((0, 8), (1, 4))),
        "w_up": scatter_about(key_of[7], (D, FF), D ** -0.5, 0.125, ((0, 8), (1, 4))),
        "w_down": scatter_about(key_of[8], (FF, D), FF ** -0.5, 0.078125, ((0, 4), (1, 8))),
        "gain_attn": jnp.clip(1.0 + 0.18 * jax.random.normal(key_of[9], (D,), jnp.float32), 0.099609375, 1.8984375).astype(jnp.bfloat16),
        "gain_mlp": jnp.clip(1.0 + 0.18 * jax.random.normal(key_of[10], (D,), jnp.float32), 0.099609375, 1.8984375).astype(jnp.bfloat16),
        "cotangent": scatter_about(key_of[11], (MICRO, TOK, D), 1.0, 6.0, ((1, 32),)),
    }


epsilon = 1e-05
masked_value = -1e+30

@jax.custom_vjp
def low(v):
    return lax.optimization_barrier(v.astype(jnp.bfloat16)).astype(jnp.float32)

@jax.custom_vjp
def low_back(v):
    return v

def low_keep(v):
    return (low(v), None)

def low_pass(kept, grad):
    return (grad,)

def back_keep(v):
    return (v, None)

def back_low(kept, grad):
    return (low(grad),)
low.defvjp(low_keep, low_pass)
low_back.defvjp(back_keep, back_low)

def angle_tables(length, width):
    half_width = width // 2
    frequency = jnp.exp(jnp.arange(half_width, dtype=jnp.float32) * (-2.0 * math.log(10000.0) / width))
    places = jnp.arange(length, dtype=jnp.float32)
    angles = places[:, None] * frequency[None, :]
    angles = jnp.concatenate([angles, angles], axis=1)
    return (jnp.cos(angles)[:, None, :], jnp.sin(angles)[:, None, :])

def rotate(values, cos_table, sine_table):
    half_width = values.shape[-1] // 2
    turned = jnp.concatenate([-values[..., half_width:], values[..., :half_width]], axis=-1)
    return values * cos_table + turned * sine_table

def visible_mask(length, span_first):
    places = jnp.arange(length, dtype=jnp.int32)
    inside = (places >= span_first) & (places < span_first + SPAN)
    return (places[:, None] >= places[None, :]) | inside[:, None] & inside[None, :]

def highest(left_side, right_side):
    return jnp.dot(left_side, right_side, precision=lax.Precision.HIGHEST)

def attend(pieces):
    query_rot, key_rot, value_low, span_first = pieces
    group_size = H // KVH
    query_grp = query_rot.reshape(SEQ, KVH, group_size, HD)
    scores = jnp.einsum('qgrd,sgd->grqs', query_grp, key_rot, precision=lax.Precision.HIGHEST)
    scores = HD ** (-0.5) * low_back(scores)
    scores = jnp.where(visible_mask(SEQ, span_first), scores, masked_value)
    row_max = lax.optimization_barrier(jnp.max(scores, axis=-1, keepdims=True))
    raised = jnp.exp(scores - row_max)
    weights_p = low(raised / lax.optimization_barrier(jnp.sum(raised, axis=-1, keepdims=True)))
    mixed_low = jnp.einsum('grqs,sgd->qgrd', weights_p, value_low, precision=lax.Precision.HIGHEST)
    return mixed_low.reshape(SEQ, H * HD)

def forward(block_in, w_query, w_key, w_value, w_out, w_gate, w_up, w_down, gain_attn, gain_mlp, span_start):
    tokens = block_in.reshape(-1, D)
    count_seq = tokens.shape[0] // SEQ
    scale_one = lax.rsqrt(lax.optimization_barrier(jnp.mean(tokens * tokens, axis=-1, keepdims=True)) + epsilon)
    normed_one = low(tokens * scale_one * gain_attn)
    cos_table, sine_table = angle_tables(SEQ, HD)
    query_raw = low_back(highest(normed_one, w_query)).reshape(count_seq, SEQ, H, HD)
    key_raw = low_back(highest(normed_one, w_key)).reshape(count_seq, SEQ, KVH, HD)
    value_low = low(low_back(highest(normed_one, w_value))).reshape(count_seq, SEQ, KVH, HD)
    query_rot = low(rotate(query_raw, cos_table, sine_table))
    key_rot = low(rotate(key_raw, cos_table, sine_table))
    mixed_all = lax.map(jax.checkpoint(attend), (query_rot, key_rot, value_low, span_start.reshape(-1)))
    mixed_all = low(low_back(mixed_all.reshape(-1, H * HD)))
    hidden_res = tokens + low_back(highest(mixed_all, w_out))
    scale_two = lax.rsqrt(lax.optimization_barrier(jnp.mean(hidden_res * hidden_res, axis=-1, keepdims=True)) + epsilon)
    normed_two = low(hidden_res * scale_two * gain_mlp)
    gate_pre = low_back(highest(normed_two, w_gate))
    up_pre = low_back(highest(normed_two, w_up))
    inner_low = low(jax.nn.silu(gate_pre) * up_pre)
    block_out = hidden_res + low_back(highest(inner_low, w_down))
    return block_out.reshape(block_in.shape)

def reference(block_in, span_start, w_query, w_key, w_value, w_out, w_gate, w_up, w_down, gain_attn, gain_mlp, cotangent):
    floats = tuple((array_in.astype(jnp.float32) for array_in in (block_in, w_query, w_key, w_value, w_out, w_gate, w_up, w_down, gain_attn, gain_mlp)))

    def closed_form(*arrays):
        return forward(*arrays, span_start)
    block_out, pullback = jax.vjp(closed_form, *floats)
    gradients = pullback(cotangent.astype(jnp.float32))
    return (block_out, gradients[0], gradients[1], gradients[2], gradients[3], gradients[4], gradients[5], gradients[6], gradients[7], gradients[8], gradients[9])
```

```python
import functools
import math

import jax
import jax.numpy as jnp
from jax import lax
from jax.experimental import pallas as pl
from jax.experimental.pallas import tpu as pltpu
from jax.sharding import Mesh, PartitionSpec as P

HD = 64
PAIR = 2 * HD
SPAN = 256
EPS = 1e-05
MASKED = -1e30
F32 = jnp.float32
BF16 = jnp.bfloat16
SWAP = [(0, 1), (1, 0)]
ROW_PAD = 16


def dot(a, b):
    return jnp.dot(a, b, preferred_element_type=F32)


def dot_lt(a, b):
    return lax.dot_general(a, b, (((0,), (0,)), ((), ())), preferred_element_type=F32)


def dot_rt(a, b):
    return lax.dot_general(a, b, (((1,), (1,)), ((), ())), preferred_element_type=F32)


def swap(value, axis):
    return lax.ppermute(value, axis, SWAP)


def after(value, *others):
    return lax.optimization_barrier((value, *others))[0]


def both_after(pair, *others):
    kept = lax.optimization_barrier((*pair, *others))
    return kept[0], kept[1]


def full_spec(shape):
    return pl.BlockSpec(shape, lambda i, *_: (0,) * len(shape))


def row_spec(rows, cols, offset=0):
    return pl.BlockSpec((rows, cols), lambda i, *_: (i + offset, 0))


def quad_spec(rows, cols):
    return pl.BlockSpec((4, 1, rows, cols), lambda i, *_: (0, i, 0, 0))


def call(kernel, scalars, grid, ins, outs, scratch=(), flops=0, exps=0):
    moved = sum(a.size * a.dtype.itemsize for a, _ in ins)
    moved += sum(math.prod(shape) * jnp.dtype(kind).itemsize for shape, kind, _ in outs)
    return pl.pallas_call(
        kernel,
        out_shape=[jax.ShapeDtypeStruct(shape, kind) for shape, kind, _ in outs],
        grid_spec=pltpu.PrefetchScalarGridSpec(
            num_scalar_prefetch=len(scalars),
            grid=(grid,),
            in_specs=[spec for _, spec in ins],
            out_specs=[spec for _, _, spec in outs],
            scratch_shapes=list(scratch),
        ),
        cost_estimate=pl.CostEstimate(flops=flops, bytes_accessed=moved, transcendentals=exps),
        compiler_params=pltpu.CompilerParams(vmem_limit_bytes=56 << 20),
    )(*scalars, *[a for a, _ in ins])


def halves_of(value, hi, x):
    width = value.shape[-1] // (2 * hi)
    parts = [value[:, k * width : (k + 1) * width] for k in range(2 * hi)]
    even, odd = parts[0::2], parts[1::2]
    own = [jnp.where(x == 0, a, b) for a, b in zip(even, odd)]
    oth = [jnp.where(x == 0, b, a) for a, b in zip(even, odd)]
    return own, oth


def put_cols(ref, index, parts):
    width = parts[0].shape[-1]
    for k, part in enumerate(parts):
        ref[(*index, slice(None), slice(k * width, (k + 1) * width))] = part.astype(ref.dtype)


def join_to(ref, own, oth, hi, x):
    width = own.shape[-1] // hi
    for k in range(hi):
        a, b = own[:, k * width : (k + 1) * width], oth[:, k * width : (k + 1) * width]
        ref[:, 2 * k * width : (2 * k + 1) * width] = jnp.where(x == 0, a, b)
        ref[:, (2 * k + 1) * width : (2 * k + 2) * width] = jnp.where(x == 0, b, a)


def norm_in_kernel(hi, at, p0, p1, p2, p3, gain_own, gain_oth, n_own, n_oth, x_own, x_oth):
    x = at[0]
    half = n_own.shape[-1]
    for k, piece in enumerate((p0, p1, p2, p3)):
        low = piece[...]
        value = low.astype(F32)
        scale = lax.rsqrt(jnp.mean(value * value, axis=-1, keepdims=True) + EPS)
        own, oth = halves_of(value, hi, x)
        width = half // hi
        for part, gain, ref in ((own, gain_own, n_own), (oth, gain_oth, n_oth)):
            put_cols(
                ref, (k, 0), [v * scale * gain[:, z * width : (z + 1) * width] for z, v in enumerate(part)]
            )
        if k == 0:
            put_cols(x_own, (), own)
            put_cols(x_oth, (), oth)


def spread_kernel(hi, at, p0, p1, p2, p3, o_own, o_oth):
    x = at[0]
    for k, piece in enumerate((p0, p1, p2, p3)):
        own, oth = halves_of(piece[...], hi, x)
        put_cols(o_own, (k, 0), own)
        put_cols(o_oth, (k, 0), oth)


def stack_kernel(p0, p1, p2, p3, o_own, o_oth):
    half = o_own.shape[-1]
    for k, piece in enumerate((p0, p1, p2, p3)):
        o_own[k, 0] = piece[:, :half]
        o_oth[k, 0] = piece[:, half:]


def rows_scale(own, oth):
    total = jnp.sum(own * own, axis=-1, keepdims=True) + jnp.sum(oth * oth, axis=-1, keepdims=True)
    return lax.rsqrt(total / (own.shape[-1] + oth.shape[-1]) + EPS)


def summed(refs):
    return refs[0][...].astype(F32) + refs[1][...].astype(F32) + refs[2][...].astype(F32)


def residual_kernel(x_own, x_oth, a0, a1, a2, b0, b1, b2, gain_own, gain_oth, h_own, h_oth, n_out):
    own = x_own[...].astype(F32) + summed((a0, a1, a2))
    oth = x_oth[...].astype(F32) + summed((b0, b1, b2))
    scale = rows_scale(own, oth)
    half = own.shape[-1]
    h_own[...] = own
    h_oth[...] = oth
    n_out[:, :half] = (own * scale * gain_own[...]).astype(BF16)
    n_out[:, half:] = (oth * scale * gain_oth[...]).astype(BF16)


def block_out_kernel(hi, at, h_own, h_oth, a0, a1, a2, b0, b1, b2, out):
    join_to(out, h_own[...] + summed((a0, a1, a2)), h_oth[...] + summed((b0, b1, b2)), hi, at[0])


def back_of(own, oth, scale, gain_own, gain_oth, up_own, up_oth):
    w_own, w_oth = up_own * gain_own, up_oth * gain_oth
    total = jnp.sum(w_own * own, axis=-1, keepdims=True) + jnp.sum(w_oth * oth, axis=-1, keepdims=True)
    cube = scale * scale * scale * (total / (own.shape[-1] + oth.shape[-1]))
    return scale * w_own - own * cube, scale * w_oth - oth * cube


def middle_kernel(
    h_own, h_oth, a0, a1, a2, b0, b1, b2, gain_own, gain_oth, u_own, u_oth, r_own, r_oth, low_out, s_own, s_oth
):
    own, oth = h_own[...], h_oth[...]
    up_own, up_oth = summed((a0, a1, a2)), summed((b0, b1, b2))
    scale = rows_scale(own, oth)
    back_own, back_oth = back_of(own, oth, scale, gain_own[...], gain_oth[...], up_own, up_oth)
    back_own = u_own[...].astype(F32) + back_own
    back_oth = u_oth[...].astype(F32) + back_oth
    half = own.shape[-1]
    r_own[...] = back_own
    r_oth[...] = back_oth
    low_out[:, :half] = back_own.astype(BF16)
    low_out[:, half:] = back_oth.astype(BF16)

    @pl.when(pl.program_id(0) == 0)
    def _():
        s_own[...] = jnp.zeros_like(s_own)
        s_oth[...] = jnp.zeros_like(s_oth)

    s_own[...] += jnp.sum(up_own * own * scale, axis=0, keepdims=True)
    s_oth[...] += jnp.sum(up_oth * oth * scale, axis=0, keepdims=True)


def grad_in_kernel(hi, at, x_own, x_oth, a0, a1, a2, b0, b1, b2, gain_own, gain_oth, r_own, r_oth, out):
    own, oth = x_own[...].astype(F32), x_oth[...].astype(F32)
    scale = rows_scale(own, oth)
    back_own, back_oth = back_of(
        own, oth, scale, gain_own[...], gain_oth[...], summed((a0, a1, a2)), summed((b0, b1, b2))
    )
    join_to(out, r_own[...] + back_own, r_oth[...] + back_oth, hi, at[0])


def partner(value):
    lane = lax.broadcasted_iota(jnp.int32, value.shape, 1)
    return jnp.where(lane % HD < HD // 2, pltpu.roll(value, PAIR - HD // 2, 1), pltpu.roll(value, HD // 2, 1))


def low_lanes(shape):
    return lax.broadcasted_iota(jnp.int32, shape, 1) < HD


def set_bias(bias, key_at, query_at, first):
    keys, queries = key_at[...], query_at[...]
    key_in = ((keys >= first) & (keys < first + SPAN)).astype(jnp.int32)
    query_in = ((queries >= first) & (queries < first + SPAN)).astype(jnp.int32)
    seen = (keys <= queries).astype(jnp.int32) + key_in * query_in
    bias[...] = jnp.where(seen > 0, 0.0, MASKED)


def attend_kernel(pairs, span, qkv, cos, sine, key_at, query_at, q_out, kv_out, o_out, lse_out, bias, key_s, val_s):
    length = cos.shape[0]
    set_bias(bias, key_at, query_at, span[pl.program_id(0)])
    kv = qkv[:, 0, :, pairs * PAIR :].reshape(length, PAIR)
    low = low_lanes(kv.shape)
    turned = kv * cos[...] + partner(kv) * sine[...]
    kv = jnp.where(low, turned, kv).astype(BF16)
    kv_out[:, 0] = kv.reshape(4, length // 4, PAIR)
    wide = kv.astype(F32)
    key_even = jnp.where(low, wide, 0.0)
    val_odd = jnp.where(low, 0.0, wide)
    key_s[0] = key_even.astype(BF16)
    key_s[1] = pltpu.roll(key_even, HD, 1).astype(BF16)
    val_s[0] = pltpu.roll(val_odd, HD, 1).T.astype(BF16)
    val_s[1] = val_odd.T.astype(BF16)

    def pair_step(j, _):
        cols = pl.ds(pl.multiple_of(j * PAIR, PAIR), PAIR)
        raw = qkv[:, 0, :, cols].reshape(length, PAIR)
        query = (raw * cos[...] + partner(raw) * sine[...]).astype(BF16)
        q_out[:, 0, :, cols] = query.reshape(4, length // 4, PAIR)
        query_t = (query.astype(F32) * HD**-0.5).T.astype(BF16)
        mixed = jnp.zeros((PAIR, length), F32)
        for k in range(2):
            scores = dot(key_s[k], query_t) + bias[...]
            top = jnp.max(scores, axis=0, keepdims=True)
            raised = jnp.exp(scores - top)
            total = jnp.sum(raised, axis=0, keepdims=True)
            lse_out[0, pl.ds(2 * j + k, 1), :] = top + jnp.log(total)
            mixed += dot(val_s[k], (raised * (1.0 / total)).astype(BF16))
        o_out[:, 0, :, cols] = mixed.T.astype(BF16).reshape(4, length // 4, PAIR)
        return 0

    lax.fori_loop(0, pairs, pair_step, 0)


def attend_back_kernel(
    pairs, span, query_in, kv_in, grad_in, lse, cos, sine, key_at, query_at, out, bias, key_s, key_t, val_s, key_g, val_g
):
    length = cos.shape[0]
    set_bias(bias, key_at, query_at, span[pl.program_id(0)])
    kv = kv_in[:, 0].reshape(length, PAIR).astype(F32)
    low = low_lanes(kv.shape)
    key_even = jnp.where(low, kv, 0.0)
    key_odd = pltpu.roll(key_even, HD, 1)
    val_odd = jnp.where(low, 0.0, kv)
    key_s[0] = key_even.astype(BF16)
    key_s[1] = key_odd.astype(BF16)
    key_t[0] = key_even.T.astype(BF16)
    key_t[1] = key_odd.T.astype(BF16)
    val_s[0] = pltpu.roll(val_odd, HD, 1).astype(BF16)
    val_s[1] = val_odd.astype(BF16)
    key_g[...] = jnp.zeros_like(key_g)
    val_g[...] = jnp.zeros_like(val_g)

    def pair_step(j, _):
        cols = pl.ds(pl.multiple_of(j * PAIR, PAIR), PAIR)
        query = query_in[:, 0, :, cols].reshape(length, PAIR)
        grad = grad_in[:, 0, :, cols].reshape(length, PAIR)
        query_t = (query.astype(F32) * HD**-0.5).T.astype(BF16)
        grad_t = grad.astype(F32).T.astype(BF16)
        query_g = jnp.zeros((PAIR, length), F32)
        for k in range(2):
            scores = dot(key_s[k], query_t) + bias[...]
            weight = jnp.exp(scores - lse[0, pl.ds(2 * j + k, 1), :])
            weight_g = dot(val_s[k], grad_t)
            val_g[k] += dot(weight.astype(BF16), grad)
            delta = jnp.sum(weight * weight_g, axis=0, keepdims=True)
            score_g = (HD**-0.5 * (weight * (weight_g - delta))).astype(BF16)
            key_g[k] += dot(score_g, query)
            query_g += dot(key_t[k], score_g)
        value = query_g.T
        value = value * cos[...] - partner(value) * sine[...]
        out[:, 0, :, cols] = value.astype(BF16).reshape(4, length // 4, PAIR)
        return 0

    lax.fori_loop(0, pairs, pair_step, 0)
    keys = key_g[0] + pltpu.roll(key_g[1], HD, 1)
    vals = val_g[1] + pltpu.roll(val_g[0], HD, 1)
    keys = keys * cos[...] - partner(keys) * sine[...]
    out[:, 0, :, pairs * PAIR :] = jnp.where(low, keys, vals).astype(BF16).reshape(4, length // 4, PAIR)


def per_device(
    block_in, span_start, w_query, w_key, w_value, w_out, w_gate, w_up, w_down, gain_attn, gain_mlp, cotangent
):
    x, y, c = lax.axis_index("fl"), lax.axis_index("th"), lax.axis_index("tl")
    hi = lax.axis_size("fh")
    batch, rows, width = block_in.shape
    own_rows, half = batch * rows, width // 2
    length = rows * 4
    depth = w_query.shape[0]
    q_cols, kv_cols = w_query.shape[1], w_key.shape[1]
    pairs = q_cols // PAIR
    at = jnp.stack([x]).astype(jnp.int32)

    shard = jnp.concatenate([w_query, w_key, w_value], axis=1)
    gains = jnp.concatenate([gain_attn, gain_mlp])[None]
    gains = jnp.pad(gains, ((0, ROW_PAD - 1), (0, shard.shape[1] - gains.shape[1])))
    shards = (jnp.concatenate([shard, gains], axis=0), w_out.T, w_gate, w_up, w_down.T)

    def gather_x(own):
        return own, swap(own, "fl")

    def flat(pair):
        return tuple(part.reshape(hi * depth, -1) for part in pair)

    own_parts = [lax.all_gather(part, "fh", axis=0, tiled=True) for part in shards]
    own_parts[0] = own_parts[0].reshape(hi, depth + ROW_PAD, -1)

    def gather_rows(piece):
        beside = swap(piece, "tl")
        across = swap(piece, "th")
        return piece, across, beside, swap(across, "tl")

    token_parts = gather_rows(block_in.reshape(own_rows, width))
    cot_parts = gather_rows(cotangent.reshape(own_rows, width))

    place = jnp.concatenate(
        [(((y + dy) % 2) * 2 + (c + dc) % 2) * rows + jnp.arange(rows, dtype=jnp.int32) for dc in (0, 1) for dy in (0, 1)]
    )
    frequency = jnp.exp(jnp.arange(HD // 2, dtype=F32) * (-2.0 * math.log(10000.0) / HD))
    angles = place.astype(F32)[:, None] * frequency[None, :]
    cos = jnp.tile(jnp.cos(angles), (1, 4))
    sine = jnp.sin(angles)
    sine = jnp.concatenate([-sine, sine, -sine, sine], axis=1)
    key_at, query_at = place[:, None], place[None, :]
    span = span_start[:, 0]
    tables = [(t, full_spec(t.shape)) for t in (cos, sine, key_at, query_at)]

    quad = (4, batch, rows)
    pieces = lambda parts: [(p, row_spec(rows, width)) for p in parts]
    spread_outs = [(quad + (half,), BF16, quad_spec(rows, half))] * 2

    def as_rows(value):
        return value.reshape(4 * own_rows, value.shape[-1])

    seq_cot = call(functools.partial(spread_kernel, hi), [at], batch, pieces(cot_parts), spread_outs)
    seq_cot = tuple(as_rows(v) for v in seq_cot)

    qkv_pair = gather_x(own_parts[0])
    out_pair = gather_x(own_parts[1])
    qkv_w = tuple(part[:, :depth].reshape(hi * depth, -1) for part in qkv_pair)
    gain_one = tuple(part[:, depth, :depth].reshape(1, half).astype(F32) for part in qkv_pair)
    gain_two = tuple(part[:, depth, depth : 2 * depth].reshape(1, half).astype(F32) for part in qkv_pair)
    gain_in = lambda gain: [(g, full_spec((1, half))) for g in gain]

    *seq_one, x_own, x_oth = call(
        functools.partial(norm_in_kernel, hi),
        [at],
        batch,
        pieces(token_parts) + gain_in(gain_one),
        spread_outs + [((own_rows, half), BF16, row_spec(rows, half))] * 2,
    )
    seq_one = tuple(as_rows(v) for v in seq_one)

    qkv = dot(seq_one[0], qkv_w[0]) + dot(seq_one[1], qkv_w[1])
    all_cols = qkv.shape[1]
    pair_spec, q_spec = quad_spec(rows, PAIR), quad_spec(rows, q_cols)
    lse_spec = pl.BlockSpec((1, 2 * pairs, length), lambda i, *_: (i, 0, 0))
    score_flops = 2 * batch * 2 * pairs * length * length * PAIR
    score_exps = batch * 2 * pairs * length * length
    query_rot, kv_rot, mixed, lse = call(
        functools.partial(attend_kernel, pairs),
        [span],
        batch,
        [(qkv.reshape(quad + (all_cols,)), quad_spec(rows, all_cols)), *tables],
        [
            (quad + (q_cols,), BF16, q_spec),
            (quad + (PAIR,), BF16, pair_spec),
            (quad + (q_cols,), BF16, q_spec),
            ((batch, 2 * pairs, length), F32, lse_spec),
        ],
        [
            pltpu.VMEM((length, length), F32),
            pltpu.VMEM((2, length, PAIR), BF16),
            pltpu.VMEM((2, PAIR, length), BF16),
        ],
        flops=2 * score_flops,
        exps=score_exps,
    )
    mixed = after(as_rows(mixed), own_parts[2])

    def scatter_rows(partial):
        came = swap(partial[2 * own_rows :], "tl")
        sent = (partial[own_rows : 2 * own_rows].astype(F32) + came[own_rows:].astype(F32)).astype(BF16)
        return partial, came, swap(sent, "th")

    def terms(pair):
        return [(t, row_spec(rows, half)) for part in pair for t in part]

    out_w = flat(out_pair)
    attn_terms = [scatter_rows(dot_rt(mixed, w).astype(BF16)) for w in out_w]
    half_ins = lambda *values: [(v, row_spec(rows, half)) for v in values]
    half_outs = [((own_rows, half), F32, row_spec(rows, half))] * 2
    low_out = [((own_rows, width), BF16, row_spec(rows, width))]
    h_own, h_oth, normed_two = call(
        residual_kernel,
        [],
        batch,
        half_ins(after(x_own, own_parts[3]), x_oth) + terms(attn_terms) + gain_in(gain_two),
        half_outs + low_out,
    )

    def stack_rows(low, *others):
        parts = gather_rows(low)
        parts = (after(parts[0], *others), *parts[1:]) if others else parts
        return tuple(as_rows(v) for v in call(stack_kernel, [], batch, pieces(parts), spread_outs))

    gate_w, up_w = flat(gather_x(own_parts[2])), flat(gather_x(own_parts[3]))
    normed_two = after(normed_two, gate_w[1])
    seq_two = stack_rows(normed_two, own_parts[4], up_w[1])

    gate_pre = dot(seq_two[0], gate_w[0]) + dot(seq_two[1], gate_w[1])
    up_pre = dot(seq_two[0], up_w[0]) + dot(seq_two[1], up_w[1])
    sigmoid = jax.nn.sigmoid(gate_pre)
    activated = gate_pre * sigmoid
    inner = (activated * up_pre).astype(BF16)
    down_w = flat(gather_x(own_parts[4]))

    def send_grad(oth, grad):
        return dot_lt(oth, grad).astype(BF16)

    def total_grad(own, grad, came):
        return (dot_lt(own, grad) + came.astype(F32)).astype(BF16)

    def reduce_z(total):
        return lax.psum_scatter(total, "fh", scatter_dimension=0, tiled=True)

    down_sent = send_grad(seq_cot[1], inner)
    down_w = both_after(down_w, down_sent)
    down_came = swap(down_sent, "fl")
    grad_inner = dot(seq_cot[0], down_w[0]) + dot(seq_cot[1], down_w[1])
    gate_g = (grad_inner * up_pre * sigmoid * (1.0 + gate_pre * (1.0 - sigmoid))).astype(BF16)
    up_g = (grad_inner * activated).astype(BF16)
    gate_sent = send_grad(seq_two[1], gate_g)
    gate_gn = after(gate_g, gate_sent)
    normed_terms = [
        scatter_rows((dot_rt(gate_gn, g) + dot_rt(up_g, u)).astype(BF16)) for g, u in zip(gate_w, up_w)
    ]
    down_total = total_grad(seq_cot[0], inner, down_came)
    grad_down = reduce_z(down_total)
    gate_sent = after(gate_sent, down_came)
    gate_came = swap(gate_sent, "fl")
    r_own, r_oth, attn_low, gain_s_own, gain_s_oth = call(
        middle_kernel,
        [],
        batch,
        half_ins(after(h_own, down_total), h_oth)
        + terms(normed_terms)
        + gain_in(gain_two)
        + half_ins(seq_cot[0], seq_cot[1]),
        half_outs + low_out + [((1, half), F32, full_spec((1, half)))] * 2,
    )
    up_sent = send_grad(seq_two[1], up_g)
    block_terms = [scatter_rows(dot_rt(inner, w).astype(BF16)) for w in down_w]

    whole_out = [((own_rows, width), F32, row_spec(rows, width))]
    (block_out,) = call(
        functools.partial(block_out_kernel, hi), [at], batch, half_ins(h_own, h_oth) + terms(block_terms), whole_out
    )

    gate_total = total_grad(seq_two[0], gate_g, gate_came)
    grad_gate = reduce_z(gate_total)
    seq_attn = stack_rows(attn_low, gate_total, up_sent, block_terms[0][1], block_terms[1][1])
    out_sent = send_grad(seq_attn[1], mixed)
    grad_mixed = (dot(seq_attn[0], out_w[0]) + dot(seq_attn[1], out_w[1])).astype(BF16)
    up_sent = after(up_sent, gate_came)
    up_came = swap(up_sent, "fl")
    grad_mixed = after(grad_mixed, grad_down)
    (qkv_g,) = call(
        functools.partial(attend_back_kernel, pairs),
        [span],
        batch,
        [
            (query_rot, q_spec),
            (kv_rot, pair_spec),
            (grad_mixed.reshape(quad + (q_cols,)), q_spec),
            (lse, lse_spec),
            *tables,
        ],
        [(quad + (all_cols,), BF16, quad_spec(rows, all_cols))],
        [
            pltpu.VMEM((length, length), F32),
            pltpu.VMEM((2, length, PAIR), BF16),
            pltpu.VMEM((2, PAIR, length), BF16),
            pltpu.VMEM((2, length, PAIR), BF16),
            pltpu.VMEM((2, length, PAIR), F32),
            pltpu.VMEM((2, length, PAIR), F32),
        ],
        flops=5 * score_flops,
        exps=score_exps,
    )
    up_total = total_grad(seq_two[0], up_g, up_came)
    grad_up = reduce_z(up_total)
    qkv_g = after(as_rows(qkv_g), up_came, grad_gate, block_out)
    out_sent = after(out_sent, up_came)
    out_came = swap(out_sent, "fl")

    partial_one = tuple(dot_rt(qkv_g, w).astype(BF16) for w in qkv_w)
    first_terms = [scatter_rows(p) for p in partial_one]
    gain_part = tuple(
        jnp.sum(p.astype(F32) * s.astype(F32), axis=0) / g[0] for p, s, g in zip(partial_one, seq_one, gain_one)
    )

    def gain_rows(one, two):
        pair = jnp.concatenate([one.reshape(hi, 1, depth), two.reshape(hi, 1, depth)], axis=2)
        return jnp.pad(pair, ((0, 0), (0, ROW_PAD - 1), (0, all_cols - 2 * depth)))

    def with_gains(grad, one, two):
        blocks = jnp.concatenate([grad.reshape(hi, depth, all_cols), gain_rows(one, two)], axis=1)
        return blocks.reshape(hi * (depth + ROW_PAD), all_cols)

    qkv_sent = with_gains(dot_lt(seq_one[1], qkv_g), gain_part[1], gain_s_oth[0]).astype(BF16)
    qkv_came = swap(qkv_sent, "fl")
    grad_out = reduce_z(total_grad(seq_attn[0], mixed, out_came))
    qkv_total = with_gains(dot_lt(seq_one[0], qkv_g), gain_part[0], gain_s_own[0])
    qkv_total = (qkv_total + qkv_came.astype(F32)).astype(BF16)
    grad_qkv = lax.psum_scatter(qkv_total, "fh", scatter_dimension=0, tiled=True)
    gain_sums = lax.psum(grad_qkv[depth, : 2 * depth].astype(F32), ("th", "tl"))

    (grad_in,) = call(
        functools.partial(grad_in_kernel, hi),
        [at],
        batch,
        half_ins(x_own, x_oth) + terms(first_terms) + gain_in(gain_one) + half_ins(r_own, r_oth),
        whole_out,
    )
    grad_qkv = grad_qkv[:depth].astype(F32)
    return (
        block_out.reshape(block_in.shape),
        grad_in.reshape(block_in.shape),
        grad_qkv[:, :q_cols],
        grad_qkv[:, q_cols : q_cols + kv_cols],
        grad_qkv[:, q_cols + kv_cols :],
        grad_out.astype(F32).T,
        grad_gate.astype(F32),
        grad_up.astype(F32),
        grad_down.astype(F32).T,
        gain_sums[:depth],
        gain_sums[depth:],
    )


def solution(mesh):
    n_fsdp, n_tp = mesh.shape["fsdp"], mesh.shape["tp"]
    fine = Mesh(mesh.devices.reshape(n_fsdp // 2, 2, n_tp // 2, 2), ("fh", "fl", "th", "tl"))
    fsdp, tp = ("fh", "fl"), ("th", "tl")
    rows = P(None, fsdp + tp, None)
    up, across, flat = P(fsdp, tp), P(tp, fsdp), P(fsdp)
    return jax.shard_map(
        per_device,
        mesh=fine,
        in_specs=(rows, P(None, fsdp), up, up, up, across, up, up, across, flat, flat, rows),
        out_specs=(rows, rows, up, up, up, across, up, up, across, flat, flat),
        check_vma=False,
    )
```

```python
import functools
import math

import jax
import jax.numpy as jnp
from jax import lax
from jax.experimental import pallas as pl
from jax.experimental.pallas import tpu as pltpu
from jax.sharding import Mesh, PartitionSpec as P

HD = 64
PAIR = 2 * HD
SPAN = 256
EPS = 1e-05
MASKED = -1e30
F32 = jnp.float32
BF16 = jnp.bfloat16
SWAP = [(0, 1), (1, 0)]
COST = {1: 1703, 2: 2220, 3: 2583, 4: 5630, 5: 1730, 6: 799, 7: 1730, 8: 799, 10: 1626, 11: 4002, 12: 3950, 13: 4338, 14: 3898, 15: 17158, 16: 2349, 17: 83025, 18: 2287, 19: 2349, 20: 1987, 21: 3821, 22: 1006, 23: 2556, 24: 1626, 25: 2143, 26: 1419, 27: 7981, 28: 2556, 29: 2066, 30: 826, 31: 26035, 32: 2066, 33: 17158, 34: 1523, 35: 1703, 36: 11984, 37: 53467, 38: 3616}
SKIP = {131, 137, 143, 116, 123, 125}
ROW_PAD = 16


def dot(a, b):
    return jnp.dot(a, b, preferred_element_type=F32)


def dot_lt(a, b):
    return lax.dot_general(a, b, (((0,), (0,)), ((), ())), preferred_element_type=F32)


def dot_rt(a, b):
    return lax.dot_general(a, b, (((1,), (1,)), ((), ())), preferred_element_type=F32)


def swap(value, axis):
    return lax.ppermute(value, axis, SWAP)


def after(step, value, *others):
    if step in SKIP:
        return value
    return lax.optimization_barrier((value, *others))[0]


def full_spec(shape):
    return pl.BlockSpec(shape, lambda i, *_: (0,) * len(shape))


def row_spec(rows, cols, offset=0):
    return pl.BlockSpec((rows, cols), lambda i, *_: (i + offset, 0))


def quad_spec(rows, cols):
    return pl.BlockSpec((4, 1, rows, cols), lambda i, *_: (0, i, 0, 0))


def two_part_outs(rows, cols, tile):
    half = rows // tile // 2
    first = pl.BlockSpec((tile, cols), lambda i, *_: (jnp.minimum(i, half - 1), 0))
    second = pl.BlockSpec((tile, cols), lambda i, *_: (jnp.maximum(i - half, 0), 0))
    return [((rows // 2, cols), BF16, first), ((rows // 2, cols), BF16, second)]


def whole_spec(array):
    return pl.BlockSpec(array.shape, lambda i, *_: (0, 0), pipeline_mode=pl.Buffered(1))


def call(step, kernel, scalars, grid, ins, outs, scratch=()):
    work = COST.get(step, 0) * 1000
    return pl.pallas_call(
        kernel,
        out_shape=[jax.ShapeDtypeStruct(shape, kind) for shape, kind, _ in outs],
        grid_spec=pltpu.PrefetchScalarGridSpec(
            num_scalar_prefetch=len(scalars),
            grid=(grid,),
            in_specs=[spec for _, spec in ins],
            out_specs=[spec for _, _, spec in outs],
            scratch_shapes=list(scratch),
        ),
        cost_estimate=pl.CostEstimate(flops=work * 300, bytes_accessed=work + step, transcendentals=0),
        compiler_params=pltpu.CompilerParams(vmem_limit_bytes=56 << 20),
    )(*scalars, *[a for a, _ in ins])


def halves_of(value, hi, x):
    width = value.shape[-1] // (2 * hi)
    parts = [value[:, k * width : (k + 1) * width] for k in range(2 * hi)]
    even, odd = parts[0::2], parts[1::2]
    own = [jnp.where(x == 0, a, b) for a, b in zip(even, odd)]
    oth = [jnp.where(x == 0, b, a) for a, b in zip(even, odd)]
    return own, oth


def put_cols(ref, index, parts):
    width = parts[0].shape[-1]
    for k, part in enumerate(parts):
        ref[(*index, slice(None), slice(k * width, (k + 1) * width))] = part.astype(ref.dtype)


def join_to(ref, own, oth, hi, x):
    width = own.shape[-1] // hi
    for k in range(hi):
        a, b = own[:, k * width : (k + 1) * width], oth[:, k * width : (k + 1) * width]
        ref[:, 2 * k * width : (2 * k + 1) * width] = jnp.where(x == 0, a, b)
        ref[:, (2 * k + 1) * width : (2 * k + 2) * width] = jnp.where(x == 0, b, a)


def norm_in_kernel(hi, at, p0, p1, p2, p3, gain_own, gain_oth, n_own, n_oth, x_own, x_oth):
    x = at[0]
    half = n_own.shape[-1]
    for k, piece in enumerate((p0, p1, p2, p3)):
        low = piece[...]
        value = low.astype(F32)
        scale = lax.rsqrt(jnp.mean(value * value, axis=-1, keepdims=True) + EPS)
        own, oth = halves_of(value, hi, x)
        width = half // hi
        for part, gain, ref in ((own, gain_own, n_own), (oth, gain_oth, n_oth)):
            put_cols(
                ref, (k, 0), [v * scale * gain[:, z * width : (z + 1) * width] for z, v in enumerate(part)]
            )
        if k == 0:
            put_cols(x_own, (), own)
            put_cols(x_oth, (), oth)


def spread_kernel(hi, at, p0, p1, p2, p3, o_own, o_oth):
    x = at[0]
    for k, piece in enumerate((p0, p1, p2, p3)):
        own, oth = halves_of(piece[...], hi, x)
        put_cols(o_own, (k, 0), own)
        put_cols(o_oth, (k, 0), oth)


def pairs_kernel(hi, at, p0, p1, p2, p3, out):
    x = at[0]
    for k, piece in enumerate((p0, p1, p2, p3)):
        own, oth = halves_of(piece[...], hi, x)
        put_cols(out, (k, 0), [part for pair in zip(own, oth) for part in pair])


def stack_kernel(p0, p1, p2, p3, o_own, o_oth):
    half = o_own.shape[-1]
    for k, piece in enumerate((p0, p1, p2, p3)):
        o_own[k, 0] = piece[:, :half]
        o_oth[k, 0] = piece[:, half:]


def rows_scale(own, oth):
    total = jnp.sum(own * own, axis=-1, keepdims=True) + jnp.sum(oth * oth, axis=-1, keepdims=True)
    return lax.rsqrt(total / (own.shape[-1] + oth.shape[-1]) + EPS)


def summed(refs):
    return refs[0][...].astype(F32) + refs[1][...].astype(F32) + refs[2][...].astype(F32)


def residual_kernel(x_own, x_oth, a0, a1, a2, b0, b1, b2, gain_own, gain_oth, h_own, h_oth, n_out):
    own = x_own[...].astype(F32) + summed((a0, a1, a2))
    oth = x_oth[...].astype(F32) + summed((b0, b1, b2))
    scale = rows_scale(own, oth)
    half = own.shape[-1]
    h_own[...] = own
    h_oth[...] = oth
    n_out[:, :half] = (own * scale * gain_own[...]).astype(BF16)
    n_out[:, half:] = (oth * scale * gain_oth[...]).astype(BF16)


def block_out_kernel(hi, at, h_own, h_oth, t0, t1, t2, out):
    x = at[0]
    width = h_own.shape[-1] // hi
    for k in range(hi):
        cols = [slice(j * width, (j + 1) * width) for j in (2 * k, 2 * k + 1)]
        own, oth = (sum(t[:, col].astype(F32) for t in (t0, t1, t2)) for col in cols)
        own += h_own[:, k * width : (k + 1) * width]
        oth += h_oth[:, k * width : (k + 1) * width]
        out[:, cols[0]] = jnp.where(x == 0, own, oth)
        out[:, cols[1]] = jnp.where(x == 0, oth, own)


def back_of(own, oth, scale, gain_own, gain_oth, up_own, up_oth):
    w_own, w_oth = up_own * gain_own, up_oth * gain_oth
    total = jnp.sum(w_own * own, axis=-1, keepdims=True) + jnp.sum(w_oth * oth, axis=-1, keepdims=True)
    cube = scale * scale * scale * (total / (own.shape[-1] + oth.shape[-1]))
    return scale * w_own - own * cube, scale * w_oth - oth * cube


def middle_kernel(
    hi, at, h_own, h_oth, a0, a1, a2, b0, b1, b2, gain_own, gain_oth, upstream, r_own, r_oth, low_out, s_own, s_oth
):
    own, oth = h_own[...], h_oth[...]
    up_own, up_oth = summed((a0, a1, a2)), summed((b0, b1, b2))
    scale = rows_scale(own, oth)
    back_own, back_oth = back_of(own, oth, scale, gain_own[...], gain_oth[...], up_own, up_oth)
    u_own, u_oth = (jnp.concatenate(part, axis=1) for part in halves_of(upstream[...].astype(F32), hi, at[0]))
    back_own = u_own + back_own
    back_oth = u_oth + back_oth
    half = own.shape[-1]
    r_own[...] = back_own
    r_oth[...] = back_oth
    low_out[:, :half] = back_own.astype(BF16)
    low_out[:, half:] = back_oth.astype(BF16)

    @pl.when(pl.program_id(0) == 0)
    def _():
        s_own[...] = jnp.zeros_like(s_own)
        s_oth[...] = jnp.zeros_like(s_oth)

    s_own[...] += jnp.sum(up_own * own * scale, axis=0, keepdims=True)
    s_oth[...] += jnp.sum(up_oth * oth * scale, axis=0, keepdims=True)


def grad_in_kernel(hi, at, x_own, x_oth, a0, a1, a2, b0, b1, b2, gain_own, gain_oth, r_own, r_oth, out):
    own, oth = x_own[...].astype(F32), x_oth[...].astype(F32)
    scale = rows_scale(own, oth)
    back_own, back_oth = back_of(
        own, oth, scale, gain_own[...], gain_oth[...], summed((a0, a1, a2)), summed((b0, b1, b2))
    )
    join_to(out, r_own[...] + back_own, r_oth[...] + back_oth, hi, at[0])


def project_kernel(n_own, n_oth, w_own, w_oth, out):
    out[...] = (dot(n_own[...], w_own[...]) + dot(n_oth[...], w_oth[...])).astype(out.dtype)


def put_rows(kept, sent, value):
    stay = pl.program_id(0) < pl.num_programs(0) // 2

    @pl.when(stay)
    def _():
        kept[...] = value

    @pl.when(jnp.logical_not(stay))
    def _():
        sent[...] = value


def project_back_kernel(rows, weight, kept, sent):
    put_rows(kept, sent, dot_rt(rows[...], weight[...]).astype(BF16))


def project_gain_kernel(grad, weight, normed, kept, sent, sums):
    part = dot_rt(grad[...], weight[...])
    put_rows(kept, sent, part.astype(BF16))

    @pl.when(pl.program_id(0) == 0)
    def _():
        sums[...] = jnp.zeros_like(sums)

    sums[...] += jnp.sum(part * normed[...].astype(F32), axis=0, keepdims=True)


def weight_grad_kernel(rows, grad, out):
    out[...] = dot_lt(rows[...], grad[...]).astype(out.dtype)


def weight_grad_add_kernel(rows, grad, came, out):
    out[...] = (dot_lt(rows[...], grad[...]) + came[...].astype(F32)).astype(BF16)


def add_kernel(first, second, out):
    out[...] = (first[...].astype(F32) + second[...].astype(F32)).astype(BF16)


def expand_kernel(n_own, n_oth, u_own, u_oth, gate_in, inner, for_gate, for_up):
    gate = gate_in[...]
    up = dot(n_own[...], u_own[...]) + dot(n_oth[...], u_oth[...])
    sigmoid = jax.nn.sigmoid(gate)
    active = gate * sigmoid
    inner[...] = (active * up).astype(BF16)
    for_gate[...] = (up * sigmoid * (1.0 + gate * (1.0 - sigmoid))).astype(BF16)
    for_up[...] = active.astype(BF16)


def inner_back_kernel(grad, weight, for_gate, for_up, gate_g, up_g):
    inner_g = dot(grad[...], weight[...])
    gate_g[...] = (inner_g * for_gate[...].astype(F32)).astype(BF16)
    up_g[...] = (inner_g * for_up[...].astype(F32)).astype(BF16)


def expand_back_kernel(gate_g, up_g, gate_w, up_w, kept, sent):
    put_rows(kept, sent, (dot_rt(gate_g[...], gate_w[...]) + dot_rt(up_g[...], up_w[...])).astype(BF16))


def partner(value):
    lane = lax.broadcasted_iota(jnp.int32, value.shape, 1)
    return jnp.where(lane % HD < HD // 2, pltpu.roll(value, PAIR - HD // 2, 1), pltpu.roll(value, HD // 2, 1))


def low_lanes(shape):
    return lax.broadcasted_iota(jnp.int32, shape, 1) < HD


def set_bias(bias, key_at, query_at, first):
    keys, queries = key_at[...], query_at[...]
    key_in = ((keys >= first) & (keys < first + SPAN)).astype(jnp.int32)
    query_in = ((queries >= first) & (queries < first + SPAN)).astype(jnp.int32)
    seen = (keys <= queries).astype(jnp.int32) + key_in * query_in
    bias[...] = jnp.where(seen > 0, 0.0, MASKED)


def attend_kernel(pairs, span, qkv, cos, sine, key_at, query_at, q_out, kv_out, o_out, lse_out, bias, key_s, val_s):
    length = cos.shape[0]
    set_bias(bias, key_at, query_at, span[pl.program_id(0)])
    kv = qkv[:, 0, :, pairs * PAIR :].reshape(length, PAIR)
    low = low_lanes(kv.shape)
    turned = kv * cos[...] + partner(kv) * sine[...]
    kv = jnp.where(low, turned, kv).astype(BF16)
    kv_out[:, 0] = kv.reshape(4, length // 4, PAIR)
    wide = kv.astype(F32)
    key_even = jnp.where(low, wide, 0.0)
    val_odd = jnp.where(low, 0.0, wide)
    key_s[0] = key_even.astype(BF16)
    key_s[1] = pltpu.roll(key_even, HD, 1).astype(BF16)
    val_s[0] = pltpu.roll(val_odd, HD, 1).T.astype(BF16)
    val_s[1] = val_odd.T.astype(BF16)

    def pair_step(j, _):
        cols = pl.ds(pl.multiple_of(j * PAIR, PAIR), PAIR)
        raw = qkv[:, 0, :, cols].reshape(length, PAIR)
        query = (raw * cos[...] + partner(raw) * sine[...]).astype(BF16)
        q_out[:, 0, :, cols] = query.reshape(4, length // 4, PAIR)
        query_t = (query.astype(F32) * HD**-0.5).T.astype(BF16)
        mixed = jnp.zeros((PAIR, length), F32)
        for k in range(2):
            scores = dot(key_s[k], query_t) + bias[...]
            top = jnp.max(scores, axis=0, keepdims=True)
            raised = jnp.exp(scores - top)
            total = jnp.sum(raised, axis=0, keepdims=True)
            lse_out[0, pl.ds(2 * j + k, 1), :] = top + jnp.log(total)
            mixed += dot(val_s[k], (raised * (1.0 / total)).astype(BF16))
        o_out[:, 0, :, cols] = mixed.T.astype(BF16).reshape(4, length // 4, PAIR)
        return 0

    lax.fori_loop(0, pairs, pair_step, 0)


def attend_back_kernel(
    pairs, span, query_in, kv_in, grad_in, lse, cos, sine, key_at, query_at, out, bias, key_s, key_t, val_s, key_g, val_g
):
    length = cos.shape[0]
    set_bias(bias, key_at, query_at, span[pl.program_id(0)])
    kv = kv_in[:, 0].reshape(length, PAIR).astype(F32)
    low = low_lanes(kv.shape)
    key_even = jnp.where(low, kv, 0.0)
    key_odd = pltpu.roll(key_even, HD, 1)
    val_odd = jnp.where(low, 0.0, kv)
    key_s[0] = key_even.astype(BF16)
    key_s[1] = key_odd.astype(BF16)
    key_t[0] = key_even.T.astype(BF16)
    key_t[1] = key_odd.T.astype(BF16)
    val_s[0] = pltpu.roll(val_odd, HD, 1).astype(BF16)
    val_s[1] = val_odd.astype(BF16)
    key_g[...] = jnp.zeros_like(key_g)
    val_g[...] = jnp.zeros_like(val_g)

    def pair_step(j, _):
        cols = pl.ds(pl.multiple_of(j * PAIR, PAIR), PAIR)
        query = query_in[:, 0, :, cols].reshape(length, PAIR)
        grad = grad_in[:, 0, :, cols].reshape(length, PAIR)
        query_t = (query.astype(F32) * HD**-0.5).T.astype(BF16)
        grad_t = grad.astype(F32).T.astype(BF16)
        query_g = jnp.zeros((PAIR, length), F32)
        for k in range(2):
            scores = dot(key_s[k], query_t) + bias[...]
            weight = jnp.exp(scores - lse[0, pl.ds(2 * j + k, 1), :])
            weight_g = dot(val_s[k], grad_t)
            val_g[k] += dot(weight.astype(BF16), grad)
            delta = jnp.sum(weight * weight_g, axis=0, keepdims=True)
            score_g = (HD**-0.5 * (weight * (weight_g - delta))).astype(BF16)
            key_g[k] += dot(score_g, query)
            query_g += dot(key_t[k], score_g)
        value = query_g.T
        value = value * cos[...] - partner(value) * sine[...]
        out[:, 0, :, cols] = value.astype(BF16).reshape(4, length // 4, PAIR)
        return 0

    lax.fori_loop(0, pairs, pair_step, 0)
    keys = key_g[0] + pltpu.roll(key_g[1], HD, 1)
    vals = val_g[1] + pltpu.roll(val_g[0], HD, 1)
    keys = keys * cos[...] - partner(keys) * sine[...]
    out[:, 0, :, pairs * PAIR :] = jnp.where(low, keys, vals).astype(BF16).reshape(4, length // 4, PAIR)


def per_device(
    block_in, span_start, w_query, w_key, w_value, w_out, w_gate, w_up, w_down, gain_attn, gain_mlp, cotangent
):
    x, y, c = (lax.axis_index(name) for name in ("fl", "th", "tl"))
    hi = lax.axis_size("fh")
    batch, rows, width = block_in.shape
    own_rows, half = batch * rows, width // 2
    length = rows * 4
    depth = w_query.shape[0]
    q_cols, kv_cols = w_query.shape[1], w_key.shape[1]
    pairs = q_cols // PAIR
    at = jnp.stack([x]).astype(jnp.int32)

    shard = jnp.concatenate([w_query, w_key, w_value], axis=1)
    gains = jnp.concatenate([gain_attn, gain_mlp])[None]
    gains = jnp.pad(gains, ((0, ROW_PAD - 1), (0, shard.shape[1] - gains.shape[1])))
    shard = jnp.concatenate([shard, gains], axis=0)

    def gather(part):
        return lax.all_gather(part, "fh", axis=0, tiled=True)

    def swap_x(value):
        return swap(value, "fl")

    down_shard = w_down.T
    down_pair = jnp.concatenate([down_shard, swap_x(down_shard)], axis=0)
    attn_own, out_own, gate_own, up_own = gather(shard), gather(w_out.T), gather(w_gate), gather(w_up)
    down_w = gather(down_pair)

    def gather_rows(piece):
        beside = swap(piece, "tl")
        across = swap(piece, "th")
        return piece, across, beside, swap(across, "tl")

    token_parts = gather_rows(block_in.reshape(own_rows, width))
    cot_own = cotangent.reshape(own_rows, width)
    cot_parts = gather_rows(after(101, cot_own, token_parts[1]))

    place = jnp.concatenate(
        [(((y + dy) % 2) * 2 + (c + dc) % 2) * rows + jnp.arange(rows, dtype=jnp.int32) for dc in (0, 1) for dy in (0, 1)]
    )
    frequency = jnp.exp(jnp.arange(HD // 2, dtype=F32) * (-2.0 * math.log(10000.0) / HD))
    angles = place.astype(F32)[:, None] * frequency[None, :]
    cos = jnp.tile(jnp.cos(angles), (1, 4))
    sine = jnp.sin(angles)
    sine = jnp.concatenate([-sine, sine, -sine, sine], axis=1)
    key_at, query_at = place[:, None], place[None, :]
    span = span_start[:, 0]
    tables = [(t, full_spec(t.shape)) for t in (cos, sine, key_at, query_at)]

    quad = (4, batch, rows)
    all_rows = 4 * own_rows
    tile = 256
    steps = all_rows // tile
    hidden = w_gate.shape[1]
    all_cols = q_cols + 2 * kv_cols
    tiles = lambda *values: [(v, row_spec(tile, v.shape[1])) for v in values]
    wholes = lambda *values: [(v, whole_spec(v)) for v in values]
    pieces = lambda parts: [(p, row_spec(rows, width)) for p in parts]
    half_ins = lambda *values: [(v, row_spec(rows, half)) for v in values]
    gain_in = lambda gain: [(g, full_spec((1, half))) for g in gain]
    spread_outs = [(quad + (half,), BF16, quad_spec(rows, half))] * 2
    half_outs = [((own_rows, half), F32, row_spec(rows, half))] * 2
    low_out = [((own_rows, width), BF16, row_spec(rows, width))]
    whole_out = [((own_rows, width), F32, row_spec(rows, width))]
    sum_outs = [((1, half), F32, full_spec((1, half)))]
    hidden_out = ((all_rows, hidden), BF16, row_spec(tile, hidden))

    def as_rows(value):
        return value.reshape(all_rows, value.shape[-1])

    def project(step, pair, weights, kind):
        cols = weights[0].shape[1]
        out = ((all_rows, cols), kind, row_spec(tile, cols))
        return call(step, project_kernel, [], steps, tiles(*pair) + wholes(*weights), [out])[0]

    def project_back(step, value, weight):
        outs = two_part_outs(all_rows, weight.shape[0], tile)
        return call(step, project_back_kernel, [], steps, tiles(value) + wholes(weight), outs)

    def weight_grad(step, value, grad, came=None, kind=BF16):
        part, cols = 256, grad.shape[1]
        ins = [(value, pl.BlockSpec((value.shape[0], part), lambda i: (0, i)))] + wholes(grad)
        ins += [] if came is None else [(came, row_spec(part, cols))]
        out = ((value.shape[1], cols), kind, row_spec(part, cols))
        kernel = weight_grad_kernel if came is None else weight_grad_add_kernel
        return call(step, kernel, [], value.shape[1] // part, ins, [out])[0]

    def scatter_rows(step, kept, sent):
        cols = kept.shape[1]
        came = swap(sent, "tl")
        (passed,) = call(
            step,
            add_kernel,
            [],
            batch,
            [(kept, row_spec(rows, cols, batch)), (came, row_spec(rows, cols, batch))],
            [((own_rows, cols), BF16, row_spec(rows, cols))],
        )
        return kept, came, swap(passed, "th"), passed

    def terms(*scattered):
        return [(t, row_spec(rows, t.shape[1])) for part in scattered for t in part[:3]]

    def stack_rows(step, low, order, *others):
        beside, across = swap(low, "tl"), swap(low, "th")
        across = after(order, across, *others)
        parts = (low, across, beside, swap(across, "tl"))
        return tuple(as_rows(v) for v in call(step, stack_kernel, [], batch, pieces(parts), spread_outs))

    attn_own = after(102, attn_own, down_pair)
    attn_pair = tuple(part.reshape(hi, depth + ROW_PAD, -1) for part in (attn_own, swap_x(attn_own)))
    qkv_w = tuple(part[:, :depth].reshape(hi * depth, -1) for part in attn_pair)
    out_w = (out_own, swap_x(after(138, out_own, attn_pair[1])))
    gain_one = tuple(part[:, depth, :depth].reshape(1, half).astype(F32) for part in attn_pair)
    gain_two = tuple(part[:, depth, depth : 2 * depth].reshape(1, half).astype(F32) for part in attn_pair)

    *seq_one, x_own, x_oth = call(
        2,
        functools.partial(norm_in_kernel, hi),
        [at],
        batch,
        pieces(token_parts) + gain_in(gain_one),
        spread_outs + [((own_rows, half), BF16, row_spec(rows, half))] * 2,
    )
    seq_one = tuple(as_rows(v) for v in seq_one)
    gate_near = after(105, after(104, gate_own, out_w[1]), seq_one[0])
    gate_w = (gate_own, swap_x(gate_near))
    up_w = (up_own, swap_x(after(106, up_own, gate_w[1])))

    qkv = project(3, seq_one, qkv_w, F32)
    qkv = after(144, after(107, qkv, out_w[1]), cot_parts[1])
    pair_spec, q_spec = quad_spec(rows, PAIR), quad_spec(rows, q_cols)
    lse_spec = pl.BlockSpec((1, 2 * pairs, length), lambda i, *_: (i, 0, 0))
    query_rot, kv_rot, mixed, lse = call(
        4,
        functools.partial(attend_kernel, pairs),
        [span],
        batch,
        [(qkv.reshape(quad + (all_cols,)), quad_spec(rows, all_cols)), *tables],
        [
            (quad + (q_cols,), BF16, q_spec),
            (quad + (PAIR,), BF16, pair_spec),
            (quad + (q_cols,), BF16, q_spec),
            ((batch, 2 * pairs, length), F32, lse_spec),
        ],
        [
            pltpu.VMEM((length, length), F32),
            pltpu.VMEM((2, length, PAIR), BF16),
            pltpu.VMEM((2, PAIR, length), BF16),
        ],
    )
    mixed = as_rows(mixed)
    attn_oth = scatter_rows(6, *project_back(5, mixed, out_w[1]))
    attn_own = scatter_rows(8, *project_back(7, after(108, mixed, attn_oth[3]), out_w[0]))
    h_own, h_oth, normed_two = call(
        9,
        residual_kernel,
        [],
        batch,
        half_ins(after(109, x_own, gate_own), x_oth) + terms(attn_own, attn_oth) + gain_in(gain_two),
        half_outs + low_out,
    )
    (seq_cot,) = call(
        1,
        functools.partial(pairs_kernel, hi),
        [at],
        batch,
        pieces((after(103, cot_own, normed_two), *cot_parts[1:])),
        [(quad + (width,), BF16, quad_spec(rows, width))],
    )
    seq_cot = as_rows(seq_cot)
    seq_two = stack_rows(10, normed_two, 111, gate_w[1], seq_cot)
    gate_pre = project(38, seq_two, gate_w, F32)
    inner, for_gate, for_up = call(
        11, expand_kernel, [], steps, tiles(*seq_two) + wholes(*up_w) + tiles(gate_pre), [hidden_out] * 3
    )

    def reduce_z(total):
        return lax.psum_scatter(total, "fh", scatter_dimension=0, tiled=True)

    down_part = weight_grad(12, seq_cot, inner)
    grad_down = reduce_z(down_part)
    gate_g, up_g = call(
        13,
        inner_back_kernel,
        [],
        steps,
        tiles(after(112, seq_cot, down_part)) + wholes(down_w) + tiles(for_gate, for_up),
        [hidden_out] * 2,
    )

    def expand_back(step, which, gate_g):
        outs = two_part_outs(all_rows, half, tile)
        ins = tiles(gate_g, up_g) + wholes(gate_w[which], up_w[which])
        return call(step, expand_back_kernel, [], steps, ins, outs)

    gate_sent = weight_grad(16, seq_two[1], gate_g)
    gate_came = swap_x(gate_sent)
    oth_parts = expand_back(14, 1, after(113, gate_g, gate_sent))
    normed_oth = scatter_rows(15, *oth_parts)
    own_parts = expand_back(17, 0, after(116, after(115, gate_g, oth_parts[0]), normed_oth[3]))
    normed_own = scatter_rows(18, *own_parts)
    up_sent = weight_grad(19, seq_two[1], after(117, up_g, normed_own[3]))
    r_own, r_oth, attn_low, gain_s_own, gain_s_oth = call(
        20,
        functools.partial(middle_kernel, hi),
        [at],
        batch,
        half_ins(after(118, h_own, up_sent), h_oth)
        + terms(normed_own, normed_oth)
        + gain_in(gain_two)
        + [(cot_own, row_spec(rows, width))],
        half_outs + low_out + sum_outs * 2,
    )
    gate_came = after(120, gate_came, attn_low)
    up_came = swap_x(after(122, up_sent, gate_came))
    gate_total = weight_grad(23, seq_two[0], gate_g, gate_came)
    grad_gate = reduce_z(gate_total)
    block_parts = project_back(21, after(119, inner, gate_total), down_w)

    seq_attn = stack_rows(24, attn_low, 123, gate_total, block_parts[0])
    block_terms = scatter_rows(22, after(124, block_parts[0], seq_attn[0]), block_parts[1])
    grad_mixed = project(25, seq_attn, out_w, BF16)
    out_sent = weight_grad(26, after(125, seq_attn[1], grad_mixed), mixed)
    up_came = after(127, after(126, up_came, out_sent), grad_down)
    out_came = swap_x(after(128, out_sent, up_came))
    up_total = weight_grad(28, seq_two[0], up_g, up_came)
    grad_up = reduce_z(up_total)
    grad_mixed = after(139, grad_mixed, up_total)
    (qkv_g,) = call(
        27,
        functools.partial(attend_back_kernel, pairs),
        [span],
        batch,
        [
            (query_rot, q_spec),
            (kv_rot, pair_spec),
            (grad_mixed.reshape(quad + (q_cols,)), q_spec),
            (lse, lse_spec),
            *tables,
        ],
        [(quad + (all_cols,), BF16, quad_spec(rows, all_cols))],
        [
            pltpu.VMEM((length, length), F32),
            pltpu.VMEM((2, length, PAIR), BF16),
            pltpu.VMEM((2, PAIR, length), BF16),
            pltpu.VMEM((2, length, PAIR), BF16),
            pltpu.VMEM((2, length, PAIR), F32),
            pltpu.VMEM((2, length, PAIR), F32),
        ],
    )
    qkv_g = after(141, after(140, after(129, as_rows(qkv_g), out_came), block_terms[2]), grad_gate)

    def project_gain(step, which, grad):
        outs = two_part_outs(all_rows, half, tile) + sum_outs
        kept, sent, sums = call(
            step, project_gain_kernel, [], steps, tiles(grad) + wholes(qkv_w[which]) + tiles(seq_one[which]), outs
        )
        return (kept, sent), sums / gain_one[which]

    def gain_rows(one, two):
        pair = jnp.concatenate([one.reshape(hi, 1, depth), two.reshape(hi, 1, depth)], axis=2)
        return jnp.pad(pair, ((0, 0), (0, ROW_PAD - 1), (0, all_cols - 2 * depth)))

    def with_gains(grad, one, two):
        return jnp.concatenate([grad.reshape(hi, depth, all_cols), gain_rows(one, two)], axis=1)

    oth_parts, oth_gain = project_gain(29, 1, qkv_g)
    first_oth = scatter_rows(30, *oth_parts)
    qkv_sent = with_gains(
        weight_grad(31, seq_one[1], after(130, qkv_g, oth_parts[0])), oth_gain, gain_s_oth
    ).astype(BF16)
    qkv_came = swap_x(after(134, qkv_sent, out_came))
    out_came = after(132, out_came, qkv_sent)
    out_total = weight_grad(34, seq_attn[0], mixed, out_came)
    own_parts, own_gain = project_gain(32, 0, after(143, after(142, after(131, qkv_g, qkv_sent), first_oth[3]), out_total))
    first_own = scatter_rows(33, *own_parts)
    grad_out = reduce_z(out_total)
    qkv_total = with_gains(weight_grad(35, seq_one[0], qkv_g, kind=F32), own_gain, gain_s_own)
    qkv_total = (qkv_total + after(135, qkv_came, grad_up).astype(F32)).astype(BF16)
    grad_qkv = reduce_z(qkv_total.reshape(hi * (depth + ROW_PAD), all_cols)).astype(F32)
    gain_sums = lax.psum(grad_qkv[depth, : 2 * depth], ("th", "tl"))
    (block_out,) = call(
        36,
        functools.partial(block_out_kernel, hi),
        [at],
        batch,
        half_ins(after(137, after(136, h_own, qkv_sent), grad_up), h_oth) + terms(block_terms),
        whole_out,
    )
    (grad_in,) = call(
        37,
        functools.partial(grad_in_kernel, hi),
        [at],
        batch,
        half_ins(x_own, x_oth) + terms(first_own, first_oth) + gain_in(gain_one) + half_ins(r_own, r_oth),
        whole_out,
    )
    grad_down = grad_down[:depth].astype(F32) + swap_x(grad_down[depth:]).astype(F32)
    return (
        block_out.reshape(block_in.shape),
        grad_in.reshape(block_in.shape),
        grad_qkv[:depth, :q_cols],
        grad_qkv[:depth, q_cols : q_cols + kv_cols],
        grad_qkv[:depth, q_cols + kv_cols :],
        grad_out.astype(F32).T,
        grad_gate.astype(F32),
        grad_up.astype(F32),
        grad_down.T,
        gain_sums[:depth],
        gain_sums[depth:],
    )


def solution(mesh):
    n_fsdp, n_tp = mesh.shape["fsdp"], mesh.shape["tp"]
    fine = Mesh(mesh.devices.reshape(n_fsdp // 2, 2, n_tp // 2, 2), ("fh", "fl", "th", "tl"))
    fsdp, tp = ("fh", "fl"), ("th", "tl")
    rows = P(None, fsdp + tp, None)
    up, across, flat = P(fsdp, tp), P(tp, fsdp), P(fsdp)
    return jax.shard_map(
        per_device,
        mesh=fine,
        in_specs=(rows, P(None, fsdp), up, up, up, across, up, up, across, flat, flat, rows),
        out_specs=(rows, rows, up, up, up, across, up, up, across, flat, flat),
        check_vma=False,
    )
```

```python
import functools
import math

import jax
import jax.numpy as jnp
from jax import lax
from jax.experimental import pallas as pl
from jax.experimental.pallas import tpu as pltpu
from jax.sharding import Mesh, PartitionSpec as P

HD = 64
PAIR = 2 * HD
SPAN = 256
EPS = 1e-05
MASKED = -1e30
F32 = jnp.float32
BF16 = jnp.bfloat16
SWAP = [(0, 1), (1, 0)]
COST = {1: 1702, 2: 2220, 3: 2582, 4: 5630, 5: 1730, 6: 798, 7: 1730, 8: 798, 9: 1498, 10: 1626, 11: 4596, 12: 3950, 13: 4338, 14: 3898, 15: 798, 16: 2348, 17: 3872, 18: 798, 19: 2348, 20: 1986, 21: 3820, 22: 1006, 23: 2556, 24: 1626, 25: 2142, 26: 8118, 27: 127702, 28: 10228, 29: 33062, 31: 1626, 32: 1476, 34: 1522, 36: 1498, 37: 53466, 38: 3898, 39: 23246}
SKIP = {133, 134, 103, 137, 139, 107, 142, 116, 150, 151, 120, 122}
ROW_PAD = 16


def dot(a, b):
    return jnp.dot(a, b, preferred_element_type=F32)


def dot_lt(a, b):
    return lax.dot_general(a, b, (((0,), (0,)), ((), ())), preferred_element_type=F32)


def dot_rt(a, b):
    return lax.dot_general(a, b, (((1,), (1,)), ((), ())), preferred_element_type=F32)


def swap(value, axis):
    return lax.ppermute(value, axis, SWAP)


def after(step, value, *others):
    if step in SKIP:
        return value
    return lax.optimization_barrier((value, *others))[0]


def full_spec(shape):
    return pl.BlockSpec(shape, lambda i, *_: (0,) * len(shape))


def row_spec(rows, cols, offset=0):
    return pl.BlockSpec((rows, cols), lambda i, *_: (i + offset, 0))


def quad_spec(rows, cols):
    return pl.BlockSpec((4, 1, rows, cols), lambda i, *_: (0, i, 0, 0))


def two_part_outs(rows, cols, tile):
    half = rows // tile // 2
    first = pl.BlockSpec((tile, cols), lambda i, *_: (jnp.minimum(i, half - 1), 0))
    second = pl.BlockSpec((tile, cols), lambda i, *_: (jnp.maximum(i - half, 0), 0))
    return [((rows // 2, cols), BF16, first), ((rows // 2, cols), BF16, second)]


def whole_spec(array):
    return pl.BlockSpec(array.shape, lambda i, *_: (0, 0), pipeline_mode=pl.Buffered(1))


def call(step, kernel, scalars, grid, ins, outs, scratch=()):
    work = COST.get(step, 0) * 1000
    return pl.pallas_call(
        kernel,
        out_shape=[jax.ShapeDtypeStruct(shape, kind) for shape, kind, _ in outs],
        grid_spec=pltpu.PrefetchScalarGridSpec(
            num_scalar_prefetch=len(scalars),
            grid=(grid,),
            in_specs=[spec for _, spec in ins],
            out_specs=[spec for _, _, spec in outs],
            scratch_shapes=list(scratch),
        ),
        cost_estimate=pl.CostEstimate(flops=work * 300, bytes_accessed=work + step, transcendentals=0),
        compiler_params=pltpu.CompilerParams(vmem_limit_bytes=56 << 20),
    )(*scalars, *[a for a, _ in ins])


def halves_of(value, hi, x):
    width = value.shape[-1] // (2 * hi)
    parts = [value[:, k * width : (k + 1) * width] for k in range(2 * hi)]
    even, odd = parts[0::2], parts[1::2]
    own = [jnp.where(x == 0, a, b) for a, b in zip(even, odd)]
    oth = [jnp.where(x == 0, b, a) for a, b in zip(even, odd)]
    return own, oth


def put_cols(ref, index, parts):
    width = parts[0].shape[-1]
    for k, part in enumerate(parts):
        ref[(*index, slice(None), slice(k * width, (k + 1) * width))] = part.astype(ref.dtype)


def join_to(ref, own, oth, hi, x):
    width = own.shape[-1] // hi
    for k in range(hi):
        a, b = own[:, k * width : (k + 1) * width], oth[:, k * width : (k + 1) * width]
        ref[:, 2 * k * width : (2 * k + 1) * width] = jnp.where(x == 0, a, b)
        ref[:, (2 * k + 1) * width : (2 * k + 2) * width] = jnp.where(x == 0, b, a)


def norm_in_kernel(hi, at, p0, p1, p2, p3, gain_own, gain_oth, n_own, n_oth, x_own, x_oth):
    x = at[0]
    half = n_own.shape[-1]
    for k, piece in enumerate((p0, p1, p2, p3)):
        low = piece[...]
        value = low.astype(F32)
        scale = lax.rsqrt(jnp.mean(value * value, axis=-1, keepdims=True) + EPS)
        own, oth = halves_of(value, hi, x)
        width = half // hi
        for part, gain, ref in ((own, gain_own, n_own), (oth, gain_oth, n_oth)):
            put_cols(
                ref, (k, 0), [v * scale * gain[:, z * width : (z + 1) * width] for z, v in enumerate(part)]
            )
        if k == 0:
            put_cols(x_own, (), own)
            put_cols(x_oth, (), oth)


def spread_kernel(hi, at, p0, p1, p2, p3, o_own, o_oth):
    x = at[0]
    for k, piece in enumerate((p0, p1, p2, p3)):
        own, oth = halves_of(piece[...], hi, x)
        put_cols(o_own, (k, 0), own)
        put_cols(o_oth, (k, 0), oth)


def pairs_kernel(hi, at, p0, p1, p2, p3, out):
    x = at[0]
    for k, piece in enumerate((p0, p1, p2, p3)):
        own, oth = halves_of(piece[...], hi, x)
        put_cols(out, (k, 0), [part for pair in zip(own, oth) for part in pair])


def stack_kernel(p0, p1, p2, p3, o_own, o_oth):
    half = o_own.shape[-1]
    for k, piece in enumerate((p0, p1, p2, p3)):
        o_own[k, 0] = piece[:, :half]
        o_oth[k, 0] = piece[:, half:]


def rows_scale(own, oth):
    total = jnp.sum(own * own, axis=-1, keepdims=True) + jnp.sum(oth * oth, axis=-1, keepdims=True)
    return lax.rsqrt(total / (own.shape[-1] + oth.shape[-1]) + EPS)


def summed(refs):
    return refs[0][...].astype(F32) + refs[1][...].astype(F32) + refs[2][...].astype(F32)


def residual_kernel(x_own, x_oth, a0, a1, a2, b0, b1, b2, gain_own, gain_oth, h_own, h_oth, n_out):
    own = x_own[...].astype(F32) + summed((a0, a1, a2))
    oth = x_oth[...].astype(F32) + summed((b0, b1, b2))
    scale = rows_scale(own, oth)
    half = own.shape[-1]
    h_own[...] = own
    h_oth[...] = oth
    n_out[:, :half] = (own * scale * gain_own[...]).astype(BF16)
    n_out[:, half:] = (oth * scale * gain_oth[...]).astype(BF16)


def block_out_kernel(hi, at, h_own, h_oth, t0, t1, t2, out):
    x = at[0]
    width = h_own.shape[-1] // hi
    for k in range(hi):
        cols = [slice(j * width, (j + 1) * width) for j in (2 * k, 2 * k + 1)]
        own, oth = (sum(t[:, col].astype(F32) for t in (t0, t1, t2)) for col in cols)
        own += h_own[:, k * width : (k + 1) * width]
        oth += h_oth[:, k * width : (k + 1) * width]
        out[:, cols[0]] = jnp.where(x == 0, own, oth)
        out[:, cols[1]] = jnp.where(x == 0, oth, own)


def back_of(own, oth, scale, gain_own, gain_oth, up_own, up_oth):
    w_own, w_oth = up_own * gain_own, up_oth * gain_oth
    total = jnp.sum(w_own * own, axis=-1, keepdims=True) + jnp.sum(w_oth * oth, axis=-1, keepdims=True)
    cube = scale * scale * scale * (total / (own.shape[-1] + oth.shape[-1]))
    return scale * w_own - own * cube, scale * w_oth - oth * cube


def middle_kernel(
    hi, at, h_own, h_oth, a0, a1, a2, b0, b1, b2, gain_own, gain_oth, upstream, r_own, r_oth, low_out, s_own, s_oth
):
    own, oth = h_own[...], h_oth[...]
    up_own, up_oth = summed((a0, a1, a2)), summed((b0, b1, b2))
    scale = rows_scale(own, oth)
    back_own, back_oth = back_of(own, oth, scale, gain_own[...], gain_oth[...], up_own, up_oth)
    u_own, u_oth = (jnp.concatenate(part, axis=1) for part in halves_of(upstream[...].astype(F32), hi, at[0]))
    back_own = u_own + back_own
    back_oth = u_oth + back_oth
    half = own.shape[-1]
    r_own[...] = back_own
    r_oth[...] = back_oth
    low_out[:, :half] = back_own.astype(BF16)
    low_out[:, half:] = back_oth.astype(BF16)

    @pl.when(pl.program_id(0) == 0)
    def _():
        s_own[...] = jnp.zeros_like(s_own)
        s_oth[...] = jnp.zeros_like(s_oth)

    s_own[...] += jnp.sum(up_own * own * scale, axis=0, keepdims=True)
    s_oth[...] += jnp.sum(up_oth * oth * scale, axis=0, keepdims=True)


def grad_in_kernel(hi, at, x_own, x_oth, a0, a1, a2, b0, b1, b2, gain_own, gain_oth, r_own, r_oth, out):
    own, oth = x_own[...].astype(F32), x_oth[...].astype(F32)
    scale = rows_scale(own, oth)
    back_own, back_oth = back_of(
        own, oth, scale, gain_own[...], gain_oth[...], summed((a0, a1, a2)), summed((b0, b1, b2))
    )
    join_to(out, r_own[...] + back_own, r_oth[...] + back_oth, hi, at[0])


def project_kernel(n_own, n_oth, w_own, w_oth, out):
    out[...] = (dot(n_own[...], w_own[...]) + dot(n_oth[...], w_oth[...])).astype(out.dtype)


def put_rows(kept, sent, value):
    stay = pl.program_id(0) < pl.num_programs(0) // 2

    @pl.when(stay)
    def _():
        kept[...] = value

    @pl.when(jnp.logical_not(stay))
    def _():
        sent[...] = value


def project_back_kernel(rows, weight, kept, sent):
    put_rows(kept, sent, dot_rt(rows[...], weight[...]).astype(BF16))


def project_gain_kernel(grad, weight, normed, kept, sent, sums):
    part = dot_rt(grad[...], weight[...])
    put_rows(kept, sent, part.astype(BF16))

    @pl.when(pl.program_id(0) == 0)
    def _():
        sums[...] = jnp.zeros_like(sums)

    sums[...] += jnp.sum(part * normed[...].astype(F32), axis=0, keepdims=True)


def weight_grad_kernel(rows, grad, out):
    out[...] = dot_lt(rows[...], grad[...]).astype(out.dtype)


def weight_grad_add_kernel(rows, grad, came, out):
    out[...] = (dot_lt(rows[...], grad[...]) + came[...].astype(F32)).astype(BF16)


def add_kernel(first, second, out):
    out[...] = (first[...].astype(F32) + second[...].astype(F32)).astype(BF16)


def total_kernel(near, came, gains, out):
    depth = near.shape[0]
    out[:depth] = (near[...] + came[...].astype(F32)).astype(BF16)
    out[depth:] = gains[...]


def expand_kernel(n_own, n_oth, u_own, u_oth, gate_in, inner, for_gate, for_up):
    gate = gate_in[...]
    up = dot(n_own[...], u_own[...]) + dot(n_oth[...], u_oth[...])
    sigmoid = jax.nn.sigmoid(gate)
    active = gate * sigmoid
    inner[...] = (active * up).astype(BF16)
    for_gate[...] = (up * sigmoid * (1.0 + gate * (1.0 - sigmoid))).astype(BF16)
    for_up[...] = active.astype(BF16)


def inner_back_kernel(grad, weight, for_gate, for_up, gate_g, up_g):
    inner_g = dot(grad[...], weight[...])
    gate_g[...] = (inner_g * for_gate[...].astype(F32)).astype(BF16)
    up_g[...] = (inner_g * for_up[...].astype(F32)).astype(BF16)


def expand_back_kernel(gate_g, up_g, gate_w, up_w, kept, sent):
    put_rows(kept, sent, (dot_rt(gate_g[...], gate_w[...]) + dot_rt(up_g[...], up_w[...])).astype(BF16))


def partner(value):
    lane = lax.broadcasted_iota(jnp.int32, value.shape, 1)
    return jnp.where(lane % HD < HD // 2, pltpu.roll(value, PAIR - HD // 2, 1), pltpu.roll(value, HD // 2, 1))


def low_lanes(shape):
    return lax.broadcasted_iota(jnp.int32, shape, 1) < HD


def set_bias(bias, key_at, query_at, first):
    keys, queries = key_at[...], query_at[...]
    key_in = ((keys >= first) & (keys < first + SPAN)).astype(jnp.int32)
    query_in = ((queries >= first) & (queries < first + SPAN)).astype(jnp.int32)
    seen = (keys <= queries).astype(jnp.int32) + key_in * query_in
    bias[...] = jnp.where(seen > 0, 0.0, MASKED)


def attend_kernel(pairs, span, qkv, cos, sine, key_at, query_at, q_out, kv_out, o_out, lse_out, bias, key_s, val_s):
    length = cos.shape[0]
    set_bias(bias, key_at, query_at, span[pl.program_id(0)])
    kv = qkv[:, 0, :, pairs * PAIR :].reshape(length, PAIR)
    low = low_lanes(kv.shape)
    turned = kv * cos[...] + partner(kv) * sine[...]
    kv = jnp.where(low, turned, kv).astype(BF16)
    kv_out[:, 0] = kv.reshape(4, length // 4, PAIR)
    wide = kv.astype(F32)
    key_even = jnp.where(low, wide, 0.0)
    val_odd = jnp.where(low, 0.0, wide)
    key_s[0] = key_even.astype(BF16)
    key_s[1] = pltpu.roll(key_even, HD, 1).astype(BF16)
    val_s[0] = pltpu.roll(val_odd, HD, 1).T.astype(BF16)
    val_s[1] = val_odd.T.astype(BF16)

    def pair_step(j, _):
        cols = pl.ds(pl.multiple_of(j * PAIR, PAIR), PAIR)
        raw = qkv[:, 0, :, cols].reshape(length, PAIR)
        query = (raw * cos[...] + partner(raw) * sine[...]).astype(BF16)
        q_out[:, 0, :, cols] = query.reshape(4, length // 4, PAIR)
        query_t = (query.astype(F32) * HD**-0.5).T.astype(BF16)
        mixed = jnp.zeros((PAIR, length), F32)
        for k in range(2):
            scores = dot(key_s[k], query_t) + bias[...]
            top = jnp.max(scores, axis=0, keepdims=True)
            raised = jnp.exp(scores - top)
            total = jnp.sum(raised, axis=0, keepdims=True)
            lse_out[0, pl.ds(2 * j + k, 1), :] = top + jnp.log(total)
            mixed += dot(val_s[k], (raised * (1.0 / total)).astype(BF16))
        o_out[:, 0, :, cols] = mixed.T.astype(BF16).reshape(4, length // 4, PAIR)
        return 0

    lax.fori_loop(0, pairs, pair_step, 0)


def attend_back_kernel(
    pairs, span, query_in, kv_in, grad_in, lse, cos, sine, key_at, query_at, out, bias, key_s, key_t, val_s, key_g, val_g
):
    length = cos.shape[0]
    set_bias(bias, key_at, query_at, span[pl.program_id(0)])
    kv = kv_in[:, 0].reshape(length, PAIR).astype(F32)
    low = low_lanes(kv.shape)
    key_even = jnp.where(low, kv, 0.0)
    key_odd = pltpu.roll(key_even, HD, 1)
    val_odd = jnp.where(low, 0.0, kv)
    key_s[0] = key_even.astype(BF16)
    key_s[1] = key_odd.astype(BF16)
    key_t[0] = key_even.T.astype(BF16)
    key_t[1] = key_odd.T.astype(BF16)
    val_s[0] = pltpu.roll(val_odd, HD, 1).astype(BF16)
    val_s[1] = val_odd.astype(BF16)
    key_g[...] = jnp.zeros_like(key_g)
    val_g[...] = jnp.zeros_like(val_g)

    def pair_step(j, _):
        cols = pl.ds(pl.multiple_of(j * PAIR, PAIR), PAIR)
        query = query_in[:, 0, :, cols].reshape(length, PAIR)
        grad = grad_in[:, 0, :, cols].reshape(length, PAIR)
        query_t = (query.astype(F32) * HD**-0.5).T.astype(BF16)
        grad_t = grad.astype(F32).T.astype(BF16)
        query_g = jnp.zeros((PAIR, length), F32)
        for k in range(2):
            scores = dot(key_s[k], query_t) + bias[...]
            weight = jnp.exp(scores - lse[0, pl.ds(2 * j + k, 1), :])
            weight_g = dot(val_s[k], grad_t)
            val_g[k] += dot(weight.astype(BF16), grad)
            delta = jnp.sum(weight * weight_g, axis=0, keepdims=True)
            score_g = (HD**-0.5 * (weight * (weight_g - delta))).astype(BF16)
            key_g[k] += dot(score_g, query)
            query_g += dot(key_t[k], score_g)
        value = query_g.T
        value = value * cos[...] - partner(value) * sine[...]
        out[:, 0, :, cols] = value.astype(BF16).reshape(4, length // 4, PAIR)
        return 0

    lax.fori_loop(0, pairs, pair_step, 0)
    keys = key_g[0] + pltpu.roll(key_g[1], HD, 1)
    vals = val_g[1] + pltpu.roll(val_g[0], HD, 1)
    keys = keys * cos[...] - partner(keys) * sine[...]
    out[:, 0, :, pairs * PAIR :] = jnp.where(low, keys, vals).astype(BF16).reshape(4, length // 4, PAIR)


def per_device(
    block_in, span_start, w_query, w_key, w_value, w_out, w_gate, w_up, w_down, gain_attn, gain_mlp, cotangent
):
    z, x, y, c = (lax.axis_index(name) for name in ("fh", "fl", "th", "tl"))
    hi = lax.axis_size("fh")
    batch, rows, width = block_in.shape
    own_rows, half = batch * rows, width // 2
    length = rows * 4
    depth = w_query.shape[0]
    q_cols, kv_cols = w_query.shape[1], w_key.shape[1]
    pairs = q_cols // PAIR
    at = jnp.stack([x]).astype(jnp.int32)

    shard = jnp.concatenate([w_query, w_key, w_value], axis=1)
    gains = jnp.concatenate([gain_attn, gain_mlp])[None]
    gains = jnp.pad(gains, ((0, ROW_PAD - 1), (0, shard.shape[1] - gains.shape[1])))
    shard = jnp.concatenate([shard, gains], axis=0)

    def gather(part):
        return lax.all_gather(part, "fh", axis=0, tiled=True)

    def swap_x(value):
        return swap(value, "fl")

    down_shard = w_down.T
    down_pair = jnp.concatenate([down_shard, swap_x(down_shard)], axis=0)
    attn_own, out_own, gate_own, up_own = gather(shard), gather(w_out.T), gather(w_gate), gather(w_up)
    down_w = gather(down_pair)

    def gather_rows(piece):
        beside = swap(piece, "tl")
        across = swap(piece, "th")
        return piece, across, beside, swap(across, "tl")

    token_parts = gather_rows(block_in.reshape(own_rows, width))
    cot_own = cotangent.reshape(own_rows, width)
    cot_parts = gather_rows(after(101, cot_own, token_parts[1]))

    place = jnp.concatenate(
        [(((y + dy) % 2) * 2 + (c + dc) % 2) * rows + jnp.arange(rows, dtype=jnp.int32) for dc in (0, 1) for dy in (0, 1)]
    )
    frequency = jnp.exp(jnp.arange(HD // 2, dtype=F32) * (-2.0 * math.log(10000.0) / HD))
    angles = place.astype(F32)[:, None] * frequency[None, :]
    cos = jnp.tile(jnp.cos(angles), (1, 4))
    sine = jnp.sin(angles)
    sine = jnp.concatenate([-sine, sine, -sine, sine], axis=1)
    key_at, query_at = place[:, None], place[None, :]
    span = span_start[:, 0]
    tables = [(t, full_spec(t.shape)) for t in (cos, sine, key_at, query_at)]

    quad = (4, batch, rows)
    all_rows = 4 * own_rows
    tile = 256
    steps = all_rows // tile
    hidden = w_gate.shape[1]
    all_cols = q_cols + 2 * kv_cols
    tiles = lambda *values: [(v, row_spec(tile, v.shape[1])) for v in values]
    wholes = lambda *values: [(v, whole_spec(v)) for v in values]
    pieces = lambda parts: [(p, row_spec(rows, width)) for p in parts]
    half_ins = lambda *values: [(v, row_spec(rows, half)) for v in values]
    gain_in = lambda gain: [(g, full_spec((1, half))) for g in gain]
    spread_outs = [(quad + (half,), BF16, quad_spec(rows, half))] * 2
    half_outs = [((own_rows, half), F32, row_spec(rows, half))] * 2
    low_out = [((own_rows, width), BF16, row_spec(rows, width))]
    whole_out = [((own_rows, width), F32, row_spec(rows, width))]
    sum_outs = [((1, half), F32, full_spec((1, half)))]
    hidden_out = ((all_rows, hidden), BF16, row_spec(tile, hidden))

    def tiles_of(size, *values):
        return [(v, row_spec(size, v.shape[1])) for v in values]

    def as_rows(value):
        return value.reshape(all_rows, value.shape[-1])

    def project(step, pair, weights, kind):
        cols = weights[0].shape[1]
        out = ((all_rows, cols), kind, row_spec(tile, cols))
        return call(step, project_kernel, [], steps, tiles(*pair) + wholes(*weights), [out])[0]

    def project_back(step, value, weight):
        outs = two_part_outs(all_rows, weight.shape[0], tile)
        return call(step, project_back_kernel, [], steps, tiles(value) + wholes(weight), outs)

    def weight_grad(step, value, grad, came=None, kind=BF16):
        part, cols = 256, grad.shape[1]
        ins = [(value, pl.BlockSpec((value.shape[0], part), lambda i: (0, i)))] + wholes(grad)
        ins += [] if came is None else [(came, row_spec(part, cols))]
        out = ((value.shape[1], cols), kind, row_spec(part, cols))
        kernel = weight_grad_kernel if came is None else weight_grad_add_kernel
        return call(step, kernel, [], value.shape[1] // part, ins, [out])[0]

    def scatter_rows(step, kept, sent, order=None, *others):
        cols = kept.shape[1]
        came = swap(sent, "tl")
        (passed,) = call(
            step,
            add_kernel,
            [],
            batch,
            [(kept, row_spec(rows, cols, batch)), (came, row_spec(rows, cols, batch))],
            [((own_rows, cols), BF16, row_spec(rows, cols))],
        )
        across = after(order, passed, *others) if others else passed
        return kept, came, swap(across, "th"), passed

    def terms(*scattered):
        return [(t, row_spec(rows, t.shape[1])) for part in scattered for t in part[:3]]

    def stack_rows(step, low, across, order, *others):
        beside, across = swap(low, "tl"), after(order, across, *others)
        parts = (low, across, beside, swap(across, "tl"))
        return tuple(as_rows(v) for v in call(step, stack_kernel, [], batch, pieces(parts), spread_outs))

    attn_own = after(102, attn_own, down_pair)
    attn_pair = tuple(part.reshape(hi, depth + ROW_PAD, -1) for part in (attn_own, swap_x(attn_own)))
    qkv_w = tuple(part[:, :depth].reshape(hi * depth, -1) for part in attn_pair)
    out_w = (out_own, swap_x(after(138, out_own, attn_pair[1])))
    gain_one = tuple(part[:, depth, :depth].reshape(1, half).astype(F32) for part in attn_pair)
    gain_two = tuple(part[:, depth, depth : 2 * depth].reshape(1, half).astype(F32) for part in attn_pair)

    *seq_one, x_own, x_oth = call(
        2,
        functools.partial(norm_in_kernel, hi),
        [at],
        batch,
        pieces(token_parts) + gain_in(gain_one),
        spread_outs + [((own_rows, half), BF16, row_spec(rows, half))] * 2,
    )
    seq_one = tuple(as_rows(v) for v in seq_one)
    gate_near = after(105, after(104, gate_own, out_w[1]), seq_one[0])
    gate_w = (gate_own, swap_x(gate_near))
    up_w = (up_own, swap_x(after(106, up_own, gate_w[1])))

    qkv = project(3, seq_one, qkv_w, F32)
    qkv = after(144, after(107, qkv, out_w[1]), cot_parts[1])
    pair_spec, q_spec = quad_spec(rows, PAIR), quad_spec(rows, q_cols)
    lse_spec = pl.BlockSpec((1, 2 * pairs, length), lambda i, *_: (i, 0, 0))
    query_rot, kv_rot, mixed, lse = call(
        4,
        functools.partial(attend_kernel, pairs),
        [span],
        batch,
        [(qkv.reshape(quad + (all_cols,)), quad_spec(rows, all_cols)), *tables],
        [
            (quad + (q_cols,), BF16, q_spec),
            (quad + (PAIR,), BF16, pair_spec),
            (quad + (q_cols,), BF16, q_spec),
            ((batch, 2 * pairs, length), F32, lse_spec),
        ],
        [
            pltpu.VMEM((length, length), F32),
            pltpu.VMEM((2, length, PAIR), BF16),
            pltpu.VMEM((2, PAIR, length), BF16),
        ],
    )
    mixed = as_rows(mixed)
    attn_oth = scatter_rows(6, *project_back(5, mixed, out_w[1]))
    attn_own = scatter_rows(8, *project_back(7, after(108, mixed, attn_oth[3]), out_w[0]))
    h_own, h_oth, normed_two = call(
        9,
        residual_kernel,
        [],
        batch,
        half_ins(after(109, x_own, gate_own), x_oth) + terms(attn_own, attn_oth) + gain_in(gain_two),
        half_outs + low_out,
    )
    (seq_cot,) = call(
        1,
        functools.partial(pairs_kernel, hi),
        [at],
        batch,
        pieces((after(103, cot_own, normed_two), *cot_parts[1:])),
        [(quad + (width,), BF16, quad_spec(rows, width))],
    )
    seq_cot = as_rows(seq_cot)
    seq_two = stack_rows(10, normed_two, swap(normed_two, "th"), 111, gate_w[1], seq_cot)
    gate_pre = project(38, seq_two, gate_w, F32)
    inner, for_gate, for_up = call(
        11, expand_kernel, [], steps, tiles(*seq_two) + wholes(*up_w) + tiles(gate_pre), [hidden_out] * 3
    )

    def reduce_z(total):
        return lax.psum_scatter(total, "fh", scatter_dimension=0, tiled=True)

    down_part = weight_grad(12, seq_cot, inner)
    grad_down = reduce_z(down_part)
    gate_g, up_g = call(
        13,
        inner_back_kernel,
        [],
        steps,
        tiles(after(112, seq_cot, down_part)) + wholes(down_w) + tiles(for_gate, for_up),
        [hidden_out] * 2,
    )

    def expand_back(step, which, gate_g):
        outs = two_part_outs(all_rows, half, tile)
        ins = tiles(gate_g, up_g) + wholes(gate_w[which], up_w[which])
        return call(step, expand_back_kernel, [], steps, ins, outs)

    gate_sent = weight_grad(16, seq_two[1], gate_g)
    gate_came = swap_x(gate_sent)
    oth_parts = expand_back(14, 1, after(113, gate_g, gate_sent))
    normed_oth = scatter_rows(15, *oth_parts)
    own_parts = expand_back(17, 0, after(116, after(115, gate_g, oth_parts[0]), normed_oth[3]))
    normed_own = scatter_rows(18, *own_parts)
    up_sent = weight_grad(19, seq_two[1], after(117, up_g, normed_own[3]))
    gate_came = after(147, gate_came, up_sent)
    gate_came = after(149, after(148, gate_came, normed_oth[2]), normed_own[2])
    up_came = swap_x(after(122, up_sent, gate_came))
    gate_total = weight_grad(23, seq_two[0], gate_g, gate_came)
    grad_gate = reduce_z(gate_total)
    r_own, r_oth, attn_low, gain_s_own, gain_s_oth = call(
        20,
        functools.partial(middle_kernel, hi),
        [at],
        batch,
        half_ins(after(120, after(118, h_own, up_sent), gate_total), h_oth)
        + terms(normed_own, normed_oth)
        + gain_in(gain_two)
        + [(cot_own, row_spec(rows, width))],
        half_outs + low_out + sum_outs * 2,
    )
    block_parts = project_back(21, after(150, after(119, inner, attn_low), gate_total), down_w)

    attn_far = swap(attn_low, "th")
    up_came = after(127, after(126, up_came, block_parts[0]), grad_down)
    up_total = weight_grad(28, seq_two[0], up_g, up_came)
    grad_up = reduce_z(up_total)
    seq_attn = stack_rows(24, attn_low, attn_far, 123, up_total)
    block_terms = scatter_rows(22, block_parts[0], after(124, block_parts[1], seq_attn[0]))
    grad_mixed = project(25, seq_attn, out_w, BF16)
    out_sent = weight_grad(26, after(125, seq_attn[1], grad_mixed), mixed)
    out_came = swap_x(after(128, out_sent, up_came))
    grad_mixed = after(156, after(139, grad_mixed, out_sent), block_terms[3])
    (qkv_g,) = call(
        27,
        functools.partial(attend_back_kernel, pairs),
        [span],
        batch,
        [
            (query_rot, q_spec),
            (kv_rot, pair_spec),
            (grad_mixed.reshape(quad + (q_cols,)), q_spec),
            (lse, lse_spec),
            *tables,
        ],
        [(quad + (all_cols,), BF16, quad_spec(rows, all_cols))],
        [
            pltpu.VMEM((length, length), F32),
            pltpu.VMEM((2, length, PAIR), BF16),
            pltpu.VMEM((2, PAIR, length), BF16),
            pltpu.VMEM((2, length, PAIR), BF16),
            pltpu.VMEM((2, length, PAIR), F32),
            pltpu.VMEM((2, length, PAIR), F32),
        ],
    )
    qkv_g = after(141, after(140, after(129, as_rows(qkv_g), out_came), block_terms[2]), grad_gate)

    def project_gain(step, which, grad):
        outs = two_part_outs(all_rows, half, tile) + sum_outs
        kept, sent, sums = call(
            step, project_gain_kernel, [], steps, tiles(grad) + wholes(qkv_w[which]) + tiles(seq_one[which]), outs
        )
        return (kept, sent), sums / gain_one[which]

    qkv_sent = weight_grad(31, seq_one[1], qkv_g)
    qkv_came = swap_x(after(134, qkv_sent, out_came))
    out_total = weight_grad(34, seq_attn[0], mixed, after(155, after(132, out_came, qkv_sent), qkv_g))
    grad_out = reduce_z(out_total)
    oth_parts, oth_gain = project_gain(29, 1, after(131, qkv_g, out_total))
    first_oth = scatter_rows(30, *oth_parts)
    own_parts, own_gain = project_gain(32, 0, after(143, after(142, qkv_g, first_oth[3]), out_total))
    first_own = scatter_rows(33, *own_parts)
    qkv_near = weight_grad(35, seq_one[0], after(133, qkv_g, first_own[3]), kind=F32)

    def gain_pair(one, two):
        return jnp.concatenate([one.reshape(hi, depth), two.reshape(hi, depth)], axis=1)

    gain_own, gain_oth = gain_pair(own_gain, gain_s_own), gain_pair(oth_gain, gain_s_oth)
    gain_both = jnp.stack([gain_own, gain_oth])
    gain_both = gain_both + swap(gain_both, "tl")
    gain_both = gain_both + swap(gain_both, "th")
    gain_rows = gain_both[0] + swap_x(gain_both[1])
    gain_rows = jnp.pad(gain_rows[:, None], ((0, 0), (0, ROW_PAD - 1), (0, all_cols - 2 * depth))).astype(BF16)
    (qkv_total,) = call(
        39,
        total_kernel,
        [],
        hi,
        tiles_of(depth, qkv_near, after(152, after(151, after(135, qkv_came, grad_up), first_oth[2]), first_own[2]))
        + tiles_of(ROW_PAD, gain_rows.reshape(hi * ROW_PAD, all_cols)),
        [((hi * (depth + ROW_PAD), all_cols), BF16, row_spec(depth + ROW_PAD, all_cols))],
    )
    grad_qkv = reduce_z(qkv_total).astype(F32)
    gain_sums = grad_qkv[depth, : 2 * depth]
    grad_qkv = grad_qkv[:depth]
    (block_out,) = call(
        36,
        functools.partial(block_out_kernel, hi),
        [at],
        batch,
        half_ins(after(137, after(136, h_own, qkv_total), grad_up), h_oth) + terms(block_terms),
        whole_out,
    )

    (grad_in,) = call(
        37,
        functools.partial(grad_in_kernel, hi),
        [at],
        batch,
        half_ins(x_own, x_oth) + terms(first_own, first_oth) + gain_in(gain_one) + half_ins(r_own, r_oth),
        whole_out,
    )
    grad_down = grad_down[:depth].astype(F32) + swap_x(grad_down[depth:]).astype(F32)
    return (
        block_out.reshape(block_in.shape),
        grad_in.reshape(block_in.shape),
        grad_qkv[:, :q_cols],
        grad_qkv[:, q_cols : q_cols + kv_cols],
        grad_qkv[:, q_cols + kv_cols :],
        grad_out.astype(F32).T,
        grad_gate.astype(F32),
        grad_up.astype(F32),
        grad_down.T,
        gain_sums[:depth],
        gain_sums[depth:],
    )


def solution(mesh):
    n_fsdp, n_tp = mesh.shape["fsdp"], mesh.shape["tp"]
    fine = Mesh(mesh.devices.reshape(n_fsdp // 2, 2, n_tp // 2, 2), ("fh", "fl", "th", "tl"))
    fsdp, tp = ("fh", "fl"), ("th", "tl")
    rows = P(None, fsdp + tp, None)
    up, across, flat = P(fsdp, tp), P(tp, fsdp), P(fsdp)
    return jax.shard_map(
        per_device,
        mesh=fine,
        in_specs=(rows, P(None, fsdp), up, up, up, across, up, up, across, flat, flat, rows),
        out_specs=(rows, rows, up, up, up, across, up, up, across, flat, flat),
        check_vma=False,
    )
```

```python
import functools
import math

import jax
import jax.numpy as jnp
from jax import lax
from jax.experimental import pallas as pl
from jax.experimental.pallas import tpu as pltpu
from jax.sharding import Mesh, PartitionSpec as P

HD = 64
PAIR = 2 * HD
SPAN = 256
EPS = 1e-05
MASKED = -1e30
F32 = jnp.float32
BF16 = jnp.bfloat16
SWAP = [(0, 1), (1, 0)]
COST = {1: 1702, 2: 2220, 3: 2582, 4: 5630, 5: 1730, 6: 798, 7: 1730, 8: 798, 9: 1498, 10: 1626, 11: 4596, 12: 3950, 13: 4338, 14: 3898, 15: 798, 16: 2348, 17: 3872, 18: 798, 19: 2348, 20: 1986, 21: 3820, 22: 1006, 23: 2556, 24: 1626, 25: 2142, 26: 8118, 27: 127702, 28: 10228, 29: 33062, 31: 1626, 32: 1476, 34: 1522, 36: 1498, 37: 53466, 38: 3898, 39: 23246}
SKIP = {133, 134, 103, 137, 107, 139, 142, 116, 150, 151, 120, 122, 158, 159}
ROW_PAD = 16


def dot(a, b):
    return jnp.dot(a, b, preferred_element_type=F32)


def dot_lt(a, b):
    return lax.dot_general(a, b, (((0,), (0,)), ((), ())), preferred_element_type=F32)


def dot_rt(a, b):
    return lax.dot_general(a, b, (((1,), (1,)), ((), ())), preferred_element_type=F32)


def swap(value, axis):
    return lax.ppermute(value, axis, SWAP)


def after(step, value, *others):
    if step in SKIP:
        return value
    return lax.optimization_barrier((value, *others))[0]


def full_spec(shape):
    return pl.BlockSpec(shape, lambda i, *_: (0,) * len(shape))


def row_spec(rows, cols, offset=0):
    return pl.BlockSpec((rows, cols), lambda i, *_: (i + offset, 0))


def quad_spec(rows, cols):
    return pl.BlockSpec((4, 1, rows, cols), lambda i, *_: (0, i, 0, 0))


def two_part_outs(rows, cols, tile):
    half = rows // tile // 2
    first = pl.BlockSpec((tile, cols), lambda i, *_: (jnp.minimum(i, half - 1), 0))
    second = pl.BlockSpec((tile, cols), lambda i, *_: (jnp.maximum(i - half, 0), 0))
    return [((rows // 2, cols), BF16, first), ((rows // 2, cols), BF16, second)]


def whole_spec(array):
    return pl.BlockSpec(array.shape, lambda i, *_: (0, 0), pipeline_mode=pl.Buffered(1))


def call(step, kernel, scalars, grid, ins, outs, scratch=()):
    work = COST.get(step, 0) * 1000
    return pl.pallas_call(
        kernel,
        out_shape=[jax.ShapeDtypeStruct(shape, kind) for shape, kind, _ in outs],
        grid_spec=pltpu.PrefetchScalarGridSpec(
            num_scalar_prefetch=len(scalars),
            grid=(grid,),
            in_specs=[spec for _, spec in ins],
            out_specs=[spec for _, _, spec in outs],
            scratch_shapes=list(scratch),
        ),
        cost_estimate=pl.CostEstimate(flops=work * 300, bytes_accessed=work + step, transcendentals=0),
        compiler_params=pltpu.CompilerParams(vmem_limit_bytes=56 << 20),
    )(*scalars, *[a for a, _ in ins])


def halves_of(value, hi, x):
    width = value.shape[-1] // (2 * hi)
    parts = [value[:, k * width : (k + 1) * width] for k in range(2 * hi)]
    even, odd = parts[0::2], parts[1::2]
    own = [jnp.where(x == 0, a, b) for a, b in zip(even, odd)]
    oth = [jnp.where(x == 0, b, a) for a, b in zip(even, odd)]
    return own, oth


def put_cols(ref, index, parts):
    width = parts[0].shape[-1]
    for k, part in enumerate(parts):
        ref[(*index, slice(None), slice(k * width, (k + 1) * width))] = part.astype(ref.dtype)


def join_to(ref, own, oth, hi, x):
    width = own.shape[-1] // hi
    for k in range(hi):
        a, b = own[:, k * width : (k + 1) * width], oth[:, k * width : (k + 1) * width]
        ref[:, 2 * k * width : (2 * k + 1) * width] = jnp.where(x == 0, a, b)
        ref[:, (2 * k + 1) * width : (2 * k + 2) * width] = jnp.where(x == 0, b, a)


def norm_in_kernel(hi, at, p0, p1, p2, p3, gain_own, gain_oth, n_own, n_oth, x_own, x_oth):
    x = at[0]
    half = n_own.shape[-1]
    for k, piece in enumerate((p0, p1, p2, p3)):
        low = piece[...]
        value = low.astype(F32)
        scale = lax.rsqrt(jnp.mean(value * value, axis=-1, keepdims=True) + EPS)
        own, oth = halves_of(value, hi, x)
        width = half // hi
        for part, gain, ref in ((own, gain_own, n_own), (oth, gain_oth, n_oth)):
            put_cols(
                ref, (k, 0), [v * scale * gain[:, z * width : (z + 1) * width] for z, v in enumerate(part)]
            )
        if k == 0:
            put_cols(x_own, (), own)
            put_cols(x_oth, (), oth)


def spread_kernel(hi, at, p0, p1, p2, p3, o_own, o_oth):
    x = at[0]
    for k, piece in enumerate((p0, p1, p2, p3)):
        own, oth = halves_of(piece[...], hi, x)
        put_cols(o_own, (k, 0), own)
        put_cols(o_oth, (k, 0), oth)


def pairs_kernel(hi, at, p0, p1, p2, p3, out):
    x = at[0]
    for k, piece in enumerate((p0, p1, p2, p3)):
        own, oth = halves_of(piece[...], hi, x)
        put_cols(out, (k, 0), [part for pair in zip(own, oth) for part in pair])


def stack_kernel(p0, p1, p2, p3, o_own, o_oth):
    half = o_own.shape[-1]
    for k, piece in enumerate((p0, p1, p2, p3)):
        o_own[k, 0] = piece[:, :half]
        o_oth[k, 0] = piece[:, half:]


def rows_scale(own, oth):
    total = jnp.sum(own * own, axis=-1, keepdims=True) + jnp.sum(oth * oth, axis=-1, keepdims=True)
    return lax.rsqrt(total / (own.shape[-1] + oth.shape[-1]) + EPS)


def summed(refs):
    return refs[0][...].astype(F32) + refs[1][...].astype(F32) + refs[2][...].astype(F32)


def residual_kernel(x_own, x_oth, a0, a1, a2, b0, b1, b2, gain_own, gain_oth, h_own, h_oth, n_out):
    own = x_own[...].astype(F32) + summed((a0, a1, a2))
    oth = x_oth[...].astype(F32) + summed((b0, b1, b2))
    scale = rows_scale(own, oth)
    half = own.shape[-1]
    h_own[...] = own
    h_oth[...] = oth
    n_out[:, :half] = (own * scale * gain_own[...]).astype(BF16)
    n_out[:, half:] = (oth * scale * gain_oth[...]).astype(BF16)


def block_out_kernel(hi, at, h_own, h_oth, t0, t1, t2, out):
    x = at[0]
    width = h_own.shape[-1] // hi
    for k in range(hi):
        cols = [slice(j * width, (j + 1) * width) for j in (2 * k, 2 * k + 1)]
        own, oth = (sum(t[:, col].astype(F32) for t in (t0, t1, t2)) for col in cols)
        own += h_own[:, k * width : (k + 1) * width]
        oth += h_oth[:, k * width : (k + 1) * width]
        out[:, cols[0]] = jnp.where(x == 0, own, oth)
        out[:, cols[1]] = jnp.where(x == 0, oth, own)


def back_of(own, oth, scale, gain_own, gain_oth, up_own, up_oth):
    w_own, w_oth = up_own * gain_own, up_oth * gain_oth
    total = jnp.sum(w_own * own, axis=-1, keepdims=True) + jnp.sum(w_oth * oth, axis=-1, keepdims=True)
    cube = scale * scale * scale * (total / (own.shape[-1] + oth.shape[-1]))
    return scale * w_own - own * cube, scale * w_oth - oth * cube


def middle_kernel(
    hi, at, h_own, h_oth, a0, a1, a2, b0, b1, b2, gain_own, gain_oth, upstream, r_own, r_oth, low_out, s_own, s_oth
):
    own, oth = h_own[...], h_oth[...]
    up_own, up_oth = summed((a0, a1, a2)), summed((b0, b1, b2))
    scale = rows_scale(own, oth)
    back_own, back_oth = back_of(own, oth, scale, gain_own[...], gain_oth[...], up_own, up_oth)
    u_own, u_oth = (jnp.concatenate(part, axis=1) for part in halves_of(upstream[...].astype(F32), hi, at[0]))
    back_own = u_own + back_own
    back_oth = u_oth + back_oth
    half = own.shape[-1]
    r_own[...] = back_own
    r_oth[...] = back_oth
    low_out[:, :half] = back_own.astype(BF16)
    low_out[:, half:] = back_oth.astype(BF16)

    @pl.when(pl.program_id(0) == 0)
    def _():
        s_own[...] = jnp.zeros_like(s_own)
        s_oth[...] = jnp.zeros_like(s_oth)

    s_own[...] += jnp.sum(up_own * own * scale, axis=0, keepdims=True)
    s_oth[...] += jnp.sum(up_oth * oth * scale, axis=0, keepdims=True)


def grad_in_kernel(hi, at, x_own, x_oth, a0, a1, a2, b0, b1, b2, gain_own, gain_oth, r_own, r_oth, out):
    own, oth = x_own[...].astype(F32), x_oth[...].astype(F32)
    scale = rows_scale(own, oth)
    back_own, back_oth = back_of(
        own, oth, scale, gain_own[...], gain_oth[...], summed((a0, a1, a2)), summed((b0, b1, b2))
    )
    join_to(out, r_own[...] + back_own, r_oth[...] + back_oth, hi, at[0])


def project_kernel(n_own, n_oth, w_own, w_oth, out):
    out[...] = (dot(n_own[...], w_own[...]) + dot(n_oth[...], w_oth[...])).astype(out.dtype)


def put_rows(kept, sent, value):
    stay = pl.program_id(0) < pl.num_programs(0) // 2

    @pl.when(stay)
    def _():
        kept[...] = value

    @pl.when(jnp.logical_not(stay))
    def _():
        sent[...] = value


def project_back_kernel(rows, weight, kept, sent):
    put_rows(kept, sent, dot_rt(rows[...], weight[...]).astype(BF16))


def project_gain_kernel(grad, weight, normed, kept, sent, sums):
    part = dot_rt(grad[...], weight[...])
    put_rows(kept, sent, part.astype(BF16))

    @pl.when(pl.program_id(0) == 0)
    def _():
        sums[...] = jnp.zeros_like(sums)

    sums[...] += jnp.sum(part * normed[...].astype(F32), axis=0, keepdims=True)


def weight_grad_kernel(rows, grad, out):
    out[...] = dot_lt(rows[...], grad[...]).astype(out.dtype)


def weight_grad_add_kernel(rows, grad, came, out):
    out[...] = (dot_lt(rows[...], grad[...]) + came[...].astype(F32)).astype(BF16)


def add_kernel(first, second, out):
    out[...] = (first[...].astype(F32) + second[...].astype(F32)).astype(BF16)


def total_kernel(near, came, gains, out):
    depth = near.shape[0]
    out[:depth] = (near[...] + came[...].astype(F32)).astype(BF16)
    out[depth:] = gains[...]


def expand_kernel(n_own, n_oth, u_own, u_oth, gate_in, inner, for_gate, for_up):
    gate = gate_in[...]
    up = dot(n_own[...], u_own[...]) + dot(n_oth[...], u_oth[...])
    sigmoid = jax.nn.sigmoid(gate)
    active = gate * sigmoid
    inner[...] = (active * up).astype(BF16)
    for_gate[...] = (up * sigmoid * (1.0 + gate * (1.0 - sigmoid))).astype(BF16)
    for_up[...] = active.astype(BF16)


def inner_back_kernel(grad, weight, for_gate, for_up, gate_g, up_g):
    inner_g = dot(grad[...], weight[...])
    gate_g[...] = (inner_g * for_gate[...].astype(F32)).astype(BF16)
    up_g[...] = (inner_g * for_up[...].astype(F32)).astype(BF16)


def expand_back_kernel(gate_g, up_g, gate_w, up_w, kept, sent):
    put_rows(kept, sent, (dot_rt(gate_g[...], gate_w[...]) + dot_rt(up_g[...], up_w[...])).astype(BF16))


def partner(value):
    lane = lax.broadcasted_iota(jnp.int32, value.shape, 1)
    return jnp.where(lane % HD < HD // 2, pltpu.roll(value, PAIR - HD // 2, 1), pltpu.roll(value, HD // 2, 1))


def low_lanes(shape):
    return lax.broadcasted_iota(jnp.int32, shape, 1) < HD


def set_bias(bias, key_at, query_at, first):
    keys, queries = key_at[...], query_at[...]
    key_in = ((keys >= first) & (keys < first + SPAN)).astype(jnp.int32)
    query_in = ((queries >= first) & (queries < first + SPAN)).astype(jnp.int32)
    seen = (keys <= queries).astype(jnp.int32) + key_in * query_in
    bias[...] = jnp.where(seen > 0, 0.0, MASKED)


def attend_kernel(pairs, span, qkv, cos, sine, key_at, query_at, q_out, kv_out, o_out, lse_out, bias, key_s, val_s):
    length = cos.shape[0]
    set_bias(bias, key_at, query_at, span[pl.program_id(0)])
    kv = qkv[:, 0, :, pairs * PAIR :].reshape(length, PAIR)
    low = low_lanes(kv.shape)
    turned = kv * cos[...] + partner(kv) * sine[...]
    kv = jnp.where(low, turned, kv).astype(BF16)
    kv_out[:, 0] = kv.reshape(4, length // 4, PAIR)
    wide = kv.astype(F32)
    key_even = jnp.where(low, wide, 0.0)
    val_odd = jnp.where(low, 0.0, wide)
    key_s[0] = key_even.astype(BF16)
    key_s[1] = pltpu.roll(key_even, HD, 1).astype(BF16)
    val_s[0] = pltpu.roll(val_odd, HD, 1).T.astype(BF16)
    val_s[1] = val_odd.T.astype(BF16)

    def pair_step(j, _):
        cols = pl.ds(pl.multiple_of(j * PAIR, PAIR), PAIR)
        raw = qkv[:, 0, :, cols].reshape(length, PAIR)
        query = (raw * cos[...] + partner(raw) * sine[...]).astype(BF16)
        q_out[:, 0, :, cols] = query.reshape(4, length // 4, PAIR)
        query_t = (query.astype(F32) * HD**-0.5).T.astype(BF16)
        mixed = jnp.zeros((PAIR, length), F32)
        for k in range(2):
            scores = dot(key_s[k], query_t) + bias[...]
            top = jnp.max(scores, axis=0, keepdims=True)
            raised = jnp.exp(scores - top)
            total = jnp.sum(raised, axis=0, keepdims=True)
            lse_out[0, pl.ds(2 * j + k, 1), :] = top + jnp.log(total)
            mixed += dot(val_s[k], (raised * (1.0 / total)).astype(BF16))
        o_out[:, 0, :, cols] = mixed.T.astype(BF16).reshape(4, length // 4, PAIR)
        return 0

    lax.fori_loop(0, pairs, pair_step, 0)


def with_terms(rows, number):
    high = number.astype(BF16).astype(F32)
    middle = (number - high).astype(BF16).astype(F32)
    low = number - high - middle
    line = lax.broadcasted_iota(jnp.int32, (16, number.shape[1]), 0)
    terms = jnp.where(line == 0, high, jnp.where(line == 1, middle, jnp.where(line == 2, low, 0.0)))
    rest = jnp.zeros((HD - 16, number.shape[1]), BF16)
    return jnp.concatenate([rows.astype(BF16), terms.astype(BF16), rest], axis=0)


def attend_back_kernel(
    pairs, span, query_in, kv_in, grad_in, mixed_in, lse, cos, sine, key_at, query_at, out, bias, key_s, key_t, val_s, key_g, val_g
):
    length = cos.shape[0]
    scale = HD**-0.5
    set_bias(bias, key_at, query_at, span[pl.program_id(0)])
    kv = kv_in[:, 0].reshape(length, PAIR).astype(F32)
    low = low_lanes(kv.shape)
    lane = lax.broadcasted_iota(jnp.int32, kv.shape, 1)
    ones = jnp.where(lane < HD + 3, 1.0, 0.0)
    key_even = jnp.where(low, kv, 0.0)
    key_s[...] = jnp.where(low, kv, ones).astype(BF16)
    val_s[...] = jnp.where(low, pltpu.roll(kv, HD, 1) * scale, ones).astype(BF16)
    key_t[0] = key_even.T.astype(BF16)
    key_t[1] = pltpu.roll(key_even, HD, 1).T.astype(BF16)
    key_g[...] = jnp.zeros_like(key_g)
    val_g[...] = jnp.zeros_like(val_g)

    def pair_step(j, _):
        cols = pl.ds(pl.multiple_of(j * PAIR, PAIR), PAIR)
        query = query_in[:, 0, :, cols].reshape(length, PAIR)
        grad = grad_in[:, 0, :, cols].reshape(length, PAIR)
        mixed = mixed_in[:, 0, :, cols].reshape(length, PAIR)
        query_t = (query.astype(F32) * scale).T
        grad_t = grad.astype(F32).T
        product = grad_t * mixed.astype(F32).T
        query_g = jnp.zeros((PAIR, length), F32)
        for k in range(2):
            part = slice(k * HD, (k + 1) * HD)
            delta = jnp.sum(product[part], axis=0, keepdims=True) * scale
            scores = dot(key_s[...], with_terms(query_t[part], -lse[0, pl.ds(2 * j + k, 1), :]))
            weight = jnp.exp(scores + bias[...])
            weight_g = dot(val_s[...], with_terms(grad_t[part], -delta))
            val_g[k] += dot(weight.astype(BF16), grad)
            score_g = (weight * weight_g).astype(BF16)
            key_g[k] += dot(score_g, query)
            query_g += dot(key_t[k], score_g)
        value = query_g.T
        value = value * cos[...] - partner(value) * sine[...]
        out[:, 0, :, cols] = value.astype(BF16).reshape(4, length // 4, PAIR)
        return 0

    lax.fori_loop(0, pairs, pair_step, 0)
    keys = key_g[0] + pltpu.roll(key_g[1], HD, 1)
    vals = val_g[1] + pltpu.roll(val_g[0], HD, 1)
    keys = keys * cos[...] - partner(keys) * sine[...]
    out[:, 0, :, pairs * PAIR :] = jnp.where(low, keys, vals).astype(BF16).reshape(4, length // 4, PAIR)


def per_device(
    block_in, span_start, w_query, w_key, w_value, w_out, w_gate, w_up, w_down, gain_attn, gain_mlp, cotangent
):
    z, x, y, c = (lax.axis_index(name) for name in ("fh", "fl", "th", "tl"))
    hi = lax.axis_size("fh")
    batch, rows, width = block_in.shape
    own_rows, half = batch * rows, width // 2
    length = rows * 4
    depth = w_query.shape[0]
    q_cols, kv_cols = w_query.shape[1], w_key.shape[1]
    pairs = q_cols // PAIR
    at = jnp.stack([x]).astype(jnp.int32)

    shard = jnp.concatenate([w_query, w_key, w_value], axis=1)
    gains = jnp.concatenate([gain_attn, gain_mlp])[None]
    gains = jnp.pad(gains, ((0, ROW_PAD - 1), (0, shard.shape[1] - gains.shape[1])))
    shard = jnp.concatenate([shard, gains], axis=0)

    def gather(part):
        return lax.all_gather(part, "fh", axis=0, tiled=True)

    def swap_x(value):
        return swap(value, "fl")

    down_shard = w_down.T
    down_pair = jnp.concatenate([down_shard, swap_x(down_shard)], axis=0)
    attn_own, out_own, gate_own, up_own = gather(shard), gather(w_out.T), gather(w_gate), gather(w_up)
    down_w = gather(down_pair)

    def gather_rows(piece):
        beside = swap(piece, "tl")
        across = swap(piece, "th")
        return piece, across, beside, swap(across, "tl")

    token_parts = gather_rows(block_in.reshape(own_rows, width))
    cot_own = cotangent.reshape(own_rows, width)
    cot_parts = gather_rows(after(101, cot_own, token_parts[1]))

    place = jnp.concatenate(
        [(((y + dy) % 2) * 2 + (c + dc) % 2) * rows + jnp.arange(rows, dtype=jnp.int32) for dc in (0, 1) for dy in (0, 1)]
    )
    frequency = jnp.exp(jnp.arange(HD // 2, dtype=F32) * (-2.0 * math.log(10000.0) / HD))
    angles = place.astype(F32)[:, None] * frequency[None, :]
    cos = jnp.tile(jnp.cos(angles), (1, 4))
    sine = jnp.sin(angles)
    sine = jnp.concatenate([-sine, sine, -sine, sine], axis=1)
    key_at, query_at = place[:, None], place[None, :]
    span = span_start[:, 0]
    tables = [(t, full_spec(t.shape)) for t in (cos, sine, key_at, query_at)]

    quad = (4, batch, rows)
    all_rows = 4 * own_rows
    tile = 256
    steps = all_rows // tile
    hidden = w_gate.shape[1]
    all_cols = q_cols + 2 * kv_cols
    tiles = lambda *values: [(v, row_spec(tile, v.shape[1])) for v in values]
    wholes = lambda *values: [(v, whole_spec(v)) for v in values]
    pieces = lambda parts: [(p, row_spec(rows, width)) for p in parts]
    half_ins = lambda *values: [(v, row_spec(rows, half)) for v in values]
    gain_in = lambda gain: [(g, full_spec((1, half))) for g in gain]
    spread_outs = [(quad + (half,), BF16, quad_spec(rows, half))] * 2
    half_outs = [((own_rows, half), F32, row_spec(rows, half))] * 2
    low_out = [((own_rows, width), BF16, row_spec(rows, width))]
    whole_out = [((own_rows, width), F32, row_spec(rows, width))]
    sum_outs = [((1, half), F32, full_spec((1, half)))]
    hidden_out = ((all_rows, hidden), BF16, row_spec(tile, hidden))

    def tiles_of(size, *values):
        return [(v, row_spec(size, v.shape[1])) for v in values]

    def as_rows(value):
        return value.reshape(all_rows, value.shape[-1])

    def project(step, pair, weights, kind):
        cols = weights[0].shape[1]
        out = ((all_rows, cols), kind, row_spec(tile, cols))
        return call(step, project_kernel, [], steps, tiles(*pair) + wholes(*weights), [out])[0]

    def project_back(step, value, weight):
        outs = two_part_outs(all_rows, weight.shape[0], tile)
        return call(step, project_back_kernel, [], steps, tiles(value) + wholes(weight), outs)

    def weight_grad(step, value, grad, came=None, kind=BF16):
        part, cols = 256, grad.shape[1]
        ins = [(value, pl.BlockSpec((value.shape[0], part), lambda i: (0, i)))] + wholes(grad)
        ins += [] if came is None else [(came, row_spec(part, cols))]
        out = ((value.shape[1], cols), kind, row_spec(part, cols))
        kernel = weight_grad_kernel if came is None else weight_grad_add_kernel
        return call(step, kernel, [], value.shape[1] // part, ins, [out])[0]

    def scatter_rows(step, kept, sent, order=None, *others):
        cols = kept.shape[1]
        came = swap(sent, "tl")
        (passed,) = call(
            step,
            add_kernel,
            [],
            batch,
            [(kept, row_spec(rows, cols, batch)), (came, row_spec(rows, cols, batch))],
            [((own_rows, cols), BF16, row_spec(rows, cols))],
        )
        across = after(order, passed, *others) if others else passed
        return kept, came, swap(across, "th"), passed

    def terms(*scattered):
        return [(t, row_spec(rows, t.shape[1])) for part in scattered for t in part[:3]]

    def stack_rows(step, low, across, order, *others):
        beside, across = swap(low, "tl"), after(order, across, *others)
        parts = (low, across, beside, swap(across, "tl"))
        return tuple(as_rows(v) for v in call(step, stack_kernel, [], batch, pieces(parts), spread_outs))

    attn_own = after(102, attn_own, down_pair)
    attn_pair = tuple(part.reshape(hi, depth + ROW_PAD, -1) for part in (attn_own, swap_x(attn_own)))
    qkv_w = tuple(part[:, :depth].reshape(hi * depth, -1) for part in attn_pair)
    out_w = (out_own, swap_x(after(138, out_own, attn_pair[1])))
    gain_one = tuple(part[:, depth, :depth].reshape(1, half).astype(F32) for part in attn_pair)
    gain_two = tuple(part[:, depth, depth : 2 * depth].reshape(1, half).astype(F32) for part in attn_pair)

    *seq_one, x_own, x_oth = call(
        2,
        functools.partial(norm_in_kernel, hi),
        [at],
        batch,
        pieces(token_parts) + gain_in(gain_one),
        spread_outs + [((own_rows, half), BF16, row_spec(rows, half))] * 2,
    )
    seq_one = tuple(as_rows(v) for v in seq_one)
    gate_near = after(105, after(104, gate_own, out_w[1]), seq_one[0])
    gate_w = (gate_own, swap_x(gate_near))
    up_w = (up_own, swap_x(after(106, up_own, gate_w[1])))

    qkv = project(3, seq_one, qkv_w, F32)
    qkv = after(144, after(107, qkv, out_w[1]), cot_parts[1])
    pair_spec, q_spec = quad_spec(rows, PAIR), quad_spec(rows, q_cols)
    lse_spec = pl.BlockSpec((1, 2 * pairs, length), lambda i, *_: (i, 0, 0))
    query_rot, kv_rot, mixed, lse = call(
        4,
        functools.partial(attend_kernel, pairs),
        [span],
        batch,
        [(qkv.reshape(quad + (all_cols,)), quad_spec(rows, all_cols)), *tables],
        [
            (quad + (q_cols,), BF16, q_spec),
            (quad + (PAIR,), BF16, pair_spec),
            (quad + (q_cols,), BF16, q_spec),
            ((batch, 2 * pairs, length), F32, lse_spec),
        ],
        [
            pltpu.VMEM((length, length), F32),
            pltpu.VMEM((2, length, PAIR), BF16),
            pltpu.VMEM((2, PAIR, length), BF16),
        ],
    )
    mixed = as_rows(mixed)
    attn_oth = scatter_rows(6, *project_back(5, mixed, out_w[1]))
    attn_own = scatter_rows(8, *project_back(7, after(108, mixed, attn_oth[3]), out_w[0]))
    h_own, h_oth, normed_two = call(
        9,
        residual_kernel,
        [],
        batch,
        half_ins(after(109, x_own, gate_own), x_oth) + terms(attn_own, attn_oth) + gain_in(gain_two),
        half_outs + low_out,
    )
    (seq_cot,) = call(
        1,
        functools.partial(pairs_kernel, hi),
        [at],
        batch,
        pieces((after(103, cot_own, normed_two), *cot_parts[1:])),
        [(quad + (width,), BF16, quad_spec(rows, width))],
    )
    seq_cot = as_rows(seq_cot)
    seq_two = stack_rows(10, normed_two, swap(normed_two, "th"), 111, gate_w[1], seq_cot)
    gate_pre = project(38, seq_two, gate_w, F32)
    inner, for_gate, for_up = call(
        11, expand_kernel, [], steps, tiles(*seq_two) + wholes(*up_w) + tiles(gate_pre), [hidden_out] * 3
    )

    def reduce_z(total):
        return lax.psum_scatter(total, "fh", scatter_dimension=0, tiled=True)

    down_part = weight_grad(12, seq_cot, inner)
    grad_down = reduce_z(down_part)
    gate_g, up_g = call(
        13,
        inner_back_kernel,
        [],
        steps,
        tiles(after(112, seq_cot, down_part)) + wholes(down_w) + tiles(for_gate, for_up),
        [hidden_out] * 2,
    )

    def expand_back(step, which, gate_g):
        outs = two_part_outs(all_rows, half, tile)
        ins = tiles(gate_g, up_g) + wholes(gate_w[which], up_w[which])
        return call(step, expand_back_kernel, [], steps, ins, outs)

    gate_sent = weight_grad(16, seq_two[1], gate_g)
    gate_came = swap_x(gate_sent)
    oth_parts = expand_back(14, 1, after(113, gate_g, gate_sent))
    normed_oth = scatter_rows(15, *oth_parts)
    own_parts = expand_back(17, 0, after(116, after(115, gate_g, oth_parts[0]), normed_oth[3]))
    normed_own = scatter_rows(18, *own_parts)
    up_sent = weight_grad(19, seq_two[1], after(117, up_g, normed_own[3]))
    gate_came = after(158, after(147, gate_came, up_sent), oth_parts[0], own_parts[0])
    gate_came = after(149, after(148, gate_came, normed_oth[2]), normed_own[2])
    up_came = swap_x(after(122, up_sent, gate_came))
    gate_total = weight_grad(23, seq_two[0], gate_g, gate_came)
    grad_gate = reduce_z(gate_total)
    r_own, r_oth, attn_low, gain_s_own, gain_s_oth = call(
        20,
        functools.partial(middle_kernel, hi),
        [at],
        batch,
        half_ins(after(120, after(118, h_own, up_sent), gate_total), h_oth)
        + terms(normed_own, normed_oth)
        + gain_in(gain_two)
        + [(cot_own, row_spec(rows, width))],
        half_outs + low_out + sum_outs * 2,
    )
    block_parts = project_back(21, after(150, after(119, inner, attn_low), gate_total), down_w)

    attn_far = swap(attn_low, "th")
    up_came = after(127, after(126, up_came, block_parts[0]), grad_down)
    up_total = weight_grad(28, seq_two[0], up_g, up_came)
    grad_up = reduce_z(up_total)
    seq_attn = stack_rows(24, attn_low, attn_far, 123, up_total)
    block_terms = scatter_rows(22, block_parts[0], after(124, block_parts[1], seq_attn[0]), 160, attn_far)
    grad_mixed = project(25, seq_attn, out_w, BF16)
    out_sent = weight_grad(26, after(125, seq_attn[1], grad_mixed), mixed)
    out_came = swap_x(after(128, out_sent, up_came))
    grad_mixed = after(156, after(139, grad_mixed, out_sent), block_terms[3])
    (qkv_g,) = call(
        27,
        functools.partial(attend_back_kernel, pairs),
        [span],
        batch,
        [
            (query_rot, q_spec),
            (kv_rot, pair_spec),
            (grad_mixed.reshape(quad + (q_cols,)), q_spec),
            (mixed.reshape(quad + (q_cols,)), q_spec),
            (lse, lse_spec),
            *tables,
        ],
        [(quad + (all_cols,), BF16, quad_spec(rows, all_cols))],
        [
            pltpu.VMEM((length, length), F32),
            pltpu.VMEM((length, PAIR), BF16),
            pltpu.VMEM((2, PAIR, length), BF16),
            pltpu.VMEM((length, PAIR), BF16),
            pltpu.VMEM((2, length, PAIR), F32),
            pltpu.VMEM((2, length, PAIR), F32),
        ],
    )
    qkv_g = after(141, after(140, after(129, as_rows(qkv_g), out_came), block_terms[2]), grad_gate)

    def project_gain(step, which, grad):
        outs = two_part_outs(all_rows, half, tile) + sum_outs
        kept, sent, sums = call(
            step, project_gain_kernel, [], steps, tiles(grad) + wholes(qkv_w[which]) + tiles(seq_one[which]), outs
        )
        return (kept, sent), sums / gain_one[which]

    qkv_sent = weight_grad(31, seq_one[1], after(159, qkv_g, out_sent))
    qkv_came = swap_x(after(134, qkv_sent, out_came))
    out_total = weight_grad(34, seq_attn[0], mixed, after(155, after(132, out_came, qkv_sent), qkv_g))
    grad_out = reduce_z(out_total)
    oth_parts, oth_gain = project_gain(29, 1, after(131, qkv_g, out_total))
    first_oth = scatter_rows(30, *oth_parts)
    own_parts, own_gain = project_gain(32, 0, after(143, after(142, qkv_g, first_oth[3]), out_total))
    first_own = scatter_rows(33, *own_parts)
    qkv_near = weight_grad(35, seq_one[0], after(133, qkv_g, first_own[3]), kind=F32)

    def gain_pair(one, two):
        return jnp.concatenate([one.reshape(hi, depth), two.reshape(hi, depth)], axis=1)

    gain_own, gain_oth = gain_pair(own_gain, gain_s_own), gain_pair(oth_gain, gain_s_oth)
    gain_both = jnp.stack([gain_own, gain_oth])
    gain_both = gain_both + swap(gain_both, "tl")
    gain_rows = gain_both[0] + swap_x(gain_both[1])
    gain_rows = jnp.pad(gain_rows[:, None], ((0, 0), (0, ROW_PAD - 1), (0, all_cols - 2 * depth))).astype(BF16)
    (qkv_total,) = call(
        39,
        total_kernel,
        [],
        hi,
        tiles_of(depth, qkv_near, after(152, after(151, after(135, qkv_came, grad_up), first_oth[2]), first_own[2]))
        + tiles_of(ROW_PAD, gain_rows.reshape(hi * ROW_PAD, all_cols)),
        [((hi * (depth + ROW_PAD), all_cols), BF16, row_spec(depth + ROW_PAD, all_cols))],
    )
    grad_qkv = reduce_z(qkv_total).astype(F32)
    gain_sums = grad_qkv[depth, : 2 * depth]
    gain_sums = gain_sums + swap(gain_sums, "th")
    grad_qkv = grad_qkv[:depth]
    (block_out,) = call(
        36,
        functools.partial(block_out_kernel, hi),
        [at],
        batch,
        half_ins(after(137, after(136, h_own, qkv_total), grad_up), h_oth) + terms(block_terms),
        whole_out,
    )

    (grad_in,) = call(
        37,
        functools.partial(grad_in_kernel, hi),
        [at],
        batch,
        half_ins(x_own, x_oth) + terms(first_own, first_oth) + gain_in(gain_one) + half_ins(r_own, r_oth),
        whole_out,
    )
    grad_down = grad_down[:depth].astype(F32) + swap_x(grad_down[depth:]).astype(F32)
    return (
        block_out.reshape(block_in.shape),
        grad_in.reshape(block_in.shape),
        grad_qkv[:, :q_cols],
        grad_qkv[:, q_cols : q_cols + kv_cols],
        grad_qkv[:, q_cols + kv_cols :],
        grad_out.astype(F32).T,
        grad_gate.astype(F32),
        grad_up.astype(F32),
        grad_down.T,
        gain_sums[:depth],
        gain_sums[depth:],
    )


def solution(mesh):
    n_fsdp, n_tp = mesh.shape["fsdp"], mesh.shape["tp"]
    fine = Mesh(mesh.devices.reshape(n_fsdp // 2, 2, n_tp // 2, 2), ("fh", "fl", "th", "tl"))
    fsdp, tp = ("fh", "fl"), ("th", "tl")
    rows = P(None, fsdp + tp, None)
    up, across, flat = P(fsdp, tp), P(tp, fsdp), P(fsdp)
    return jax.shard_map(
        per_device,
        mesh=fine,
        in_specs=(rows, P(None, fsdp), up, up, up, across, up, up, across, flat, flat, rows),
        out_specs=(rows, rows, up, up, up, across, up, up, across, flat, flat),
        check_vma=False,
    )
```

```python
import functools
import math

import jax
import jax.numpy as jnp
from jax import lax
from jax.experimental import pallas as pl
from jax.experimental.pallas import tpu as pltpu
from jax.sharding import Mesh, PartitionSpec as P

HD = 64
PAIR = 2 * HD
SPAN = 256
EPS = 1e-05
MASKED = -1e30
F32 = jnp.float32
BF16 = jnp.bfloat16
SWAP = [(0, 1), (1, 0)]
COST = {1: 1702, 2: 2220, 3: 2582, 4: 5630, 5: 1730, 6: 798, 7: 1730, 8: 798, 9: 1498, 10: 1626, 11: 4596, 12: 3950, 13: 4338, 14: 3898, 15: 798, 16: 2348, 17: 3872, 18: 798, 19: 2348, 20: 1986, 21: 3820, 22: 1006, 23: 2556, 24: 1626, 25: 2142, 26: 8118, 27: 127702, 28: 10228, 38: 3898}
SKIP = {161, 103, 136, 137, 107, 139, 140, 142, 116, 150, 120, 122, 158, 159}
ROW_PAD = 16


def dot(a, b):
    return jnp.dot(a, b, preferred_element_type=F32)


def dot_lt(a, b):
    return lax.dot_general(a, b, (((0,), (0,)), ((), ())), preferred_element_type=F32)


def dot_rt(a, b):
    return lax.dot_general(a, b, (((1,), (1,)), ((), ())), preferred_element_type=F32)


def swap(value, axis):
    return lax.ppermute(value, axis, SWAP)


def after(step, value, *others):
    if step in SKIP:
        return value
    return lax.optimization_barrier((value, *others))[0]


def full_spec(shape):
    return pl.BlockSpec(shape, lambda i, *_: (0,) * len(shape))


def row_spec(rows, cols, offset=0):
    return pl.BlockSpec((rows, cols), lambda i, *_: (i + offset, 0))


def quad_spec(rows, cols):
    return pl.BlockSpec((4, 1, rows, cols), lambda i, *_: (0, i, 0, 0))


def two_part_outs(rows, cols, tile):
    half = rows // tile // 2
    first = pl.BlockSpec((tile, cols), lambda i, *_: (jnp.minimum(i, half - 1), 0))
    second = pl.BlockSpec((tile, cols), lambda i, *_: (jnp.maximum(i - half, 0), 0))
    return [((rows // 2, cols), BF16, first), ((rows // 2, cols), BF16, second)]


def whole_spec(array):
    return pl.BlockSpec(array.shape, lambda i, *_: (0, 0), pipeline_mode=pl.Buffered(1))


def call(step, kernel, scalars, grid, ins, outs, scratch=()):
    work = COST.get(step, 0) * 1000
    return pl.pallas_call(
        kernel,
        out_shape=[jax.ShapeDtypeStruct(shape, kind) for shape, kind, _ in outs],
        grid_spec=pltpu.PrefetchScalarGridSpec(
            num_scalar_prefetch=len(scalars),
            grid=(grid,),
            in_specs=[spec for _, spec in ins],
            out_specs=[spec for _, _, spec in outs],
            scratch_shapes=list(scratch),
        ),
        cost_estimate=pl.CostEstimate(flops=work * 300, bytes_accessed=work + step, transcendentals=0),
        compiler_params=pltpu.CompilerParams(vmem_limit_bytes=56 << 20),
    )(*scalars, *[a for a, _ in ins])


def halves_of(value, hi, x):
    width = value.shape[-1] // (2 * hi)
    parts = [value[:, k * width : (k + 1) * width] for k in range(2 * hi)]
    even, odd = parts[0::2], parts[1::2]
    own = [jnp.where(x == 0, a, b) for a, b in zip(even, odd)]
    oth = [jnp.where(x == 0, b, a) for a, b in zip(even, odd)]
    return own, oth


def put_cols(ref, index, parts):
    width = parts[0].shape[-1]
    for k, part in enumerate(parts):
        ref[(*index, slice(None), slice(k * width, (k + 1) * width))] = part.astype(ref.dtype)


def join_to(ref, own, oth, hi, x):
    width = own.shape[-1] // hi
    for k in range(hi):
        a, b = own[:, k * width : (k + 1) * width], oth[:, k * width : (k + 1) * width]
        ref[:, 2 * k * width : (2 * k + 1) * width] = jnp.where(x == 0, a, b)
        ref[:, (2 * k + 1) * width : (2 * k + 2) * width] = jnp.where(x == 0, b, a)


def norm_in_kernel(hi, at, p0, p1, p2, p3, gain_own, gain_oth, n_own, n_oth, x_own, x_oth):
    x = at[0]
    half = n_own.shape[-1]
    for k, piece in enumerate((p0, p1, p2, p3)):
        low = piece[...]
        value = low.astype(F32)
        scale = lax.rsqrt(jnp.mean(value * value, axis=-1, keepdims=True) + EPS)
        own, oth = halves_of(value, hi, x)
        width = half // hi
        for part, gain, ref in ((own, gain_own, n_own), (oth, gain_oth, n_oth)):
            put_cols(
                ref, (k, 0), [v * scale * gain[:, z * width : (z + 1) * width] for z, v in enumerate(part)]
            )
        if k == 0:
            put_cols(x_own, (), own)
            put_cols(x_oth, (), oth)


def spread_kernel(hi, at, p0, p1, p2, p3, o_own, o_oth):
    x = at[0]
    for k, piece in enumerate((p0, p1, p2, p3)):
        own, oth = halves_of(piece[...], hi, x)
        put_cols(o_own, (k, 0), own)
        put_cols(o_oth, (k, 0), oth)


def pairs_kernel(hi, at, p0, p1, p2, p3, out):
    x = at[0]
    for k, piece in enumerate((p0, p1, p2, p3)):
        own, oth = halves_of(piece[...], hi, x)
        put_cols(out, (k, 0), [part for pair in zip(own, oth) for part in pair])


def stack_kernel(p0, p1, p2, p3, o_own, o_oth):
    half = o_own.shape[-1]
    for k, piece in enumerate((p0, p1, p2, p3)):
        o_own[k, 0] = piece[:, :half]
        o_oth[k, 0] = piece[:, half:]


def rows_scale(own, oth):
    total = jnp.sum(own * own, axis=-1, keepdims=True) + jnp.sum(oth * oth, axis=-1, keepdims=True)
    return lax.rsqrt(total / (own.shape[-1] + oth.shape[-1]) + EPS)


def summed(refs):
    return refs[0][...].astype(F32) + refs[1][...].astype(F32) + refs[2][...].astype(F32)


def residual_kernel(x_own, x_oth, a0, a1, a2, b0, b1, b2, gain_own, gain_oth, h_own, h_oth, n_out):
    own = x_own[...].astype(F32) + summed((a0, a1, a2))
    oth = x_oth[...].astype(F32) + summed((b0, b1, b2))
    scale = rows_scale(own, oth)
    half = own.shape[-1]
    h_own[...] = own
    h_oth[...] = oth
    n_out[:, :half] = (own * scale * gain_own[...]).astype(BF16)
    n_out[:, half:] = (oth * scale * gain_oth[...]).astype(BF16)


def block_out_kernel(hi, at, h_own, h_oth, t0, t1, t2, out):
    x = at[0]
    width = h_own.shape[-1] // hi
    for k in range(hi):
        cols = [slice(j * width, (j + 1) * width) for j in (2 * k, 2 * k + 1)]
        own, oth = (sum(t[:, col].astype(F32) for t in (t0, t1, t2)) for col in cols)
        own += h_own[:, k * width : (k + 1) * width]
        oth += h_oth[:, k * width : (k + 1) * width]
        out[:, cols[0]] = jnp.where(x == 0, own, oth)
        out[:, cols[1]] = jnp.where(x == 0, oth, own)


def back_of(own, oth, scale, gain_own, gain_oth, up_own, up_oth):
    w_own, w_oth = up_own * gain_own, up_oth * gain_oth
    total = jnp.sum(w_own * own, axis=-1, keepdims=True) + jnp.sum(w_oth * oth, axis=-1, keepdims=True)
    cube = scale * scale * scale * (total / (own.shape[-1] + oth.shape[-1]))
    return scale * w_own - own * cube, scale * w_oth - oth * cube


def middle_kernel(
    hi, at, h_own, h_oth, a0, a1, a2, b0, b1, b2, gain_own, gain_oth, upstream, r_own, r_oth, low_out, s_own, s_oth
):
    own, oth = h_own[...], h_oth[...]
    up_own, up_oth = summed((a0, a1, a2)), summed((b0, b1, b2))
    scale = rows_scale(own, oth)
    back_own, back_oth = back_of(own, oth, scale, gain_own[...], gain_oth[...], up_own, up_oth)
    u_own, u_oth = (jnp.concatenate(part, axis=1) for part in halves_of(upstream[...].astype(F32), hi, at[0]))
    back_own = u_own + back_own
    back_oth = u_oth + back_oth
    half = own.shape[-1]
    r_own[...] = back_own
    r_oth[...] = back_oth
    low_out[:, :half] = back_own.astype(BF16)
    low_out[:, half:] = back_oth.astype(BF16)

    @pl.when(pl.program_id(0) == 0)
    def _():
        s_own[...] = jnp.zeros_like(s_own)
        s_oth[...] = jnp.zeros_like(s_oth)

    s_own[...] += jnp.sum(up_own * own * scale, axis=0, keepdims=True)
    s_oth[...] += jnp.sum(up_oth * oth * scale, axis=0, keepdims=True)


def grad_in_kernel(hi, at, x_own, x_oth, a0, a1, a2, b0, b1, b2, gain_own, gain_oth, r_own, r_oth, out):
    own, oth = x_own[...].astype(F32), x_oth[...].astype(F32)
    scale = rows_scale(own, oth)
    back_own, back_oth = back_of(
        own, oth, scale, gain_own[...], gain_oth[...], summed((a0, a1, a2)), summed((b0, b1, b2))
    )
    join_to(out, r_own[...] + back_own, r_oth[...] + back_oth, hi, at[0])


def project_kernel(n_own, n_oth, w_own, w_oth, out):
    out[...] = (dot(n_own[...], w_own[...]) + dot(n_oth[...], w_oth[...])).astype(out.dtype)


def put_rows(kept, sent, value):
    stay = pl.program_id(0) < pl.num_programs(0) // 2

    @pl.when(stay)
    def _():
        kept[...] = value

    @pl.when(jnp.logical_not(stay))
    def _():
        sent[...] = value


def project_back_kernel(rows, weight, kept, sent):
    put_rows(kept, sent, dot_rt(rows[...], weight[...]).astype(BF16))


def project_gain_kernel(grad, weight, normed, kept, sent, sums):
    part = dot_rt(grad[...], weight[...])
    put_rows(kept, sent, part.astype(BF16))

    @pl.when(pl.program_id(0) == 0)
    def _():
        sums[...] = jnp.zeros_like(sums)

    sums[...] += jnp.sum(part * normed[...].astype(F32), axis=0, keepdims=True)


def weight_grad_kernel(rows, grad, out):
    out[...] = dot_lt(rows[...], grad[...]).astype(out.dtype)


def weight_grad_add_kernel(rows, grad, came, out):
    out[...] = (dot_lt(rows[...], grad[...]) + came[...].astype(F32)).astype(BF16)


def add_kernel(first, second, out):
    out[...] = (first[...].astype(F32) + second[...].astype(F32)).astype(BF16)


def total_kernel(near, came, gains, out):
    depth = near.shape[0]
    out[:depth] = (near[...] + came[...].astype(F32)).astype(BF16)
    out[depth:] = gains[...]


def expand_kernel(n_own, n_oth, u_own, u_oth, gate_in, inner, for_gate, for_up):
    gate = gate_in[...]
    up = dot(n_own[...], u_own[...]) + dot(n_oth[...], u_oth[...])
    sigmoid = jax.nn.sigmoid(gate)
    active = gate * sigmoid
    inner[...] = (active * up).astype(BF16)
    for_gate[...] = (up * sigmoid * (1.0 + gate * (1.0 - sigmoid))).astype(BF16)
    for_up[...] = active.astype(BF16)


def inner_back_kernel(grad, weight, for_gate, for_up, gate_g, up_g):
    inner_g = dot(grad[...], weight[...])
    gate_g[...] = (inner_g * for_gate[...].astype(F32)).astype(BF16)
    up_g[...] = (inner_g * for_up[...].astype(F32)).astype(BF16)


def expand_back_kernel(gate_g, up_g, gate_w, up_w, kept, sent):
    put_rows(kept, sent, (dot_rt(gate_g[...], gate_w[...]) + dot_rt(up_g[...], up_w[...])).astype(BF16))


def partner(value):
    lane = lax.broadcasted_iota(jnp.int32, value.shape, 1)
    return jnp.where(lane % HD < HD // 2, pltpu.roll(value, PAIR - HD // 2, 1), pltpu.roll(value, HD // 2, 1))


def low_lanes(shape):
    return lax.broadcasted_iota(jnp.int32, shape, 1) < HD


def set_bias(bias, key_at, query_at, first):
    keys, queries = key_at[...], query_at[...]
    key_in = ((keys >= first) & (keys < first + SPAN)).astype(jnp.int32)
    query_in = ((queries >= first) & (queries < first + SPAN)).astype(jnp.int32)
    seen = (keys <= queries).astype(jnp.int32) + key_in * query_in
    bias[...] = jnp.where(seen > 0, 0.0, MASKED)


def attend_kernel(pairs, span, qkv, cos, sine, key_at, query_at, q_out, kv_out, o_out, lse_out, bias, key_s, val_s):
    length = cos.shape[0]
    set_bias(bias, key_at, query_at, span[pl.program_id(0)])
    kv = qkv[:, 0, :, pairs * PAIR :].reshape(length, PAIR)
    low = low_lanes(kv.shape)
    turned = kv * cos[...] + partner(kv) * sine[...]
    kv = jnp.where(low, turned, kv).astype(BF16)
    kv_out[:, 0] = kv.reshape(4, length // 4, PAIR)
    wide = kv.astype(F32)
    key_even = jnp.where(low, wide, 0.0)
    val_odd = jnp.where(low, 0.0, wide)
    key_s[0] = key_even.astype(BF16)
    key_s[1] = pltpu.roll(key_even, HD, 1).astype(BF16)
    val_s[0] = pltpu.roll(val_odd, HD, 1).T.astype(BF16)
    val_s[1] = val_odd.T.astype(BF16)

    def pair_step(j, _):
        cols = pl.ds(pl.multiple_of(j * PAIR, PAIR), PAIR)
        raw = qkv[:, 0, :, cols].reshape(length, PAIR)
        query = (raw * cos[...] + partner(raw) * sine[...]).astype(BF16)
        q_out[:, 0, :, cols] = query.reshape(4, length // 4, PAIR)
        query_t = (query.astype(F32) * HD**-0.5).T.astype(BF16)
        mixed = jnp.zeros((PAIR, length), F32)
        for k in range(2):
            scores = dot(key_s[k], query_t) + bias[...]
            top = jnp.max(scores, axis=0, keepdims=True)
            raised = jnp.exp(scores - top)
            total = jnp.sum(raised, axis=0, keepdims=True)
            lse_out[0, pl.ds(2 * j + k, 1), :] = top + jnp.log(total)
            mixed += dot(val_s[k], (raised * (1.0 / total)).astype(BF16))
        o_out[:, 0, :, cols] = mixed.T.astype(BF16).reshape(4, length // 4, PAIR)
        return 0

    lax.fori_loop(0, pairs, pair_step, 0)


def with_terms(rows, number):
    high = number.astype(BF16).astype(F32)
    middle = (number - high).astype(BF16).astype(F32)
    low = number - high - middle
    line = lax.broadcasted_iota(jnp.int32, (16, number.shape[1]), 0)
    terms = jnp.where(line == 0, high, jnp.where(line == 1, middle, jnp.where(line == 2, low, 0.0)))
    rest = jnp.zeros((HD - 16, number.shape[1]), BF16)
    return jnp.concatenate([rows.astype(BF16), terms.astype(BF16), rest], axis=0)


def attend_back_kernel(
    pairs, span, query_in, kv_in, grad_in, mixed_in, lse, cos, sine, key_at, query_at, out, bias, key_s, key_t, val_s, key_g, val_g
):
    length = cos.shape[0]
    scale = HD**-0.5
    set_bias(bias, key_at, query_at, span[pl.program_id(0)])
    kv = kv_in[:, 0].reshape(length, PAIR).astype(F32)
    low = low_lanes(kv.shape)
    lane = lax.broadcasted_iota(jnp.int32, kv.shape, 1)
    ones = jnp.where(lane < HD + 3, 1.0, 0.0)
    key_even = jnp.where(low, kv, 0.0)
    key_s[...] = jnp.where(low, kv, ones).astype(BF16)
    val_s[...] = jnp.where(low, pltpu.roll(kv, HD, 1) * scale, ones).astype(BF16)
    key_t[0] = key_even.T.astype(BF16)
    key_t[1] = pltpu.roll(key_even, HD, 1).T.astype(BF16)
    key_g[...] = jnp.zeros_like(key_g)
    val_g[...] = jnp.zeros_like(val_g)

    def pair_step(j, _):
        cols = pl.ds(pl.multiple_of(j * PAIR, PAIR), PAIR)
        query = query_in[:, 0, :, cols].reshape(length, PAIR)
        grad = grad_in[:, 0, :, cols].reshape(length, PAIR)
        mixed = mixed_in[:, 0, :, cols].reshape(length, PAIR)
        query_t = (query.astype(F32) * scale).T
        grad_t = grad.astype(F32).T
        product = grad_t * mixed.astype(F32).T
        query_g = jnp.zeros((PAIR, length), F32)
        for k in range(2):
            part = slice(k * HD, (k + 1) * HD)
            delta = jnp.sum(product[part], axis=0, keepdims=True) * scale
            scores = dot(key_s[...], with_terms(query_t[part], -lse[0, pl.ds(2 * j + k, 1), :]))
            weight = jnp.exp(scores + bias[...])
            weight_g = dot(val_s[...], with_terms(grad_t[part], -delta))
            val_g[k] += dot(weight.astype(BF16), grad)
            score_g = (weight * weight_g).astype(BF16)
            key_g[k] += dot(score_g, query)
            query_g += dot(key_t[k], score_g)
        value = query_g.T
        value = value * cos[...] - partner(value) * sine[...]
        out[:, 0, :, cols] = value.astype(BF16).reshape(4, length // 4, PAIR)
        return 0

    lax.fori_loop(0, pairs, pair_step, 0)
    keys = key_g[0] + pltpu.roll(key_g[1], HD, 1)
    vals = val_g[1] + pltpu.roll(val_g[0], HD, 1)
    keys = keys * cos[...] - partner(keys) * sine[...]
    out[:, 0, :, pairs * PAIR :] = jnp.where(low, keys, vals).astype(BF16).reshape(4, length // 4, PAIR)


def per_device(
    block_in, span_start, w_query, w_key, w_value, w_out, w_gate, w_up, w_down, gain_attn, gain_mlp, cotangent
):
    z, x, y, c = (lax.axis_index(name) for name in ("fh", "fl", "th", "tl"))
    hi = lax.axis_size("fh")
    batch, rows, width = block_in.shape
    own_rows, half = batch * rows, width // 2
    length = rows * 4
    depth = w_query.shape[0]
    q_cols, kv_cols = w_query.shape[1], w_key.shape[1]
    pairs = q_cols // PAIR
    at = jnp.stack([x]).astype(jnp.int32)

    shard = jnp.concatenate([w_query, w_key, w_value], axis=1)
    gains = jnp.concatenate([gain_attn, gain_mlp])[None]
    gains = jnp.pad(gains, ((0, ROW_PAD - 1), (0, shard.shape[1] - gains.shape[1])))
    shard = jnp.concatenate([shard, gains], axis=0)

    def gather(part):
        return lax.all_gather(part, "fh", axis=0, tiled=True)

    def swap_x(value):
        return swap(value, "fl")

    down_shard = w_down.T
    down_pair = jnp.concatenate([down_shard, swap_x(down_shard)], axis=0)
    attn_own, out_own, gate_own, up_own = gather(shard), gather(w_out.T), gather(w_gate), gather(w_up)
    down_w = gather(down_pair)

    def gather_rows(piece):
        beside = swap(piece, "tl")
        across = swap(piece, "th")
        return piece, across, beside, swap(across, "tl")

    token_parts = gather_rows(block_in.reshape(own_rows, width))
    cot_own = cotangent.reshape(own_rows, width)
    cot_parts = gather_rows(after(101, cot_own, token_parts[1]))

    place = jnp.concatenate(
        [(((y + dy) % 2) * 2 + (c + dc) % 2) * rows + jnp.arange(rows, dtype=jnp.int32) for dc in (0, 1) for dy in (0, 1)]
    )
    frequency = jnp.exp(jnp.arange(HD // 2, dtype=F32) * (-2.0 * math.log(10000.0) / HD))
    angles = place.astype(F32)[:, None] * frequency[None, :]
    cos = jnp.tile(jnp.cos(angles), (1, 4))
    sine = jnp.sin(angles)
    sine = jnp.concatenate([-sine, sine, -sine, sine], axis=1)
    key_at, query_at = place[:, None], place[None, :]
    span = span_start[:, 0]
    tables = [(t, full_spec(t.shape)) for t in (cos, sine, key_at, query_at)]

    quad = (4, batch, rows)
    all_rows = 4 * own_rows
    tile = 256
    steps = all_rows // tile
    hidden = w_gate.shape[1]
    all_cols = q_cols + 2 * kv_cols
    tiles = lambda *values: [(v, row_spec(tile, v.shape[1])) for v in values]
    wholes = lambda *values: [(v, whole_spec(v)) for v in values]
    pieces = lambda parts: [(p, row_spec(rows, width)) for p in parts]
    half_ins = lambda *values: [(v, row_spec(rows, half)) for v in values]
    gain_in = lambda gain: [(g, full_spec((1, half))) for g in gain]
    spread_outs = [(quad + (half,), BF16, quad_spec(rows, half))] * 2
    half_outs = [((own_rows, half), F32, row_spec(rows, half))] * 2
    low_out = [((own_rows, width), BF16, row_spec(rows, width))]
    whole_out = [((own_rows, width), F32, row_spec(rows, width))]
    sum_outs = [((1, half), F32, full_spec((1, half)))]
    hidden_out = ((all_rows, hidden), BF16, row_spec(tile, hidden))

    def tiles_of(size, *values):
        return [(v, row_spec(size, v.shape[1])) for v in values]

    def as_rows(value):
        return value.reshape(all_rows, value.shape[-1])

    def project(step, pair, weights, kind):
        cols = weights[0].shape[1]
        out = ((all_rows, cols), kind, row_spec(tile, cols))
        return call(step, project_kernel, [], steps, tiles(*pair) + wholes(*weights), [out])[0]

    def project_back(step, value, weight):
        outs = two_part_outs(all_rows, weight.shape[0], tile)
        return call(step, project_back_kernel, [], steps, tiles(value) + wholes(weight), outs)

    def weight_grad(step, value, grad, came=None, kind=BF16):
        part, cols = 256, grad.shape[1]
        ins = [(value, pl.BlockSpec((value.shape[0], part), lambda i: (0, i)))] + wholes(grad)
        ins += [] if came is None else [(came, row_spec(part, cols))]
        out = ((value.shape[1], cols), kind, row_spec(part, cols))
        kernel = weight_grad_kernel if came is None else weight_grad_add_kernel
        return call(step, kernel, [], value.shape[1] // part, ins, [out])[0]

    def scatter_rows(step, kept, sent, order=None, *others):
        cols = kept.shape[1]
        came = swap(sent, "tl")
        (passed,) = call(
            step,
            add_kernel,
            [],
            batch,
            [(kept, row_spec(rows, cols, batch)), (came, row_spec(rows, cols, batch))],
            [((own_rows, cols), BF16, row_spec(rows, cols))],
        )
        across = after(order, passed, *others) if others else passed
        return kept, came, swap(across, "th"), passed

    def terms(*scattered):
        return [(t, row_spec(rows, t.shape[1])) for part in scattered for t in part[:3]]

    def stack_rows(step, low, across, order, *others):
        beside, across = swap(low, "tl"), after(order, across, *others)
        parts = (low, across, beside, swap(across, "tl"))
        return tuple(as_rows(v) for v in call(step, stack_kernel, [], batch, pieces(parts), spread_outs))

    attn_own = after(102, attn_own, down_pair)
    attn_pair = tuple(part.reshape(hi, depth + ROW_PAD, -1) for part in (attn_own, swap_x(attn_own)))
    qkv_w = tuple(part[:, :depth].reshape(hi * depth, -1) for part in attn_pair)
    out_w = (out_own, swap_x(after(138, out_own, attn_pair[1])))
    gain_one = tuple(part[:, depth, :depth].reshape(1, half).astype(F32) for part in attn_pair)
    gain_two = tuple(part[:, depth, depth : 2 * depth].reshape(1, half).astype(F32) for part in attn_pair)

    *seq_one, x_own, x_oth = call(
        2,
        functools.partial(norm_in_kernel, hi),
        [at],
        batch,
        pieces(token_parts) + gain_in(gain_one),
        spread_outs + [((own_rows, half), BF16, row_spec(rows, half))] * 2,
    )
    seq_one = tuple(as_rows(v) for v in seq_one)
    gate_near = after(105, after(104, gate_own, out_w[1]), seq_one[0])
    gate_w = (gate_own, swap_x(gate_near))
    up_w = (up_own, swap_x(after(106, up_own, gate_w[1])))

    qkv = project(3, seq_one, qkv_w, F32)
    qkv = after(144, after(107, qkv, out_w[1]), cot_parts[1])
    pair_spec, q_spec = quad_spec(rows, PAIR), quad_spec(rows, q_cols)
    lse_spec = pl.BlockSpec((1, 2 * pairs, length), lambda i, *_: (i, 0, 0))
    query_rot, kv_rot, mixed, lse = call(
        4,
        functools.partial(attend_kernel, pairs),
        [span],
        batch,
        [(qkv.reshape(quad + (all_cols,)), quad_spec(rows, all_cols)), *tables],
        [
            (quad + (q_cols,), BF16, q_spec),
            (quad + (PAIR,), BF16, pair_spec),
            (quad + (q_cols,), BF16, q_spec),
            ((batch, 2 * pairs, length), F32, lse_spec),
        ],
        [
            pltpu.VMEM((length, length), F32),
            pltpu.VMEM((2, length, PAIR), BF16),
            pltpu.VMEM((2, PAIR, length), BF16),
        ],
    )
    mixed = as_rows(mixed)
    attn_oth = scatter_rows(6, *project_back(5, mixed, out_w[1]))
    attn_own = scatter_rows(8, *project_back(7, after(108, mixed, attn_oth[3]), out_w[0]))
    h_own, h_oth, normed_two = call(
        9,
        residual_kernel,
        [],
        batch,
        half_ins(after(109, x_own, gate_own), x_oth) + terms(attn_own, attn_oth) + gain_in(gain_two),
        half_outs + low_out,
    )
    (seq_cot,) = call(
        1,
        functools.partial(pairs_kernel, hi),
        [at],
        batch,
        pieces((after(103, cot_own, normed_two), *cot_parts[1:])),
        [(quad + (width,), BF16, quad_spec(rows, width))],
    )
    seq_cot = as_rows(seq_cot)
    seq_two = stack_rows(10, normed_two, swap(normed_two, "th"), 111, gate_w[1], seq_cot)
    gate_pre = project(38, seq_two, gate_w, F32)
    inner, for_gate, for_up = call(
        11, expand_kernel, [], steps, tiles(*seq_two) + wholes(*up_w) + tiles(gate_pre), [hidden_out] * 3
    )

    def reduce_z(total):
        return lax.psum_scatter(total, "fh", scatter_dimension=0, tiled=True)

    down_part = weight_grad(12, seq_cot, inner)
    grad_down = reduce_z(down_part)
    gate_g, up_g = call(
        13,
        inner_back_kernel,
        [],
        steps,
        tiles(after(112, seq_cot, down_part)) + wholes(down_w) + tiles(for_gate, for_up),
        [hidden_out] * 2,
    )

    def expand_back(step, which, gate_g):
        outs = two_part_outs(all_rows, half, tile)
        ins = tiles(gate_g, up_g) + wholes(gate_w[which], up_w[which])
        return call(step, expand_back_kernel, [], steps, ins, outs)

    gate_sent = weight_grad(16, seq_two[1], gate_g)
    gate_came = swap_x(gate_sent)
    oth_parts = expand_back(14, 1, after(113, gate_g, gate_sent))
    normed_oth = scatter_rows(15, *oth_parts)
    own_parts = expand_back(17, 0, after(116, after(115, gate_g, oth_parts[0]), normed_oth[3]))
    normed_own = scatter_rows(18, *own_parts)
    up_sent = weight_grad(19, seq_two[1], after(117, up_g, normed_own[3]))
    gate_came = after(158, after(147, gate_came, up_sent), oth_parts[0], own_parts[0])
    gate_came = after(149, after(148, gate_came, normed_oth[2]), normed_own[2])
    up_came = swap_x(after(122, up_sent, gate_came))
    gate_total = weight_grad(23, seq_two[0], gate_g, gate_came)
    grad_gate = reduce_z(gate_total)
    r_own, r_oth, attn_low, gain_s_own, gain_s_oth = call(
        20,
        functools.partial(middle_kernel, hi),
        [at],
        batch,
        half_ins(after(120, after(118, h_own, up_sent), gate_total), h_oth)
        + terms(normed_own, normed_oth)
        + gain_in(gain_two)
        + [(cot_own, row_spec(rows, width))],
        half_outs + low_out + sum_outs * 2,
    )
    block_parts = project_back(21, after(150, after(119, inner, attn_low), gate_total), down_w)

    attn_far = swap(attn_low, "th")
    up_came = after(127, after(126, up_came, block_parts[0]), grad_down)
    up_total = weight_grad(28, seq_two[0], up_g, up_came)
    grad_up = reduce_z(up_total)
    seq_attn = stack_rows(24, attn_low, attn_far, 123, up_total)
    block_terms = scatter_rows(22, block_parts[0], after(124, block_parts[1], seq_attn[0]), 160, attn_far)
    grad_mixed = project(25, seq_attn, out_w, BF16)
    out_sent = weight_grad(26, after(125, seq_attn[1], grad_mixed), mixed)
    out_came = swap_x(after(128, out_sent, up_came))
    grad_mixed = after(156, after(139, grad_mixed, out_sent), block_terms[3])
    (qkv_g,) = call(
        27,
        functools.partial(attend_back_kernel, pairs),
        [span],
        batch,
        [
            (query_rot, q_spec),
            (kv_rot, pair_spec),
            (grad_mixed.reshape(quad + (q_cols,)), q_spec),
            (mixed.reshape(quad + (q_cols,)), q_spec),
            (lse, lse_spec),
            *tables,
        ],
        [(quad + (all_cols,), BF16, quad_spec(rows, all_cols))],
        [
            pltpu.VMEM((length, length), F32),
            pltpu.VMEM((length, PAIR), BF16),
            pltpu.VMEM((2, PAIR, length), BF16),
            pltpu.VMEM((length, PAIR), BF16),
            pltpu.VMEM((2, length, PAIR), F32),
            pltpu.VMEM((2, length, PAIR), F32),
        ],
    )
    qkv_g = after(141, after(140, after(129, as_rows(qkv_g), out_came), block_terms[2]), grad_gate)

    def project_gain(step, which, grad):
        outs = two_part_outs(all_rows, half, tile) + sum_outs
        kept, sent, sums = call(
            step, project_gain_kernel, [], steps, tiles(grad) + wholes(qkv_w[which]) + tiles(seq_one[which]), outs
        )
        return (kept, sent), sums / gain_one[which]

    oth_parts, oth_gain = project_gain(29, 1, qkv_g)
    first_oth = scatter_rows(30, *oth_parts)
    qkv_sent = weight_grad(31, seq_one[1], after(167, after(161, after(130, qkv_g, oth_parts[0]), first_oth[3]), block_terms[2]))
    qkv_came = swap_x(after(134, qkv_sent, out_came))
    out_total = weight_grad(34, seq_attn[0], mixed, after(132, out_came, qkv_sent))
    grad_out = reduce_z(out_total)
    own_parts, own_gain = project_gain(32, 0, after(131, qkv_g, out_total))
    qkv_near = weight_grad(35, seq_one[0], after(133, qkv_g, own_parts[0]), kind=F32)

    def gain_pair(one, two):
        return jnp.concatenate([one.reshape(hi, depth), two.reshape(hi, depth)], axis=1)

    gain_own, gain_oth = gain_pair(own_gain, gain_s_own), gain_pair(oth_gain, gain_s_oth)
    gain_both = jnp.stack([gain_own, gain_oth])
    gain_both = gain_both + swap(gain_both, "tl")
    gain_rows = gain_both[0] + swap_x(gain_both[1])
    gain_rows = jnp.pad(gain_rows[:, None], ((0, 0), (0, ROW_PAD - 1), (0, all_cols - 2 * depth))).astype(BF16)
    (qkv_total,) = call(
        39,
        total_kernel,
        [],
        hi,
        tiles_of(depth, qkv_near, after(152, after(151, after(135, qkv_came, grad_up), first_oth[2]), qkv_near))
        + tiles_of(ROW_PAD, gain_rows.reshape(hi * ROW_PAD, all_cols)),
        [((hi * (depth + ROW_PAD), all_cols), BF16, row_spec(depth + ROW_PAD, all_cols))],
    )
    first_own = scatter_rows(33, own_parts[0], after(166, own_parts[1], qkv_total))
    grad_qkv = reduce_z(qkv_total).astype(F32)
    gain_sums = grad_qkv[depth, : 2 * depth]
    gain_sums = gain_sums + swap(gain_sums, "th")
    grad_qkv = grad_qkv[:depth]
    (block_out,) = call(
        36,
        functools.partial(block_out_kernel, hi),
        [at],
        batch,
        half_ins(after(137, after(136, h_own, qkv_total), grad_up), h_oth) + terms(block_terms),
        whole_out,
    )

    (grad_in,) = call(
        37,
        functools.partial(grad_in_kernel, hi),
        [at],
        batch,
        half_ins(x_own, x_oth) + terms(first_own, first_oth) + gain_in(gain_one) + half_ins(r_own, r_oth),
        whole_out,
    )
    grad_down = grad_down[:depth].astype(F32) + swap_x(grad_down[depth:]).astype(F32)
    return (
        block_out.reshape(block_in.shape),
        grad_in.reshape(block_in.shape),
        grad_qkv[:, :q_cols],
        grad_qkv[:, q_cols : q_cols + kv_cols],
        grad_qkv[:, q_cols + kv_cols :],
        grad_out.astype(F32).T,
        grad_gate.astype(F32),
        grad_up.astype(F32),
        grad_down.T,
        gain_sums[:depth],
        gain_sums[depth:],
    )


def solution(mesh):
    n_fsdp, n_tp = mesh.shape["fsdp"], mesh.shape["tp"]
    fine = Mesh(mesh.devices.reshape(n_fsdp // 2, 2, n_tp // 2, 2), ("fh", "fl", "th", "tl"))
    fsdp, tp = ("fh", "fl"), ("th", "tl")
    rows = P(None, fsdp + tp, None)
    up, across, flat = P(fsdp, tp), P(tp, fsdp), P(fsdp)
    return jax.shard_map(
        per_device,
        mesh=fine,
        in_specs=(rows, P(None, fsdp), up, up, up, across, up, up, across, flat, flat, rows),
        out_specs=(rows, rows, up, up, up, across, up, up, across, flat, flat),
        check_vma=False,
    )
```

```python
import functools
import math

import jax
import jax.numpy as jnp
from jax import lax
from jax.experimental import pallas as pl
from jax.experimental.pallas import tpu as pltpu
from jax.sharding import Mesh, PartitionSpec as P

HD = 64
PAIR = 2 * HD
SPAN = 256
EPS = 1e-05
MASKED = -1e30
F32 = jnp.float32
BF16 = jnp.bfloat16
SWAP = [(0, 1), (1, 0)]
COST = {1: 1702, 2: 2220, 3: 2582, 4: 5630, 5: 1730, 6: 798, 7: 1730, 8: 798, 9: 1498, 10: 1626, 11: 4596, 12: 3950, 13: 4338, 14: 3898, 15: 798, 16: 2348, 17: 3872, 18: 798, 19: 2348, 20: 1986, 21: 3820, 22: 1006, 23: 2556, 24: 1626, 25: 2142, 26: 8118, 27: 127702, 28: 10228, 38: 3898}
SKIP = {136, 137, 139, 140, 142, 150, 158, 159, 161, 103, 170, 107, 174, 116, 120, 122}
ROW_PAD = 16


def dot(a, b):
    return jnp.dot(a, b, preferred_element_type=F32)


def dot_lt(a, b):
    return lax.dot_general(a, b, (((0,), (0,)), ((), ())), preferred_element_type=F32)


def dot_rt(a, b):
    return lax.dot_general(a, b, (((1,), (1,)), ((), ())), preferred_element_type=F32)


def swap(value, axis):
    return lax.ppermute(value, axis, SWAP)


def after(step, value, *others):
    if step in SKIP:
        return value
    return lax.optimization_barrier((value, *others))[0]


def full_spec(shape):
    return pl.BlockSpec(shape, lambda i, *_: (0,) * len(shape))


def row_spec(rows, cols, offset=0):
    return pl.BlockSpec((rows, cols), lambda i, *_: (i + offset, 0))


def quad_spec(rows, cols):
    return pl.BlockSpec((4, 1, rows, cols), lambda i, *_: (0, i, 0, 0))


def two_part_outs(rows, cols, tile):
    half = rows // tile // 2
    first = pl.BlockSpec((tile, cols), lambda i, *_: (jnp.minimum(i, half - 1), 0))
    second = pl.BlockSpec((tile, cols), lambda i, *_: (jnp.maximum(i - half, 0), 0))
    return [((rows // 2, cols), BF16, first), ((rows // 2, cols), BF16, second)]


def whole_spec(array):
    return pl.BlockSpec(array.shape, lambda i, *_: (0, 0), pipeline_mode=pl.Buffered(1))


def call(step, kernel, scalars, grid, ins, outs, scratch=()):
    work = COST.get(step, 0) * 1000
    return pl.pallas_call(
        kernel,
        out_shape=[jax.ShapeDtypeStruct(shape, kind) for shape, kind, _ in outs],
        grid_spec=pltpu.PrefetchScalarGridSpec(
            num_scalar_prefetch=len(scalars),
            grid=(grid,),
            in_specs=[spec for _, spec in ins],
            out_specs=[spec for _, _, spec in outs],
            scratch_shapes=list(scratch),
        ),
        cost_estimate=pl.CostEstimate(flops=work * 300, bytes_accessed=work + step, transcendentals=0),
        compiler_params=pltpu.CompilerParams(vmem_limit_bytes=56 << 20),
    )(*scalars, *[a for a, _ in ins])


def halves_of(value, hi, x):
    width = value.shape[-1] // (2 * hi)
    parts = [value[:, k * width : (k + 1) * width] for k in range(2 * hi)]
    even, odd = parts[0::2], parts[1::2]
    own = [jnp.where(x == 0, a, b) for a, b in zip(even, odd)]
    oth = [jnp.where(x == 0, b, a) for a, b in zip(even, odd)]
    return own, oth


def put_cols(ref, index, parts):
    width = parts[0].shape[-1]
    for k, part in enumerate(parts):
        ref[(*index, slice(None), slice(k * width, (k + 1) * width))] = part.astype(ref.dtype)


def join_to(ref, own, oth, hi, x):
    width = own.shape[-1] // hi
    for k in range(hi):
        a, b = own[:, k * width : (k + 1) * width], oth[:, k * width : (k + 1) * width]
        ref[:, 2 * k * width : (2 * k + 1) * width] = jnp.where(x == 0, a, b)
        ref[:, (2 * k + 1) * width : (2 * k + 2) * width] = jnp.where(x == 0, b, a)


def norm_in_kernel(hi, at, p0, p1, p2, p3, gain_own, gain_oth, n_own, n_oth, x_own, x_oth):
    x = at[0]
    half = n_own.shape[-1]
    for k, piece in enumerate((p0, p1, p2, p3)):
        low = piece[...]
        value = low.astype(F32)
        scale = lax.rsqrt(jnp.mean(value * value, axis=-1, keepdims=True) + EPS)
        own, oth = halves_of(value, hi, x)
        width = half // hi
        for part, gain, ref in ((own, gain_own, n_own), (oth, gain_oth, n_oth)):
            put_cols(
                ref, (k, 0), [v * scale * gain[:, z * width : (z + 1) * width] for z, v in enumerate(part)]
            )
        if k == 0:
            put_cols(x_own, (), own)
            put_cols(x_oth, (), oth)


def spread_kernel(hi, at, p0, p1, p2, p3, o_own, o_oth):
    x = at[0]
    for k, piece in enumerate((p0, p1, p2, p3)):
        own, oth = halves_of(piece[...], hi, x)
        put_cols(o_own, (k, 0), own)
        put_cols(o_oth, (k, 0), oth)


def pairs_kernel(hi, at, p0, p1, p2, p3, out):
    x = at[0]
    for k, piece in enumerate((p0, p1, p2, p3)):
        own, oth = halves_of(piece[...], hi, x)
        put_cols(out, (k, 0), [part for pair in zip(own, oth) for part in pair])


def stack_kernel(p0, p1, p2, p3, o_own, o_oth):
    half = o_own.shape[-1]
    for k, piece in enumerate((p0, p1, p2, p3)):
        o_own[k, 0] = piece[:, :half]
        o_oth[k, 0] = piece[:, half:]


def rows_scale(own, oth):
    total = jnp.sum(own * own, axis=-1, keepdims=True) + jnp.sum(oth * oth, axis=-1, keepdims=True)
    return lax.rsqrt(total / (own.shape[-1] + oth.shape[-1]) + EPS)


def summed(refs):
    return refs[0][...].astype(F32) + refs[1][...].astype(F32) + refs[2][...].astype(F32)


def residual_kernel(x_own, x_oth, a0, a1, a2, b0, b1, b2, gain_own, gain_oth, h_own, h_oth, n_out):
    own = x_own[...].astype(F32) + summed((a0, a1, a2))
    oth = x_oth[...].astype(F32) + summed((b0, b1, b2))
    scale = rows_scale(own, oth)
    half = own.shape[-1]
    h_own[...] = own
    h_oth[...] = oth
    n_out[:, :half] = (own * scale * gain_own[...]).astype(BF16)
    n_out[:, half:] = (oth * scale * gain_oth[...]).astype(BF16)


def block_out_kernel(hi, at, h_own, h_oth, t0, t1, t2, out):
    x = at[0]
    width = h_own.shape[-1] // hi
    for k in range(hi):
        cols = [slice(j * width, (j + 1) * width) for j in (2 * k, 2 * k + 1)]
        own, oth = (sum(t[:, col].astype(F32) for t in (t0, t1, t2)) for col in cols)
        own += h_own[:, k * width : (k + 1) * width]
        oth += h_oth[:, k * width : (k + 1) * width]
        out[:, cols[0]] = jnp.where(x == 0, own, oth)
        out[:, cols[1]] = jnp.where(x == 0, oth, own)


def back_of(own, oth, scale, gain_own, gain_oth, up_own, up_oth):
    w_own, w_oth = up_own * gain_own, up_oth * gain_oth
    total = jnp.sum(w_own * own, axis=-1, keepdims=True) + jnp.sum(w_oth * oth, axis=-1, keepdims=True)
    cube = scale * scale * scale * (total / (own.shape[-1] + oth.shape[-1]))
    return scale * w_own - own * cube, scale * w_oth - oth * cube


def middle_kernel(
    hi, at, h_own, h_oth, a0, a1, a2, b0, b1, b2, gain_own, gain_oth, upstream, r_own, r_oth, low_out, s_own, s_oth
):
    own, oth = h_own[...], h_oth[...]
    up_own, up_oth = summed((a0, a1, a2)), summed((b0, b1, b2))
    scale = rows_scale(own, oth)
    back_own, back_oth = back_of(own, oth, scale, gain_own[...], gain_oth[...], up_own, up_oth)
    u_own, u_oth = (jnp.concatenate(part, axis=1) for part in halves_of(upstream[...].astype(F32), hi, at[0]))
    back_own = u_own + back_own
    back_oth = u_oth + back_oth
    half = own.shape[-1]
    r_own[...] = back_own
    r_oth[...] = back_oth
    low_out[:, :half] = back_own.astype(BF16)
    low_out[:, half:] = back_oth.astype(BF16)

    @pl.when(pl.program_id(0) == 0)
    def _():
        s_own[...] = jnp.zeros_like(s_own)
        s_oth[...] = jnp.zeros_like(s_oth)

    s_own[...] += jnp.sum(up_own * own * scale, axis=0, keepdims=True)
    s_oth[...] += jnp.sum(up_oth * oth * scale, axis=0, keepdims=True)


def grad_in_kernel(hi, at, x_own, x_oth, a0, a1, a2, b0, b1, b2, gain_own, gain_oth, r_own, r_oth, out):
    own, oth = x_own[...].astype(F32), x_oth[...].astype(F32)
    scale = rows_scale(own, oth)
    back_own, back_oth = back_of(
        own, oth, scale, gain_own[...], gain_oth[...], summed((a0, a1, a2)), summed((b0, b1, b2))
    )
    join_to(out, r_own[...] + back_own, r_oth[...] + back_oth, hi, at[0])


def project_kernel(n_own, n_oth, w_own, w_oth, out):
    out[...] = (dot(n_own[...], w_own[...]) + dot(n_oth[...], w_oth[...])).astype(out.dtype)


def put_rows(kept, sent, value):
    stay = pl.program_id(0) < pl.num_programs(0) // 2

    @pl.when(stay)
    def _():
        kept[...] = value

    @pl.when(jnp.logical_not(stay))
    def _():
        sent[...] = value


def project_back_kernel(rows, weight, kept, sent):
    put_rows(kept, sent, dot_rt(rows[...], weight[...]).astype(BF16))


def project_gain_kernel(grad, weight, normed, kept, sent, sums):
    part = dot_rt(grad[...], weight[...])
    put_rows(kept, sent, part.astype(BF16))

    @pl.when(pl.program_id(0) == 0)
    def _():
        sums[...] = jnp.zeros_like(sums)

    sums[...] += jnp.sum(part * normed[...].astype(F32), axis=0, keepdims=True)


def weight_grad_kernel(rows, grad, out):
    out[...] = dot_lt(rows[...], grad[...]).astype(out.dtype)


def weight_grad_add_kernel(rows, grad, came, out):
    out[...] = (dot_lt(rows[...], grad[...]) + came[...].astype(F32)).astype(BF16)


def add_kernel(first, second, out):
    out[...] = (first[...].astype(F32) + second[...].astype(F32)).astype(BF16)


def total_kernel(near, came, gains, out):
    depth = near.shape[0]
    out[:depth] = (near[...] + came[...].astype(F32)).astype(BF16)
    out[depth:] = gains[...]


def expand_kernel(n_own, n_oth, u_own, u_oth, gate_in, inner, for_gate, for_up):
    gate = gate_in[...]
    up = dot(n_own[...], u_own[...]) + dot(n_oth[...], u_oth[...])
    sigmoid = jax.nn.sigmoid(gate)
    active = gate * sigmoid
    inner[...] = (active * up).astype(BF16)
    for_gate[...] = (up * sigmoid * (1.0 + gate * (1.0 - sigmoid))).astype(BF16)
    for_up[...] = active.astype(BF16)


def inner_back_kernel(grad, weight, for_gate, for_up, gate_g, up_g):
    inner_g = dot(grad[...], weight[...])
    gate_g[...] = (inner_g * for_gate[...].astype(F32)).astype(BF16)
    up_g[...] = (inner_g * for_up[...].astype(F32)).astype(BF16)


def expand_back_kernel(gate_g, up_g, gate_w, up_w, kept, sent):
    put_rows(kept, sent, (dot_rt(gate_g[...], gate_w[...]) + dot_rt(up_g[...], up_w[...])).astype(BF16))


def partner(value):
    lane = lax.broadcasted_iota(jnp.int32, value.shape, 1)
    return jnp.where(lane % HD < HD // 2, pltpu.roll(value, PAIR - HD // 2, 1), pltpu.roll(value, HD // 2, 1))


def low_lanes(shape):
    return lax.broadcasted_iota(jnp.int32, shape, 1) < HD


def set_bias(bias, key_at, query_at, first):
    keys, queries = key_at[...], query_at[...]
    key_in = ((keys >= first) & (keys < first + SPAN)).astype(jnp.int32)
    query_in = ((queries >= first) & (queries < first + SPAN)).astype(jnp.int32)
    seen = (keys <= queries).astype(jnp.int32) + key_in * query_in
    bias[...] = jnp.where(seen > 0, 0.0, MASKED)


def attend_kernel(pairs, span, qkv, cos, sine, key_at, query_at, q_out, kv_out, o_out, lse_out, bias, key_s, val_s):
    length = cos.shape[0]
    set_bias(bias, key_at, query_at, span[pl.program_id(0)])
    kv = qkv[:, 0, :, pairs * PAIR :].reshape(length, PAIR)
    low = low_lanes(kv.shape)
    turned = kv * cos[...] + partner(kv) * sine[...]
    kv = jnp.where(low, turned, kv).astype(BF16)
    kv_out[:, 0] = kv.reshape(4, length // 4, PAIR)
    wide = kv.astype(F32)
    key_even = jnp.where(low, wide, 0.0)
    val_odd = jnp.where(low, 0.0, wide)
    key_s[0] = key_even.astype(BF16)
    key_s[1] = pltpu.roll(key_even, HD, 1).astype(BF16)
    val_s[0] = pltpu.roll(val_odd, HD, 1).T.astype(BF16)
    val_s[1] = val_odd.T.astype(BF16)

    def pair_step(j, _):
        cols = pl.ds(pl.multiple_of(j * PAIR, PAIR), PAIR)
        raw = qkv[:, 0, :, cols].reshape(length, PAIR)
        query = (raw * cos[...] + partner(raw) * sine[...]).astype(BF16)
        q_out[:, 0, :, cols] = query.reshape(4, length // 4, PAIR)
        query_t = (query.astype(F32) * HD**-0.5).T.astype(BF16)
        mixed = jnp.zeros((PAIR, length), F32)
        for k in range(2):
            scores = dot(key_s[k], query_t) + bias[...]
            top = jnp.max(scores, axis=0, keepdims=True)
            raised = jnp.exp(scores - top)
            total = jnp.sum(raised, axis=0, keepdims=True)
            lse_out[0, pl.ds(2 * j + k, 1), :] = top + jnp.log(total)
            mixed += dot(val_s[k], (raised * (1.0 / total)).astype(BF16))
        o_out[:, 0, :, cols] = mixed.T.astype(BF16).reshape(4, length // 4, PAIR)
        return 0

    lax.fori_loop(0, pairs, pair_step, 0)


def with_terms(rows, number):
    high = number.astype(BF16).astype(F32)
    middle = (number - high).astype(BF16).astype(F32)
    low = number - high - middle
    line = lax.broadcasted_iota(jnp.int32, (16, number.shape[1]), 0)
    terms = jnp.where(line == 0, high, jnp.where(line == 1, middle, jnp.where(line == 2, low, 0.0)))
    rest = jnp.zeros((HD - 16, number.shape[1]), BF16)
    return jnp.concatenate([rows.astype(BF16), terms.astype(BF16), rest], axis=0)


def attend_back_kernel(
    pairs, span, query_in, kv_in, grad_in, mixed_in, lse, cos, sine, key_at, query_at, out, bias, key_s, key_t, val_s, key_g, val_g
):
    length = cos.shape[0]
    scale = HD**-0.5
    set_bias(bias, key_at, query_at, span[pl.program_id(0)])
    kv = kv_in[:, 0].reshape(length, PAIR).astype(F32)
    low = low_lanes(kv.shape)
    lane = lax.broadcasted_iota(jnp.int32, kv.shape, 1)
    ones = jnp.where(lane < HD + 3, 1.0, 0.0)
    key_even = jnp.where(low, kv, 0.0)
    key_s[...] = jnp.where(low, kv, ones).astype(BF16)
    val_s[...] = jnp.where(low, pltpu.roll(kv, HD, 1) * scale, ones).astype(BF16)
    key_t[0] = key_even.T.astype(BF16)
    key_t[1] = pltpu.roll(key_even, HD, 1).T.astype(BF16)
    key_g[...] = jnp.zeros_like(key_g)
    val_g[...] = jnp.zeros_like(val_g)

    def pair_step(j, _):
        cols = pl.ds(pl.multiple_of(j * PAIR, PAIR), PAIR)
        query = query_in[:, 0, :, cols].reshape(length, PAIR)
        grad = grad_in[:, 0, :, cols].reshape(length, PAIR)
        mixed = mixed_in[:, 0, :, cols].reshape(length, PAIR)
        query_t = (query.astype(F32) * scale).T
        grad_t = grad.astype(F32).T
        product = grad_t * mixed.astype(F32).T
        query_g = jnp.zeros((PAIR, length), F32)
        for k in range(2):
            part = slice(k * HD, (k + 1) * HD)
            delta = jnp.sum(product[part], axis=0, keepdims=True) * scale
            scores = dot(key_s[...], with_terms(query_t[part], -lse[0, pl.ds(2 * j + k, 1), :]))
            weight = jnp.exp(scores + bias[...])
            weight_g = dot(val_s[...], with_terms(grad_t[part], -delta))
            val_g[k] += dot(weight.astype(BF16), grad)
            score_g = (weight * weight_g).astype(BF16)
            key_g[k] += dot(score_g, query)
            query_g += dot(key_t[k], score_g)
        value = query_g.T
        value = value * cos[...] - partner(value) * sine[...]
        out[:, 0, :, cols] = value.astype(BF16).reshape(4, length // 4, PAIR)
        return 0

    lax.fori_loop(0, pairs, pair_step, 0)
    keys = key_g[0] + pltpu.roll(key_g[1], HD, 1)
    vals = val_g[1] + pltpu.roll(val_g[0], HD, 1)
    keys = keys * cos[...] - partner(keys) * sine[...]
    out[:, 0, :, pairs * PAIR :] = jnp.where(low, keys, vals).astype(BF16).reshape(4, length // 4, PAIR)


def per_device(
    block_in, span_start, w_query, w_key, w_value, w_out, w_gate, w_up, w_down, gain_attn, gain_mlp, cotangent
):
    z, x, y, c = (lax.axis_index(name) for name in ("fh", "fl", "th", "tl"))
    hi = lax.axis_size("fh")
    batch, rows, width = block_in.shape
    own_rows, half = batch * rows, width // 2
    length = rows * 4
    depth = w_query.shape[0]
    q_cols, kv_cols = w_query.shape[1], w_key.shape[1]
    pairs = q_cols // PAIR
    at = jnp.stack([x]).astype(jnp.int32)

    shard = jnp.concatenate([w_query, w_key, w_value], axis=1)
    gains = jnp.concatenate([gain_attn, gain_mlp])[None]
    gains = jnp.pad(gains, ((0, ROW_PAD - 1), (0, shard.shape[1] - gains.shape[1])))
    shard = jnp.concatenate([shard, gains], axis=0)

    def gather(part):
        return lax.all_gather(part, "fh", axis=0, tiled=True)

    def swap_x(value):
        return swap(value, "fl")

    down_shard = w_down.T
    down_pair = jnp.concatenate([down_shard, swap_x(down_shard)], axis=0)
    attn_own, out_own, gate_own, up_own = gather(shard), gather(w_out.T), gather(w_gate), gather(w_up)
    down_w = gather(down_pair)

    def gather_rows(piece):
        beside = swap(piece, "tl")
        across = swap(piece, "th")
        return piece, across, beside, swap(across, "tl")

    token_parts = gather_rows(block_in.reshape(own_rows, width))
    cot_own = cotangent.reshape(own_rows, width)
    cot_parts = gather_rows(after(101, cot_own, token_parts[1]))

    place = jnp.concatenate(
        [(((y + dy) % 2) * 2 + (c + dc) % 2) * rows + jnp.arange(rows, dtype=jnp.int32) for dc in (0, 1) for dy in (0, 1)]
    )
    frequency = jnp.exp(jnp.arange(HD // 2, dtype=F32) * (-2.0 * math.log(10000.0) / HD))
    angles = place.astype(F32)[:, None] * frequency[None, :]
    cos = jnp.tile(jnp.cos(angles), (1, 4))
    sine = jnp.sin(angles)
    sine = jnp.concatenate([-sine, sine, -sine, sine], axis=1)
    key_at, query_at = place[:, None], place[None, :]
    span = span_start[:, 0]
    tables = [(t, full_spec(t.shape)) for t in (cos, sine, key_at, query_at)]

    quad = (4, batch, rows)
    all_rows = 4 * own_rows
    tile = 256
    steps = all_rows // tile
    hidden = w_gate.shape[1]
    all_cols = q_cols + 2 * kv_cols
    tiles = lambda *values: [(v, row_spec(tile, v.shape[1])) for v in values]
    wholes = lambda *values: [(v, whole_spec(v)) for v in values]
    pieces = lambda parts: [(p, row_spec(rows, width)) for p in parts]
    half_ins = lambda *values: [(v, row_spec(rows, half)) for v in values]
    gain_in = lambda gain: [(g, full_spec((1, half))) for g in gain]
    spread_outs = [(quad + (half,), BF16, quad_spec(rows, half))] * 2
    half_outs = [((own_rows, half), F32, row_spec(rows, half))] * 2
    low_out = [((own_rows, width), BF16, row_spec(rows, width))]
    whole_out = [((own_rows, width), F32, row_spec(rows, width))]
    sum_outs = [((1, half), F32, full_spec((1, half)))]
    hidden_out = ((all_rows, hidden), BF16, row_spec(tile, hidden))

    def tiles_of(size, *values):
        return [(v, row_spec(size, v.shape[1])) for v in values]

    def as_rows(value):
        return value.reshape(all_rows, value.shape[-1])

    def project(step, pair, weights, kind):
        cols = weights[0].shape[1]
        out = ((all_rows, cols), kind, row_spec(tile, cols))
        return call(step, project_kernel, [], steps, tiles(*pair) + wholes(*weights), [out])[0]

    def project_back(step, value, weight):
        outs = two_part_outs(all_rows, weight.shape[0], tile)
        return call(step, project_back_kernel, [], steps, tiles(value) + wholes(weight), outs)

    def weight_grad(step, value, grad, came=None, kind=BF16):
        part, cols = 256, grad.shape[1]
        ins = [(value, pl.BlockSpec((value.shape[0], part), lambda i: (0, i)))] + wholes(grad)
        ins += [] if came is None else [(came, row_spec(part, cols))]
        out = ((value.shape[1], cols), kind, row_spec(part, cols))
        kernel = weight_grad_kernel if came is None else weight_grad_add_kernel
        return call(step, kernel, [], value.shape[1] // part, ins, [out])[0]

    def scatter_rows(step, kept, sent, order=None, *others):
        cols = kept.shape[1]
        came = swap(sent, "tl")
        (passed,) = call(
            step,
            add_kernel,
            [],
            batch,
            [(kept, row_spec(rows, cols, batch)), (came, row_spec(rows, cols, batch))],
            [((own_rows, cols), BF16, row_spec(rows, cols))],
        )
        across = after(order, passed, *others) if others else passed
        return kept, came, swap(across, "th"), passed

    def terms(*scattered):
        return [(t, row_spec(rows, t.shape[1])) for part in scattered for t in part[:3]]

    def stack_rows(step, low, across, order, *others):
        beside, across = swap(low, "tl"), after(order, across, *others)
        parts = (low, across, beside, swap(across, "tl"))
        return tuple(as_rows(v) for v in call(step, stack_kernel, [], batch, pieces(parts), spread_outs))

    attn_own = after(102, attn_own, down_pair)
    attn_pair = tuple(part.reshape(hi, depth + ROW_PAD, -1) for part in (attn_own, swap_x(attn_own)))
    qkv_w = tuple(part[:, :depth].reshape(hi * depth, -1) for part in attn_pair)
    out_w = (out_own, swap_x(after(138, out_own, attn_pair[1])))
    gain_one = tuple(part[:, depth, :depth].reshape(1, half).astype(F32) for part in attn_pair)
    gain_two = tuple(part[:, depth, depth : 2 * depth].reshape(1, half).astype(F32) for part in attn_pair)

    *seq_one, x_own, x_oth = call(
        2,
        functools.partial(norm_in_kernel, hi),
        [at],
        batch,
        pieces(token_parts) + gain_in(gain_one),
        spread_outs + [((own_rows, half), BF16, row_spec(rows, half))] * 2,
    )
    seq_one = tuple(as_rows(v) for v in seq_one)
    gate_near = after(105, after(104, gate_own, out_w[1]), seq_one[0])
    gate_w = (gate_own, swap_x(gate_near))
    up_w = (up_own, swap_x(after(106, up_own, gate_w[1])))

    qkv = project(3, seq_one, qkv_w, F32)
    qkv = after(144, after(107, qkv, out_w[1]), cot_parts[1])
    pair_spec, q_spec = quad_spec(rows, PAIR), quad_spec(rows, q_cols)
    lse_spec = pl.BlockSpec((1, 2 * pairs, length), lambda i, *_: (i, 0, 0))
    query_rot, kv_rot, mixed, lse = call(
        4,
        functools.partial(attend_kernel, pairs),
        [span],
        batch,
        [(qkv.reshape(quad + (all_cols,)), quad_spec(rows, all_cols)), *tables],
        [
            (quad + (q_cols,), BF16, q_spec),
            (quad + (PAIR,), BF16, pair_spec),
            (quad + (q_cols,), BF16, q_spec),
            ((batch, 2 * pairs, length), F32, lse_spec),
        ],
        [
            pltpu.VMEM((length, length), F32),
            pltpu.VMEM((2, length, PAIR), BF16),
            pltpu.VMEM((2, PAIR, length), BF16),
        ],
    )
    mixed = as_rows(mixed)
    attn_oth = scatter_rows(6, *project_back(5, mixed, out_w[1]))
    attn_own = scatter_rows(8, *project_back(7, after(108, mixed, attn_oth[3]), out_w[0]))
    h_own, h_oth, normed_two = call(
        9,
        residual_kernel,
        [],
        batch,
        half_ins(after(109, x_own, gate_own), x_oth) + terms(attn_own, attn_oth) + gain_in(gain_two),
        half_outs + low_out,
    )
    (seq_cot,) = call(
        1,
        functools.partial(pairs_kernel, hi),
        [at],
        batch,
        pieces((after(103, cot_own, normed_two), *cot_parts[1:])),
        [(quad + (width,), BF16, quad_spec(rows, width))],
    )
    seq_cot = as_rows(seq_cot)
    seq_two = stack_rows(10, normed_two, swap(normed_two, "th"), 111, gate_w[1], seq_cot)
    gate_pre = project(38, seq_two, gate_w, F32)
    inner, for_gate, for_up = call(
        11, expand_kernel, [], steps, tiles(*seq_two) + wholes(*up_w) + tiles(gate_pre), [hidden_out] * 3
    )

    def reduce_z(total):
        return lax.psum_scatter(total, "fh", scatter_dimension=0, tiled=True)

    down_part = weight_grad(12, seq_cot, inner)
    grad_down = reduce_z(down_part)
    gate_g, up_g = call(
        13,
        inner_back_kernel,
        [],
        steps,
        tiles(after(112, seq_cot, down_part)) + wholes(down_w) + tiles(for_gate, for_up),
        [hidden_out] * 2,
    )

    def expand_back(step, which, gate_g):
        outs = two_part_outs(all_rows, half, tile)
        ins = tiles(gate_g, up_g) + wholes(gate_w[which], up_w[which])
        return call(step, expand_back_kernel, [], steps, ins, outs)

    gate_sent = weight_grad(16, seq_two[1], gate_g)
    gate_came = swap_x(gate_sent)
    oth_parts = expand_back(14, 1, after(113, gate_g, gate_sent))
    normed_oth = scatter_rows(15, *oth_parts)
    own_parts = expand_back(17, 0, after(116, after(115, gate_g, oth_parts[0]), normed_oth[3]))
    normed_own = scatter_rows(18, *own_parts)
    up_sent = weight_grad(19, seq_two[1], after(117, up_g, normed_own[3]))
    gate_came = after(158, after(147, gate_came, up_sent), oth_parts[0], own_parts[0])
    gate_came = after(149, after(148, gate_came, normed_oth[2]), normed_own[2])
    up_came = swap_x(after(122, up_sent, gate_came))
    gate_total = weight_grad(23, seq_two[0], gate_g, gate_came)
    grad_gate = reduce_z(gate_total)
    r_own, r_oth, attn_low, gain_s_own, gain_s_oth = call(
        20,
        functools.partial(middle_kernel, hi),
        [at],
        batch,
        half_ins(after(120, after(118, h_own, up_sent), gate_total), h_oth)
        + terms(normed_own, normed_oth)
        + gain_in(gain_two)
        + [(cot_own, row_spec(rows, width))],
        half_outs + low_out + sum_outs * 2,
    )
    block_parts = project_back(21, after(150, after(119, inner, attn_low), gate_total), down_w)

    attn_far = swap(attn_low, "th")
    up_came = after(127, after(126, up_came, block_parts[0]), grad_down)
    up_total = weight_grad(28, seq_two[0], up_g, up_came)
    grad_up = reduce_z(up_total)
    seq_attn = stack_rows(24, attn_low, attn_far, 123, up_total)
    block_terms = scatter_rows(22, block_parts[0], after(124, block_parts[1], seq_attn[0]), 160, attn_far)
    grad_mixed = project(25, seq_attn, out_w, BF16)
    out_sent = weight_grad(26, after(125, seq_attn[1], grad_mixed), mixed)
    out_came = swap_x(after(128, out_sent, up_came))
    grad_mixed = after(156, after(139, grad_mixed, out_sent), block_terms[3])
    (qkv_g,) = call(
        27,
        functools.partial(attend_back_kernel, pairs),
        [span],
        batch,
        [
            (query_rot, q_spec),
            (kv_rot, pair_spec),
            (grad_mixed.reshape(quad + (q_cols,)), q_spec),
            (mixed.reshape(quad + (q_cols,)), q_spec),
            (lse, lse_spec),
            *tables,
        ],
        [(quad + (all_cols,), BF16, quad_spec(rows, all_cols))],
        [
            pltpu.VMEM((length, length), F32),
            pltpu.VMEM((length, PAIR), BF16),
            pltpu.VMEM((2, PAIR, length), BF16),
            pltpu.VMEM((length, PAIR), BF16),
            pltpu.VMEM((2, length, PAIR), F32),
            pltpu.VMEM((2, length, PAIR), F32),
        ],
    )
    qkv_g = after(141, after(140, after(129, as_rows(qkv_g), out_came), block_terms[2]), grad_gate)

    def project_gain(step, which, grad):
        outs = two_part_outs(all_rows, half, tile) + sum_outs
        kept, sent, sums = call(
            step, project_gain_kernel, [], steps, tiles(grad) + wholes(qkv_w[which]) + tiles(seq_one[which]), outs
        )
        return (kept, sent), sums / gain_one[which]

    oth_parts, oth_gain = project_gain(29, 1, qkv_g)
    first_oth = scatter_rows(30, *oth_parts)
    qkv_sent = weight_grad(31, seq_one[1], after(167, after(161, after(130, qkv_g, oth_parts[0]), first_oth[3]), block_terms[2]))
    qkv_came = swap_x(after(134, qkv_sent, out_came))
    out_total = weight_grad(34, seq_attn[0], mixed, after(174, after(132, out_came, qkv_sent), first_oth[3]))
    grad_out = reduce_z(out_total)
    own_parts, own_gain = project_gain(32, 0, after(173, after(131, qkv_g, out_total), first_oth[3]))
    first_own = scatter_rows(33, *own_parts)
    qkv_near = weight_grad(35, seq_one[0], after(133, qkv_g, own_parts[0]), kind=F32)

    def gain_pair(one, two):
        return jnp.concatenate([one.reshape(hi, depth), two.reshape(hi, depth)], axis=1)

    gain_own, gain_oth = gain_pair(own_gain, gain_s_own), gain_pair(oth_gain, gain_s_oth)
    gain_both = jnp.stack([gain_own, gain_oth])
    gain_both = gain_both + swap(gain_both, "tl")
    gain_rows = gain_both[0] + swap_x(gain_both[1])
    gain_rows = jnp.pad(gain_rows[:, None], ((0, 0), (0, ROW_PAD - 1), (0, all_cols - 2 * depth))).astype(BF16)
    (qkv_total,) = call(
        39,
        total_kernel,
        [],
        hi,
        tiles_of(depth, qkv_near, after(170, after(152, after(151, after(135, qkv_came, grad_up), first_oth[2]), qkv_near), first_own[3]))
        + tiles_of(ROW_PAD, gain_rows.reshape(hi * ROW_PAD, all_cols)),
        [((hi * (depth + ROW_PAD), all_cols), BF16, row_spec(depth + ROW_PAD, all_cols))],
    )
    grad_qkv = reduce_z(qkv_total).astype(F32)
    gain_sums = grad_qkv[depth, : 2 * depth]
    gain_sums = gain_sums + swap(gain_sums, "th")
    grad_qkv = grad_qkv[:depth]
    (block_out,) = call(
        36,
        functools.partial(block_out_kernel, hi),
        [at],
        batch,
        half_ins(after(137, after(136, h_own, qkv_total), grad_up), h_oth) + terms(block_terms),
        whole_out,
    )

    (grad_in,) = call(
        37,
        functools.partial(grad_in_kernel, hi),
        [at],
        batch,
        half_ins(x_own, x_oth) + terms(first_own, first_oth) + gain_in(gain_one) + half_ins(r_own, r_oth),
        whole_out,
    )
    down_came = swap_x(grad_down[depth:])
    if 171 not in SKIP:
        down_came, block_out, grad_in = lax.optimization_barrier((down_came, block_out, grad_in))
    elif 172 not in SKIP:
        down_came, block_out = lax.optimization_barrier((down_came, block_out))
    grad_down = grad_down[:depth].astype(F32) + down_came.astype(F32)
    return (
        block_out.reshape(block_in.shape),
        grad_in.reshape(block_in.shape),
        grad_qkv[:, :q_cols],
        grad_qkv[:, q_cols : q_cols + kv_cols],
        grad_qkv[:, q_cols + kv_cols :],
        grad_out.astype(F32).T,
        grad_gate.astype(F32),
        grad_up.astype(F32),
        grad_down.T,
        gain_sums[:depth],
        gain_sums[depth:],
    )


def solution(mesh):
    n_fsdp, n_tp = mesh.shape["fsdp"], mesh.shape["tp"]
    fine = Mesh(mesh.devices.reshape(n_fsdp // 2, 2, n_tp // 2, 2), ("fh", "fl", "th", "tl"))
    fsdp, tp = ("fh", "fl"), ("th", "tl")
    rows = P(None, fsdp + tp, None)
    up, across, flat = P(fsdp, tp), P(tp, fsdp), P(fsdp)
    return jax.shard_map(
        per_device,
        mesh=fine,
        in_specs=(rows, P(None, fsdp), up, up, up, across, up, up, across, flat, flat, rows),
        out_specs=(rows, rows, up, up, up, across, up, up, across, flat, flat),
        check_vma=False,
    )
```

```python
import functools
import math

import jax
import jax.numpy as jnp
from jax import lax
from jax.experimental import pallas as pl
from jax.experimental.pallas import tpu as pltpu
from jax.sharding import Mesh, PartitionSpec as P

HD = 64
PAIR = 2 * HD
SPAN = 256
EPS = 1e-05
MASKED = -1e30
F32 = jnp.float32
BF16 = jnp.bfloat16
SWAP = [(0, 1), (1, 0)]
COST = {1: 1702, 2: 2220, 3: 2582, 4: 5630, 5: 1730, 6: 798, 7: 1730, 8: 798, 9: 1498, 10: 1626, 11: 4596, 12: 3950, 13: 4338, 14: 3898, 15: 798, 16: 2348, 17: 3872, 18: 798, 19: 2348, 20: 1986, 21: 3820, 22: 1006, 23: 2556, 24: 1626, 25: 2142, 26: 8118, 27: 127702, 28: 10228, 38: 3898}
SKIP = {136, 137, 139, 140, 142, 150, 158, 159, 161, 103, 170, 107, 174, 116, 120, 122}
ROW_PAD = 16


def dot(a, b):
    return jnp.dot(a, b, preferred_element_type=F32)


def dot_lt(a, b):
    return lax.dot_general(a, b, (((0,), (0,)), ((), ())), preferred_element_type=F32)


def dot_rt(a, b):
    return lax.dot_general(a, b, (((1,), (1,)), ((), ())), preferred_element_type=F32)


def swap(value, axis):
    return lax.ppermute(value, axis, SWAP)


def after(step, value, *others):
    if step in SKIP:
        return value
    return lax.optimization_barrier((value, *others))[0]


def full_spec(shape):
    return pl.BlockSpec(shape, lambda i, *_: (0,) * len(shape))


def row_spec(rows, cols, offset=0):
    return pl.BlockSpec((rows, cols), lambda i, *_: (i + offset, 0))


def quad_spec(rows, cols):
    return pl.BlockSpec((4, 1, rows, cols), lambda i, *_: (0, i, 0, 0))


def two_part_outs(rows, cols, tile):
    half = rows // tile // 2
    first = pl.BlockSpec((tile, cols), lambda i, *_: (jnp.minimum(i, half - 1), 0))
    second = pl.BlockSpec((tile, cols), lambda i, *_: (jnp.maximum(i - half, 0), 0))
    return [((rows // 2, cols), BF16, first), ((rows // 2, cols), BF16, second)]


def whole_spec(array):
    return pl.BlockSpec(array.shape, lambda i, *_: (0, 0), pipeline_mode=pl.Buffered(1))


def call(step, kernel, scalars, grid, ins, outs, scratch=()):
    work = COST.get(step, 0) * 1000
    return pl.pallas_call(
        kernel,
        out_shape=[jax.ShapeDtypeStruct(shape, kind) for shape, kind, _ in outs],
        grid_spec=pltpu.PrefetchScalarGridSpec(
            num_scalar_prefetch=len(scalars),
            grid=(grid,),
            in_specs=[spec for _, spec in ins],
            out_specs=[spec for _, _, spec in outs],
            scratch_shapes=list(scratch),
        ),
        cost_estimate=pl.CostEstimate(flops=work * 300, bytes_accessed=work + step, transcendentals=0),
        compiler_params=pltpu.CompilerParams(vmem_limit_bytes=30 << 20),
    )(*scalars, *[a for a, _ in ins])


def halves_of(value, hi, x):
    width = value.shape[-1] // (2 * hi)
    parts = [value[:, k * width : (k + 1) * width] for k in range(2 * hi)]
    even, odd = parts[0::2], parts[1::2]
    own = [jnp.where(x == 0, a, b) for a, b in zip(even, odd)]
    oth = [jnp.where(x == 0, b, a) for a, b in zip(even, odd)]
    return own, oth


def put_cols(ref, index, parts):
    width = parts[0].shape[-1]
    for k, part in enumerate(parts):
        ref[(*index, slice(None), slice(k * width, (k + 1) * width))] = part.astype(ref.dtype)


def join_to(ref, own, oth, hi, x):
    width = own.shape[-1] // hi
    for k in range(hi):
        a, b = own[:, k * width : (k + 1) * width], oth[:, k * width : (k + 1) * width]
        ref[:, 2 * k * width : (2 * k + 1) * width] = jnp.where(x == 0, a, b)
        ref[:, (2 * k + 1) * width : (2 * k + 2) * width] = jnp.where(x == 0, b, a)


def norm_in_kernel(hi, at, p0, p1, p2, p3, gain_own, gain_oth, n_own, n_oth, x_own, x_oth):
    x = at[0]
    half = n_own.shape[-1]
    for k, piece in enumerate((p0, p1, p2, p3)):
        low = piece[...]
        value = low.astype(F32)
        scale = lax.rsqrt(jnp.mean(value * value, axis=-1, keepdims=True) + EPS)
        own, oth = halves_of(value, hi, x)
        width = half // hi
        for part, gain, ref in ((own, gain_own, n_own), (oth, gain_oth, n_oth)):
            put_cols(
                ref, (k, 0), [v * scale * gain[:, z * width : (z + 1) * width] for z, v in enumerate(part)]
            )
        if k == 0:
            put_cols(x_own, (), own)
            put_cols(x_oth, (), oth)


def spread_kernel(hi, at, p0, p1, p2, p3, o_own, o_oth):
    x = at[0]
    for k, piece in enumerate((p0, p1, p2, p3)):
        own, oth = halves_of(piece[...], hi, x)
        put_cols(o_own, (k, 0), own)
        put_cols(o_oth, (k, 0), oth)


def pairs_kernel(hi, at, p0, p1, p2, p3, out):
    x = at[0]
    for k, piece in enumerate((p0, p1, p2, p3)):
        own, oth = halves_of(piece[...], hi, x)
        put_cols(out, (k, 0), [part for pair in zip(own, oth) for part in pair])


def stack_kernel(p0, p1, p2, p3, o_own, o_oth):
    half = o_own.shape[-1]
    for k, piece in enumerate((p0, p1, p2, p3)):
        o_own[k, 0] = piece[:, :half]
        o_oth[k, 0] = piece[:, half:]


def rows_scale(own, oth):
    total = jnp.sum(own * own, axis=-1, keepdims=True) + jnp.sum(oth * oth, axis=-1, keepdims=True)
    return lax.rsqrt(total / (own.shape[-1] + oth.shape[-1]) + EPS)


def summed(refs):
    return refs[0][...].astype(F32) + refs[1][...].astype(F32) + refs[2][...].astype(F32)


def residual_kernel(x_own, x_oth, a0, a1, a2, b0, b1, b2, gain_own, gain_oth, h_own, h_oth, n_out):
    own = x_own[...].astype(F32) + summed((a0, a1, a2))
    oth = x_oth[...].astype(F32) + summed((b0, b1, b2))
    scale = rows_scale(own, oth)
    half = own.shape[-1]
    h_own[...] = own
    h_oth[...] = oth
    n_out[:, :half] = (own * scale * gain_own[...]).astype(BF16)
    n_out[:, half:] = (oth * scale * gain_oth[...]).astype(BF16)


def block_out_kernel(hi, at, h_own, h_oth, t0, t1, t2, out):
    x = at[0]
    width = h_own.shape[-1] // hi
    for k in range(hi):
        cols = [slice(j * width, (j + 1) * width) for j in (2 * k, 2 * k + 1)]
        own, oth = (sum(t[:, col].astype(F32) for t in (t0, t1, t2)) for col in cols)
        own += h_own[:, k * width : (k + 1) * width]
        oth += h_oth[:, k * width : (k + 1) * width]
        out[:, cols[0]] = jnp.where(x == 0, own, oth)
        out[:, cols[1]] = jnp.where(x == 0, oth, own)


def back_of(own, oth, scale, gain_own, gain_oth, up_own, up_oth):
    w_own, w_oth = up_own * gain_own, up_oth * gain_oth
    total = jnp.sum(w_own * own, axis=-1, keepdims=True) + jnp.sum(w_oth * oth, axis=-1, keepdims=True)
    cube = scale * scale * scale * (total / (own.shape[-1] + oth.shape[-1]))
    return scale * w_own - own * cube, scale * w_oth - oth * cube


def middle_kernel(
    hi, at, h_own, h_oth, a0, a1, a2, b0, b1, b2, gain_own, gain_oth, upstream, r_own, r_oth, low_out, s_own, s_oth
):
    own, oth = h_own[...], h_oth[...]
    up_own, up_oth = summed((a0, a1, a2)), summed((b0, b1, b2))
    scale = rows_scale(own, oth)
    back_own, back_oth = back_of(own, oth, scale, gain_own[...], gain_oth[...], up_own, up_oth)
    u_own, u_oth = (jnp.concatenate(part, axis=1) for part in halves_of(upstream[...].astype(F32), hi, at[0]))
    back_own = u_own + back_own
    back_oth = u_oth + back_oth
    half = own.shape[-1]
    r_own[...] = back_own
    r_oth[...] = back_oth
    low_out[:, :half] = back_own.astype(BF16)
    low_out[:, half:] = back_oth.astype(BF16)

    @pl.when(pl.program_id(0) == 0)
    def _():
        s_own[...] = jnp.zeros_like(s_own)
        s_oth[...] = jnp.zeros_like(s_oth)

    s_own[...] += jnp.sum(up_own * own * scale, axis=0, keepdims=True)
    s_oth[...] += jnp.sum(up_oth * oth * scale, axis=0, keepdims=True)


def grad_in_kernel(hi, at, x_own, x_oth, a0, a1, a2, b0, b1, b2, gain_own, gain_oth, r_own, r_oth, out):
    own, oth = x_own[...].astype(F32), x_oth[...].astype(F32)
    scale = rows_scale(own, oth)
    back_own, back_oth = back_of(
        own, oth, scale, gain_own[...], gain_oth[...], summed((a0, a1, a2)), summed((b0, b1, b2))
    )
    join_to(out, r_own[...] + back_own, r_oth[...] + back_oth, hi, at[0])


def project_kernel(n_own, n_oth, w_own, w_oth, out):
    out[...] = (dot(n_own[...], w_own[...]) + dot(n_oth[...], w_oth[...])).astype(out.dtype)


def put_rows(kept, sent, value):
    stay = pl.program_id(0) < pl.num_programs(0) // 2

    @pl.when(stay)
    def _():
        kept[...] = value

    @pl.when(jnp.logical_not(stay))
    def _():
        sent[...] = value


def project_back_kernel(rows, weight, kept, sent):
    put_rows(kept, sent, dot_rt(rows[...], weight[...]).astype(BF16))


def project_gain_kernel(grad, weight, normed, kept, sent, sums):
    part = dot_rt(grad[...], weight[...])
    put_rows(kept, sent, part.astype(BF16))

    @pl.when(pl.program_id(0) == 0)
    def _():
        sums[...] = jnp.zeros_like(sums)

    sums[...] += jnp.sum(part * normed[...].astype(F32), axis=0, keepdims=True)


def weight_grad_kernel(rows, grad, out):
    out[...] = dot_lt(rows[...], grad[...]).astype(out.dtype)


def weight_grad_add_kernel(rows, grad, came, out):
    out[...] = (dot_lt(rows[...], grad[...]) + came[...].astype(F32)).astype(BF16)


def add_kernel(first, second, out):
    out[...] = (first[...].astype(F32) + second[...].astype(F32)).astype(BF16)


def total_kernel(near, came, gains, out):
    depth = near.shape[0]
    out[:depth] = (near[...] + came[...].astype(F32)).astype(BF16)
    out[depth:] = gains[...]


def expand_kernel(n_own, n_oth, u_own, u_oth, gate_in, inner, for_gate, for_up):
    gate = gate_in[...]
    up = dot(n_own[...], u_own[...]) + dot(n_oth[...], u_oth[...])
    sigmoid = jax.nn.sigmoid(gate)
    active = gate * sigmoid
    inner[...] = (active * up).astype(BF16)
    for_gate[...] = (up * sigmoid * (1.0 + gate * (1.0 - sigmoid))).astype(BF16)
    for_up[...] = active.astype(BF16)


def inner_back_kernel(grad, weight, for_gate, for_up, gate_g, up_g):
    inner_g = dot(grad[...], weight[...])
    gate_g[...] = (inner_g * for_gate[...].astype(F32)).astype(BF16)
    up_g[...] = (inner_g * for_up[...].astype(F32)).astype(BF16)


def expand_back_kernel(gate_g, up_g, gate_w, up_w, kept, sent):
    put_rows(kept, sent, (dot_rt(gate_g[...], gate_w[...]) + dot_rt(up_g[...], up_w[...])).astype(BF16))


def partner(value):
    lane = lax.broadcasted_iota(jnp.int32, value.shape, 1)
    return jnp.where(lane % HD < HD // 2, pltpu.roll(value, PAIR - HD // 2, 1), pltpu.roll(value, HD // 2, 1))


def low_lanes(shape):
    return lax.broadcasted_iota(jnp.int32, shape, 1) < HD


def set_bias(bias, key_at, query_at, first):
    keys, queries = key_at[...], query_at[...]
    key_in = ((keys >= first) & (keys < first + SPAN)).astype(jnp.int32)
    query_in = ((queries >= first) & (queries < first + SPAN)).astype(jnp.int32)
    seen = (keys <= queries).astype(jnp.int32) + key_in * query_in
    bias[...] = jnp.where(seen > 0, 0.0, MASKED)


def attend_kernel(pairs, span, qkv, cos, sine, key_at, query_at, q_out, kv_out, o_out, lse_out, bias, key_s, val_s):
    length = cos.shape[0]
    set_bias(bias, key_at, query_at, span[pl.program_id(0)])
    kv = qkv[:, 0, :, pairs * PAIR :].reshape(length, PAIR)
    low = low_lanes(kv.shape)
    turned = kv * cos[...] + partner(kv) * sine[...]
    kv = jnp.where(low, turned, kv).astype(BF16)
    kv_out[:, 0] = kv.reshape(4, length // 4, PAIR)
    wide = kv.astype(F32)
    key_even = jnp.where(low, wide, 0.0)
    val_odd = jnp.where(low, 0.0, wide)
    key_s[0] = key_even.astype(BF16)
    key_s[1] = pltpu.roll(key_even, HD, 1).astype(BF16)
    val_s[0] = pltpu.roll(val_odd, HD, 1).T.astype(BF16)
    val_s[1] = val_odd.T.astype(BF16)

    def pair_step(j, _):
        cols = pl.ds(pl.multiple_of(j * PAIR, PAIR), PAIR)
        raw = qkv[:, 0, :, cols].reshape(length, PAIR)
        query = (raw * cos[...] + partner(raw) * sine[...]).astype(BF16)
        q_out[:, 0, :, cols] = query.reshape(4, length // 4, PAIR)
        query_t = (query.astype(F32) * HD**-0.5).T.astype(BF16)
        mixed = jnp.zeros((PAIR, length), F32)
        for k in range(2):
            scores = dot(key_s[k], query_t) + bias[...]
            top = jnp.max(scores, axis=0, keepdims=True)
            raised = jnp.exp(scores - top)
            total = jnp.sum(raised, axis=0, keepdims=True)
            lse_out[0, pl.ds(2 * j + k, 1), :] = top + jnp.log(total)
            mixed += dot(val_s[k], (raised * (1.0 / total)).astype(BF16))
        o_out[:, 0, :, cols] = mixed.T.astype(BF16).reshape(4, length // 4, PAIR)
        return 0

    lax.fori_loop(0, pairs, pair_step, 0)


def with_terms(rows, number):
    high = number.astype(BF16).astype(F32)
    middle = (number - high).astype(BF16).astype(F32)
    low = number - high - middle
    line = lax.broadcasted_iota(jnp.int32, (16, number.shape[1]), 0)
    terms = jnp.where(line == 0, high, jnp.where(line == 1, middle, jnp.where(line == 2, low, 0.0)))
    rest = jnp.zeros((HD - 16, number.shape[1]), BF16)
    return jnp.concatenate([rows.astype(BF16), terms.astype(BF16), rest], axis=0)


def attend_back_kernel(
    pairs, span, query_in, kv_in, grad_in, mixed_in, lse, cos, sine, key_at, query_at, out, bias, key_s, key_t, val_s, key_g, val_g
):
    length = cos.shape[0]
    scale = HD**-0.5
    set_bias(bias, key_at, query_at, span[pl.program_id(0)])
    kv = kv_in[:, 0].reshape(length, PAIR).astype(F32)
    low = low_lanes(kv.shape)
    lane = lax.broadcasted_iota(jnp.int32, kv.shape, 1)
    ones = jnp.where(lane < HD + 3, 1.0, 0.0)
    key_even = jnp.where(low, kv, 0.0)
    key_s[...] = jnp.where(low, kv, ones).astype(BF16)
    val_s[...] = jnp.where(low, pltpu.roll(kv, HD, 1) * scale, ones).astype(BF16)
    key_t[0] = key_even.T.astype(BF16)
    key_t[1] = pltpu.roll(key_even, HD, 1).T.astype(BF16)
    key_g[...] = jnp.zeros_like(key_g)
    val_g[...] = jnp.zeros_like(val_g)

    def pair_step(j, _):
        cols = pl.ds(pl.multiple_of(j * PAIR, PAIR), PAIR)
        query = query_in[:, 0, :, cols].reshape(length, PAIR)
        grad = grad_in[:, 0, :, cols].reshape(length, PAIR)
        mixed = mixed_in[:, 0, :, cols].reshape(length, PAIR)
        query_t = (query.astype(F32) * scale).T
        grad_t = grad.astype(F32).T
        product = grad_t * mixed.astype(F32).T
        query_g = jnp.zeros((PAIR, length), F32)
        for k in range(2):
            part = slice(k * HD, (k + 1) * HD)
            delta = jnp.sum(product[part], axis=0, keepdims=True) * scale
            scores = dot(key_s[...], with_terms(query_t[part], -lse[0, pl.ds(2 * j + k, 1), :]))
            weight = jnp.exp(scores + bias[...])
            weight_g = dot(val_s[...], with_terms(grad_t[part], -delta))
            val_g[k] += dot(weight.astype(BF16), grad)
            score_g = (weight * weight_g).astype(BF16)
            key_g[k] += dot(score_g, query)
            query_g += dot(key_t[k], score_g)
        value = query_g.T
        value = value * cos[...] - partner(value) * sine[...]
        out[:, 0, :, cols] = value.astype(BF16).reshape(4, length // 4, PAIR)
        return 0

    lax.fori_loop(0, pairs, pair_step, 0)
    keys = key_g[0] + pltpu.roll(key_g[1], HD, 1)
    vals = val_g[1] + pltpu.roll(val_g[0], HD, 1)
    keys = keys * cos[...] - partner(keys) * sine[...]
    out[:, 0, :, pairs * PAIR :] = jnp.where(low, keys, vals).astype(BF16).reshape(4, length // 4, PAIR)


def per_device(
    block_in, span_start, w_query, w_key, w_value, w_out, w_gate, w_up, w_down, gain_attn, gain_mlp, cotangent
):
    z, x, y, c = (lax.axis_index(name) for name in ("fh", "fl", "th", "tl"))
    hi = lax.axis_size("fh")
    batch, rows, width = block_in.shape
    own_rows, half = batch * rows, width // 2
    length = rows * 4
    depth = w_query.shape[0]
    q_cols, kv_cols = w_query.shape[1], w_key.shape[1]
    pairs = q_cols // PAIR
    at = jnp.stack([x]).astype(jnp.int32)

    shard = jnp.concatenate([w_query, w_key, w_value], axis=1)
    gains = jnp.concatenate([gain_attn, gain_mlp])[None]
    gains = jnp.pad(gains, ((0, ROW_PAD - 1), (0, shard.shape[1] - gains.shape[1])))
    shard = jnp.concatenate([shard, gains], axis=0)

    def gather(part):
        return lax.all_gather(part, "fh", axis=0, tiled=True)

    def swap_x(value):
        return swap(value, "fl")

    down_shard = w_down.T
    down_pair = jnp.concatenate([down_shard, swap_x(down_shard)], axis=0)
    attn_own, out_own, gate_own, up_own = gather(shard), gather(w_out.T), gather(w_gate), gather(w_up)
    down_w = gather(down_pair)

    def gather_rows(piece):
        beside = swap(piece, "tl")
        across = swap(piece, "th")
        return piece, across, beside, swap(across, "tl")

    token_parts = gather_rows(block_in.reshape(own_rows, width))
    cot_own = cotangent.reshape(own_rows, width)
    cot_parts = gather_rows(after(101, cot_own, token_parts[1]))

    place = jnp.concatenate(
        [(((y + dy) % 2) * 2 + (c + dc) % 2) * rows + jnp.arange(rows, dtype=jnp.int32) for dc in (0, 1) for dy in (0, 1)]
    )
    frequency = jnp.exp(jnp.arange(HD // 2, dtype=F32) * (-2.0 * math.log(10000.0) / HD))
    angles = place.astype(F32)[:, None] * frequency[None, :]
    cos = jnp.tile(jnp.cos(angles), (1, 4))
    sine = jnp.sin(angles)
    sine = jnp.concatenate([-sine, sine, -sine, sine], axis=1)
    key_at, query_at = place[:, None], place[None, :]
    span = span_start[:, 0]
    tables = [(t, full_spec(t.shape)) for t in (cos, sine, key_at, query_at)]

    quad = (4, batch, rows)
    all_rows = 4 * own_rows
    tile = 256
    steps = all_rows // tile
    hidden = w_gate.shape[1]
    all_cols = q_cols + 2 * kv_cols
    tiles = lambda *values: [(v, row_spec(tile, v.shape[1])) for v in values]
    wholes = lambda *values: [(v, whole_spec(v)) for v in values]
    pieces = lambda parts: [(p, row_spec(rows, width)) for p in parts]
    half_ins = lambda *values: [(v, row_spec(rows, half)) for v in values]
    gain_in = lambda gain: [(g, full_spec((1, half))) for g in gain]
    spread_outs = [(quad + (half,), BF16, quad_spec(rows, half))] * 2
    half_outs = [((own_rows, half), F32, row_spec(rows, half))] * 2
    low_out = [((own_rows, width), BF16, row_spec(rows, width))]
    whole_out = [((own_rows, width), F32, row_spec(rows, width))]
    sum_outs = [((1, half), F32, full_spec((1, half)))]
    hidden_out = ((all_rows, hidden), BF16, row_spec(tile, hidden))

    def tiles_of(size, *values):
        return [(v, row_spec(size, v.shape[1])) for v in values]

    def as_rows(value):
        return value.reshape(all_rows, value.shape[-1])

    def project(step, pair, weights, kind):
        cols = weights[0].shape[1]
        out = ((all_rows, cols), kind, row_spec(tile, cols))
        return call(step, project_kernel, [], steps, tiles(*pair) + wholes(*weights), [out])[0]

    def project_back(step, value, weight):
        outs = two_part_outs(all_rows, weight.shape[0], tile)
        return call(step, project_back_kernel, [], steps, tiles(value) + wholes(weight), outs)

    def weight_grad(step, value, grad, came=None, kind=BF16):
        part, cols = 256, grad.shape[1]
        ins = [(value, pl.BlockSpec((value.shape[0], part), lambda i: (0, i)))] + wholes(grad)
        ins += [] if came is None else [(came, row_spec(part, cols))]
        out = ((value.shape[1], cols), kind, row_spec(part, cols))
        kernel = weight_grad_kernel if came is None else weight_grad_add_kernel
        return call(step, kernel, [], value.shape[1] // part, ins, [out])[0]

    def scatter_rows(step, kept, sent, order=None, *others):
        cols = kept.shape[1]
        came = swap(sent, "tl")
        (passed,) = call(
            step,
            add_kernel,
            [],
            batch,
            [(kept, row_spec(rows, cols, batch)), (came, row_spec(rows, cols, batch))],
            [((own_rows, cols), BF16, row_spec(rows, cols))],
        )
        across = after(order, passed, *others) if others else passed
        return kept, came, swap(across, "th"), passed

    def terms(*scattered):
        return [(t, row_spec(rows, t.shape[1])) for part in scattered for t in part[:3]]

    def stack_rows(step, low, across, order, *others):
        beside, across = swap(low, "tl"), after(order, across, *others)
        parts = (low, across, beside, swap(across, "tl"))
        return tuple(as_rows(v) for v in call(step, stack_kernel, [], batch, pieces(parts), spread_outs))

    attn_own = after(102, attn_own, down_pair)
    attn_pair = tuple(part.reshape(hi, depth + ROW_PAD, -1) for part in (attn_own, swap_x(attn_own)))
    qkv_w = tuple(part[:, :depth].reshape(hi * depth, -1) for part in attn_pair)
    out_w = (out_own, swap_x(after(138, out_own, attn_pair[1])))
    gain_one = tuple(part[:, depth, :depth].reshape(1, half).astype(F32) for part in attn_pair)
    gain_two = tuple(part[:, depth, depth : 2 * depth].reshape(1, half).astype(F32) for part in attn_pair)

    *seq_one, x_own, x_oth = call(
        2,
        functools.partial(norm_in_kernel, hi),
        [at],
        batch,
        pieces(token_parts) + gain_in(gain_one),
        spread_outs + [((own_rows, half), BF16, row_spec(rows, half))] * 2,
    )
    seq_one = tuple(as_rows(v) for v in seq_one)
    gate_near = after(105, after(104, gate_own, out_w[1]), seq_one[0])
    gate_w = (gate_own, swap_x(gate_near))
    up_w = (up_own, swap_x(after(106, up_own, gate_w[1])))

    qkv = project(3, seq_one, qkv_w, F32)
    qkv = after(144, after(107, qkv, out_w[1]), cot_parts[1])
    pair_spec, q_spec = quad_spec(rows, PAIR), quad_spec(rows, q_cols)
    lse_spec = pl.BlockSpec((1, 2 * pairs, length), lambda i, *_: (i, 0, 0))
    query_rot, kv_rot, mixed, lse = call(
        4,
        functools.partial(attend_kernel, pairs),
        [span],
        batch,
        [(qkv.reshape(quad + (all_cols,)), quad_spec(rows, all_cols)), *tables],
        [
            (quad + (q_cols,), BF16, q_spec),
            (quad + (PAIR,), BF16, pair_spec),
            (quad + (q_cols,), BF16, q_spec),
            ((batch, 2 * pairs, length), F32, lse_spec),
        ],
        [
            pltpu.VMEM((length, length), F32),
            pltpu.VMEM((2, length, PAIR), BF16),
            pltpu.VMEM((2, PAIR, length), BF16),
        ],
    )
    mixed = as_rows(mixed)
    attn_oth = scatter_rows(6, *project_back(5, mixed, out_w[1]))
    attn_own = scatter_rows(8, *project_back(7, after(108, mixed, attn_oth[3]), out_w[0]))
    h_own, h_oth, normed_two = call(
        9,
        residual_kernel,
        [],
        batch,
        half_ins(after(109, x_own, gate_own), x_oth) + terms(attn_own, attn_oth) + gain_in(gain_two),
        half_outs + low_out,
    )
    (seq_cot,) = call(
        1,
        functools.partial(pairs_kernel, hi),
        [at],
        batch,
        pieces((after(103, cot_own, normed_two), *cot_parts[1:])),
        [(quad + (width,), BF16, quad_spec(rows, width))],
    )
    seq_cot = as_rows(seq_cot)
    seq_two = stack_rows(10, normed_two, swap(normed_two, "th"), 111, gate_w[1], seq_cot)
    gate_pre = project(38, seq_two, gate_w, F32)
    inner, for_gate, for_up = call(
        11, expand_kernel, [], steps, tiles(*seq_two) + wholes(*up_w) + tiles(gate_pre), [hidden_out] * 3
    )

    def reduce_z(total):
        return lax.psum_scatter(total, "fh", scatter_dimension=0, tiled=True)

    down_part = weight_grad(12, seq_cot, inner)
    grad_down = reduce_z(down_part)
    gate_g, up_g = call(
        13,
        inner_back_kernel,
        [],
        steps,
        tiles(after(112, seq_cot, down_part)) + wholes(down_w) + tiles(for_gate, for_up),
        [hidden_out] * 2,
    )

    def expand_back(step, which, gate_g):
        outs = two_part_outs(all_rows, half, tile)
        ins = tiles(gate_g, up_g) + wholes(gate_w[which], up_w[which])
        return call(step, expand_back_kernel, [], steps, ins, outs)

    gate_sent = weight_grad(16, seq_two[1], gate_g)
    gate_came = swap_x(gate_sent)
    oth_parts = expand_back(14, 1, after(113, gate_g, gate_sent))
    normed_oth = scatter_rows(15, *oth_parts)
    own_parts = expand_back(17, 0, after(116, after(115, gate_g, oth_parts[0]), normed_oth[3]))
    normed_own = scatter_rows(18, *own_parts)
    up_sent = weight_grad(19, seq_two[1], after(117, up_g, normed_own[3]))
    gate_came = after(158, after(147, gate_came, up_sent), oth_parts[0], own_parts[0])
    gate_came = after(149, after(148, gate_came, normed_oth[2]), normed_own[2])
    up_came = swap_x(after(122, up_sent, gate_came))
    gate_total = weight_grad(23, seq_two[0], gate_g, gate_came)
    grad_gate = reduce_z(gate_total)
    r_own, r_oth, attn_low, gain_s_own, gain_s_oth = call(
        20,
        functools.partial(middle_kernel, hi),
        [at],
        batch,
        half_ins(after(120, after(118, h_own, up_sent), gate_total), h_oth)
        + terms(normed_own, normed_oth)
        + gain_in(gain_two)
        + [(cot_own, row_spec(rows, width))],
        half_outs + low_out + sum_outs * 2,
    )
    block_parts = project_back(21, after(150, after(119, inner, attn_low), gate_total), down_w)

    attn_far = swap(attn_low, "th")
    up_came = after(127, after(126, up_came, block_parts[0]), grad_down)
    up_total = weight_grad(28, seq_two[0], up_g, up_came)
    grad_up = reduce_z(up_total)
    seq_attn = stack_rows(24, attn_low, attn_far, 123, up_total)
    block_terms = scatter_rows(22, block_parts[0], after(124, block_parts[1], seq_attn[0]), 160, attn_far)
    grad_mixed = project(25, seq_attn, out_w, BF16)
    out_sent = weight_grad(26, after(125, seq_attn[1], grad_mixed), mixed)
    out_came = swap_x(after(128, out_sent, up_came))
    grad_mixed = after(156, after(139, grad_mixed, out_sent), block_terms[3])
    (qkv_g,) = call(
        27,
        functools.partial(attend_back_kernel, pairs),
        [span],
        batch,
        [
            (query_rot, q_spec),
            (kv_rot, pair_spec),
            (grad_mixed.reshape(quad + (q_cols,)), q_spec),
            (mixed.reshape(quad + (q_cols,)), q_spec),
            (lse, lse_spec),
            *tables,
        ],
        [(quad + (all_cols,), BF16, quad_spec(rows, all_cols))],
        [
            pltpu.VMEM((length, length), F32),
            pltpu.VMEM((length, PAIR), BF16),
            pltpu.VMEM((2, PAIR, length), BF16),
            pltpu.VMEM((length, PAIR), BF16),
            pltpu.VMEM((2, length, PAIR), F32),
            pltpu.VMEM((2, length, PAIR), F32),
        ],
    )
    qkv_g = after(141, after(140, after(129, as_rows(qkv_g), out_came), block_terms[2]), grad_gate)

    def project_gain(step, which, grad):
        outs = two_part_outs(all_rows, half, tile) + sum_outs
        kept, sent, sums = call(
            step, project_gain_kernel, [], steps, tiles(grad) + wholes(qkv_w[which]) + tiles(seq_one[which]), outs
        )
        return (kept, sent), sums / gain_one[which]

    oth_parts, oth_gain = project_gain(29, 1, qkv_g)
    first_oth = scatter_rows(30, *oth_parts)
    qkv_sent = weight_grad(31, seq_one[1], after(167, after(161, after(130, qkv_g, oth_parts[0]), first_oth[3]), block_terms[2]))
    qkv_came = swap_x(after(134, qkv_sent, out_came))
    out_total = weight_grad(34, seq_attn[0], mixed, after(174, after(132, out_came, qkv_sent), first_oth[3]))
    grad_out = reduce_z(out_total)
    own_parts, own_gain = project_gain(32, 0, after(173, after(131, qkv_g, out_total), first_oth[3]))
    first_own = scatter_rows(33, *own_parts)
    qkv_near = weight_grad(35, seq_one[0], after(133, qkv_g, own_parts[0]), kind=F32)

    def gain_pair(one, two):
        return jnp.concatenate([one.reshape(hi, depth), two.reshape(hi, depth)], axis=1)

    gain_own, gain_oth = gain_pair(own_gain, gain_s_own), gain_pair(oth_gain, gain_s_oth)
    gain_both = jnp.stack([gain_own, gain_oth])
    gain_both = gain_both + swap(gain_both, "tl")
    gain_rows = gain_both[0] + swap_x(gain_both[1])
    gain_rows = jnp.pad(gain_rows[:, None], ((0, 0), (0, ROW_PAD - 1), (0, all_cols - 2 * depth))).astype(BF16)
    (qkv_total,) = call(
        39,
        total_kernel,
        [],
        hi,
        tiles_of(depth, qkv_near, after(170, after(152, after(151, after(135, qkv_came, grad_up), first_oth[2]), qkv_near), first_own[3]))
        + tiles_of(ROW_PAD, gain_rows.reshape(hi * ROW_PAD, all_cols)),
        [((hi * (depth + ROW_PAD), all_cols), BF16, row_spec(depth + ROW_PAD, all_cols))],
    )
    grad_qkv = reduce_z(qkv_total).astype(F32)
    gain_sums = grad_qkv[depth, : 2 * depth]
    gain_sums = gain_sums + swap(gain_sums, "th")
    grad_qkv = grad_qkv[:depth]
    (block_out,) = call(
        36,
        functools.partial(block_out_kernel, hi),
        [at],
        batch,
        half_ins(after(137, after(136, h_own, qkv_total), grad_up), h_oth) + terms(block_terms),
        whole_out,
    )

    (grad_in,) = call(
        37,
        functools.partial(grad_in_kernel, hi),
        [at],
        batch,
        half_ins(x_own, x_oth) + terms(first_own, first_oth) + gain_in(gain_one) + half_ins(r_own, r_oth),
        whole_out,
    )
    down_came = swap_x(grad_down[depth:])
    if 171 not in SKIP:
        down_came, block_out, grad_in = lax.optimization_barrier((down_came, block_out, grad_in))
    elif 172 not in SKIP:
        down_came, block_out = lax.optimization_barrier((down_came, block_out))
    grad_down = grad_down[:depth].astype(F32) + down_came.astype(F32)
    return (
        block_out.reshape(block_in.shape),
        grad_in.reshape(block_in.shape),
        grad_qkv[:, :q_cols],
        grad_qkv[:, q_cols : q_cols + kv_cols],
        grad_qkv[:, q_cols + kv_cols :],
        grad_out.astype(F32).T,
        grad_gate.astype(F32),
        grad_up.astype(F32),
        grad_down.T,
        gain_sums[:depth],
        gain_sums[depth:],
    )


def solution(mesh):
    n_fsdp, n_tp = mesh.shape["fsdp"], mesh.shape["tp"]
    fine = Mesh(mesh.devices.reshape(n_fsdp // 2, 2, n_tp // 2, 2), ("fh", "fl", "th", "tl"))
    fsdp, tp = ("fh", "fl"), ("th", "tl")
    rows = P(None, fsdp + tp, None)
    up, across, flat = P(fsdp, tp), P(tp, fsdp), P(fsdp)
    return jax.shard_map(
        per_device,
        mesh=fine,
        in_specs=(rows, P(None, fsdp), up, up, up, across, up, up, across, flat, flat, rows),
        out_specs=(rows, rows, up, up, up, across, up, up, across, flat, flat),
        check_vma=False,
    )
```

```python
import functools
import math

import jax
import jax.numpy as jnp
from jax import lax
from jax.experimental import pallas as pl
from jax.experimental.pallas import tpu as pltpu
from jax.sharding import Mesh, PartitionSpec as P

HD = 64
PAIR = 2 * HD
SPAN = 256
EPS = 1e-05
MASKED = -1e30
F32 = jnp.float32
BF16 = jnp.bfloat16
SWAP = [(0, 1), (1, 0)]
COST = {1: 1702, 2: 2220, 3: 2582, 4: 5630, 5: 1730, 6: 798, 7: 1730, 8: 798, 9: 1498, 10: 1626, 11: 4596, 12: 3950, 13: 4338, 14: 3898, 15: 798, 16: 2348, 17: 3872, 18: 798, 19: 2348, 20: 1986, 21: 3820, 22: 1006, 23: 2556, 24: 1626, 25: 2142, 26: 8118, 27: 127702, 28: 10228, 38: 3898}
SKIP = {136, 137, 139, 140, 142, 150, 158, 159, 161, 103, 170, 107, 174, 116, 120, 122}
ROW_PAD = 16


def dot(a, b):
    return jnp.dot(a, b, preferred_element_type=F32)


def dot_lt(a, b):
    return lax.dot_general(a, b, (((0,), (0,)), ((), ())), preferred_element_type=F32)


def dot_rt(a, b):
    return lax.dot_general(a, b, (((1,), (1,)), ((), ())), preferred_element_type=F32)


def swap(value, axis):
    return lax.ppermute(value, axis, SWAP)


def after(step, value, *others):
    if step in SKIP:
        return value
    return lax.optimization_barrier((value, *others))[0]


def full_spec(shape):
    return pl.BlockSpec(shape, lambda i, *_: (0,) * len(shape))


def row_spec(rows, cols, offset=0):
    return pl.BlockSpec((rows, cols), lambda i, *_: (i + offset, 0))


def quad_spec(rows, cols):
    return pl.BlockSpec((4, 1, rows, cols), lambda i, *_: (0, i, 0, 0))


def two_part_outs(rows, cols, tile):
    half = rows // tile // 2
    first = pl.BlockSpec((tile, cols), lambda i, *_: (jnp.minimum(i, half - 1), 0))
    second = pl.BlockSpec((tile, cols), lambda i, *_: (jnp.maximum(i - half, 0), 0))
    return [((rows // 2, cols), BF16, first), ((rows // 2, cols), BF16, second)]


def whole_spec(array):
    return pl.BlockSpec(array.shape, lambda i, *_: (0, 0), pipeline_mode=pl.Buffered(1))


def call(step, kernel, scalars, grid, ins, outs, scratch=()):
    work = COST.get(step, 0) * 1000
    return pl.pallas_call(
        kernel,
        out_shape=[jax.ShapeDtypeStruct(shape, kind) for shape, kind, _ in outs],
        grid_spec=pltpu.PrefetchScalarGridSpec(
            num_scalar_prefetch=len(scalars),
            grid=(grid,),
            in_specs=[spec for _, spec in ins],
            out_specs=[spec for _, _, spec in outs],
            scratch_shapes=list(scratch),
        ),
        cost_estimate=pl.CostEstimate(flops=work * 300, bytes_accessed=work + step, transcendentals=0),
        compiler_params=pltpu.CompilerParams(vmem_limit_bytes=48 << 20),
    )(*scalars, *[a for a, _ in ins])


def halves_of(value, hi, x):
    width = value.shape[-1] // (2 * hi)
    parts = [value[:, k * width : (k + 1) * width] for k in range(2 * hi)]
    even, odd = parts[0::2], parts[1::2]
    own = [jnp.where(x == 0, a, b) for a, b in zip(even, odd)]
    oth = [jnp.where(x == 0, b, a) for a, b in zip(even, odd)]
    return own, oth


def put_cols(ref, index, parts):
    width = parts[0].shape[-1]
    for k, part in enumerate(parts):
        ref[(*index, slice(None), slice(k * width, (k + 1) * width))] = part.astype(ref.dtype)


def join_to(ref, own, oth, hi, x):
    width = own.shape[-1] // hi
    for k in range(hi):
        a, b = own[:, k * width : (k + 1) * width], oth[:, k * width : (k + 1) * width]
        ref[:, 2 * k * width : (2 * k + 1) * width] = jnp.where(x == 0, a, b)
        ref[:, (2 * k + 1) * width : (2 * k + 2) * width] = jnp.where(x == 0, b, a)


def norm_in_kernel(hi, at, p0, p1, p2, p3, gain_own, gain_oth, n_own, n_oth, x_own, x_oth):
    x = at[0]
    half = n_own.shape[-1]
    for k, piece in enumerate((p0, p1, p2, p3)):
        low = piece[...]
        value = low.astype(F32)
        scale = lax.rsqrt(jnp.mean(value * value, axis=-1, keepdims=True) + EPS)
        own, oth = halves_of(value, hi, x)
        width = half // hi
        for part, gain, ref in ((own, gain_own, n_own), (oth, gain_oth, n_oth)):
            put_cols(
                ref, (k, 0), [v * scale * gain[:, z * width : (z + 1) * width] for z, v in enumerate(part)]
            )
        if k == 0:
            put_cols(x_own, (), own)
            put_cols(x_oth, (), oth)


def spread_kernel(hi, at, p0, p1, p2, p3, o_own, o_oth):
    x = at[0]
    for k, piece in enumerate((p0, p1, p2, p3)):
        own, oth = halves_of(piece[...], hi, x)
        put_cols(o_own, (k, 0), own)
        put_cols(o_oth, (k, 0), oth)


def pairs_kernel(hi, at, p0, p1, p2, p3, out):
    x = at[0]
    for k, piece in enumerate((p0, p1, p2, p3)):
        own, oth = halves_of(piece[...], hi, x)
        put_cols(out, (k, 0), [part for pair in zip(own, oth) for part in pair])


def stack_kernel(p0, p1, p2, p3, o_own, o_oth):
    half = o_own.shape[-1]
    for k, piece in enumerate((p0, p1, p2, p3)):
        o_own[k, 0] = piece[:, :half]
        o_oth[k, 0] = piece[:, half:]


def rows_scale(own, oth):
    total = jnp.sum(own * own, axis=-1, keepdims=True) + jnp.sum(oth * oth, axis=-1, keepdims=True)
    return lax.rsqrt(total / (own.shape[-1] + oth.shape[-1]) + EPS)


def summed(refs):
    return refs[0][...].astype(F32) + refs[1][...].astype(F32) + refs[2][...].astype(F32)


def residual_kernel(x_own, x_oth, a0, a1, a2, b0, b1, b2, gain_own, gain_oth, h_own, h_oth, n_out):
    own = x_own[...].astype(F32) + summed((a0, a1, a2))
    oth = x_oth[...].astype(F32) + summed((b0, b1, b2))
    scale = rows_scale(own, oth)
    half = own.shape[-1]
    h_own[...] = own
    h_oth[...] = oth
    n_out[:, :half] = (own * scale * gain_own[...]).astype(BF16)
    n_out[:, half:] = (oth * scale * gain_oth[...]).astype(BF16)


def block_out_kernel(hi, at, h_own, h_oth, t0, t1, t2, out):
    x = at[0]
    width = h_own.shape[-1] // hi
    for k in range(hi):
        cols = [slice(j * width, (j + 1) * width) for j in (2 * k, 2 * k + 1)]
        own, oth = (sum(t[:, col].astype(F32) for t in (t0, t1, t2)) for col in cols)
        own += h_own[:, k * width : (k + 1) * width]
        oth += h_oth[:, k * width : (k + 1) * width]
        out[:, cols[0]] = jnp.where(x == 0, own, oth)
        out[:, cols[1]] = jnp.where(x == 0, oth, own)


def back_of(own, oth, scale, gain_own, gain_oth, up_own, up_oth):
    w_own, w_oth = up_own * gain_own, up_oth * gain_oth
    total = jnp.sum(w_own * own, axis=-1, keepdims=True) + jnp.sum(w_oth * oth, axis=-1, keepdims=True)
    cube = scale * scale * scale * (total / (own.shape[-1] + oth.shape[-1]))
    return scale * w_own - own * cube, scale * w_oth - oth * cube


def middle_kernel(
    hi, at, h_own, h_oth, a0, a1, a2, b0, b1, b2, gain_own, gain_oth, upstream, r_own, r_oth, low_out, s_own, s_oth
):
    own, oth = h_own[...], h_oth[...]
    up_own, up_oth = summed((a0, a1, a2)), summed((b0, b1, b2))
    scale = rows_scale(own, oth)
    back_own, back_oth = back_of(own, oth, scale, gain_own[...], gain_oth[...], up_own, up_oth)
    u_own, u_oth = (jnp.concatenate(part, axis=1) for part in halves_of(upstream[...].astype(F32), hi, at[0]))
    back_own = u_own + back_own
    back_oth = u_oth + back_oth
    half = own.shape[-1]
    r_own[...] = back_own
    r_oth[...] = back_oth
    low_out[:, :half] = back_own.astype(BF16)
    low_out[:, half:] = back_oth.astype(BF16)

    @pl.when(pl.program_id(0) == 0)
    def _():
        s_own[...] = jnp.zeros_like(s_own)
        s_oth[...] = jnp.zeros_like(s_oth)

    s_own[...] += jnp.sum(up_own * own * scale, axis=0, keepdims=True)
    s_oth[...] += jnp.sum(up_oth * oth * scale, axis=0, keepdims=True)


def grad_in_kernel(hi, at, x_own, x_oth, a0, a1, a2, b0, b1, b2, gain_own, gain_oth, r_own, r_oth, out):
    own, oth = x_own[...].astype(F32), x_oth[...].astype(F32)
    scale = rows_scale(own, oth)
    back_own, back_oth = back_of(
        own, oth, scale, gain_own[...], gain_oth[...], summed((a0, a1, a2)), summed((b0, b1, b2))
    )
    join_to(out, r_own[...] + back_own, r_oth[...] + back_oth, hi, at[0])


def project_kernel(n_own, n_oth, w_own, w_oth, out):
    out[...] = (dot(n_own[...], w_own[...]) + dot(n_oth[...], w_oth[...])).astype(out.dtype)


def put_rows(kept, sent, value):
    stay = pl.program_id(0) < pl.num_programs(0) // 2

    @pl.when(stay)
    def _():
        kept[...] = value

    @pl.when(jnp.logical_not(stay))
    def _():
        sent[...] = value


def project_back_kernel(rows, weight, kept, sent):
    put_rows(kept, sent, dot_rt(rows[...], weight[...]).astype(BF16))


def project_gain_kernel(grad, weight, normed, kept, sent, sums):
    part = dot_rt(grad[...], weight[...])
    put_rows(kept, sent, part.astype(BF16))

    @pl.when(pl.program_id(0) == 0)
    def _():
        sums[...] = jnp.zeros_like(sums)

    sums[...] += jnp.sum(part * normed[...].astype(F32), axis=0, keepdims=True)


def weight_grad_kernel(rows, grad, out):
    out[...] = dot_lt(rows[...], grad[...]).astype(out.dtype)


def weight_grad_add_kernel(rows, grad, came, out):
    out[...] = (dot_lt(rows[...], grad[...]) + came[...].astype(F32)).astype(BF16)


def add_kernel(first, second, out):
    out[...] = (first[...].astype(F32) + second[...].astype(F32)).astype(BF16)


def total_kernel(near, came, gains, out):
    depth = near.shape[0]
    out[:depth] = (near[...] + came[...].astype(F32)).astype(BF16)
    out[depth:] = gains[...]


def expand_kernel(n_own, n_oth, u_own, u_oth, gate_in, inner, for_gate, for_up):
    gate = gate_in[...]
    up = dot(n_own[...], u_own[...]) + dot(n_oth[...], u_oth[...])
    sigmoid = jax.nn.sigmoid(gate)
    active = gate * sigmoid
    inner[...] = (active * up).astype(BF16)
    for_gate[...] = (up * sigmoid * (1.0 + gate * (1.0 - sigmoid))).astype(BF16)
    for_up[...] = active.astype(BF16)


def inner_back_kernel(grad, weight, for_gate, for_up, gate_g, up_g):
    inner_g = dot(grad[...], weight[...])
    gate_g[...] = (inner_g * for_gate[...].astype(F32)).astype(BF16)
    up_g[...] = (inner_g * for_up[...].astype(F32)).astype(BF16)


def expand_back_kernel(gate_g, up_g, gate_w, up_w, kept, sent):
    put_rows(kept, sent, (dot_rt(gate_g[...], gate_w[...]) + dot_rt(up_g[...], up_w[...])).astype(BF16))


def partner(value):
    lane = lax.broadcasted_iota(jnp.int32, value.shape, 1)
    return jnp.where(lane % HD < HD // 2, pltpu.roll(value, PAIR - HD // 2, 1), pltpu.roll(value, HD // 2, 1))


def low_lanes(shape):
    return lax.broadcasted_iota(jnp.int32, shape, 1) < HD


def set_bias(bias, key_at, query_at, first):
    keys, queries = key_at[...], query_at[...]
    key_in = ((keys >= first) & (keys < first + SPAN)).astype(jnp.int32)
    query_in = ((queries >= first) & (queries < first + SPAN)).astype(jnp.int32)
    seen = (keys <= queries).astype(jnp.int32) + key_in * query_in
    bias[...] = jnp.where(seen > 0, 0.0, MASKED)


def attend_kernel(pairs, span, qkv, cos, sine, key_at, query_at, q_out, kv_out, o_out, lse_out, bias, key_s, val_s):
    length = cos.shape[0]
    set_bias(bias, key_at, query_at, span[pl.program_id(0)])
    kv = qkv[:, 0, :, pairs * PAIR :].reshape(length, PAIR)
    low = low_lanes(kv.shape)
    turned = kv * cos[...] + partner(kv) * sine[...]
    kv = jnp.where(low, turned, kv).astype(BF16)
    kv_out[:, 0] = kv.reshape(4, length // 4, PAIR)
    wide = kv.astype(F32)
    key_even = jnp.where(low, wide, 0.0)
    val_odd = jnp.where(low, 0.0, wide)
    key_s[0] = key_even.astype(BF16)
    key_s[1] = pltpu.roll(key_even, HD, 1).astype(BF16)
    val_s[0] = pltpu.roll(val_odd, HD, 1).T.astype(BF16)
    val_s[1] = val_odd.T.astype(BF16)

    def pair_step(j, _):
        cols = pl.ds(pl.multiple_of(j * PAIR, PAIR), PAIR)
        raw = qkv[:, 0, :, cols].reshape(length, PAIR)
        query = (raw * cos[...] + partner(raw) * sine[...]).astype(BF16)
        q_out[:, 0, :, cols] = query.reshape(4, length // 4, PAIR)
        query_t = (query.astype(F32) * HD**-0.5).T.astype(BF16)
        mixed = jnp.zeros((PAIR, length), F32)
        for k in range(2):
            scores = dot(key_s[k], query_t) + bias[...]
            top = jnp.max(scores, axis=0, keepdims=True)
            raised = jnp.exp(scores - top)
            total = jnp.sum(raised, axis=0, keepdims=True)
            lse_out[0, pl.ds(2 * j + k, 1), :] = top + jnp.log(total)
            mixed += dot(val_s[k], (raised * (1.0 / total)).astype(BF16))
        o_out[:, 0, :, cols] = mixed.T.astype(BF16).reshape(4, length // 4, PAIR)
        return 0

    lax.fori_loop(0, pairs, pair_step, 0)


def with_terms(rows, number):
    high = number.astype(BF16).astype(F32)
    middle = (number - high).astype(BF16).astype(F32)
    low = number - high - middle
    line = lax.broadcasted_iota(jnp.int32, (16, number.shape[1]), 0)
    terms = jnp.where(line == 0, high, jnp.where(line == 1, middle, jnp.where(line == 2, low, 0.0)))
    rest = jnp.zeros((HD - 16, number.shape[1]), BF16)
    return jnp.concatenate([rows.astype(BF16), terms.astype(BF16), rest], axis=0)


def attend_back_kernel(
    pairs, span, query_in, kv_in, grad_in, mixed_in, lse, cos, sine, key_at, query_at, out, bias, key_s, key_t, val_s, key_g, val_g
):
    length = cos.shape[0]
    scale = HD**-0.5
    set_bias(bias, key_at, query_at, span[pl.program_id(0)])
    kv = kv_in[:, 0].reshape(length, PAIR).astype(F32)
    low = low_lanes(kv.shape)
    lane = lax.broadcasted_iota(jnp.int32, kv.shape, 1)
    ones = jnp.where(lane < HD + 3, 1.0, 0.0)
    key_even = jnp.where(low, kv, 0.0)
    key_s[...] = jnp.where(low, kv, ones).astype(BF16)
    val_s[...] = jnp.where(low, pltpu.roll(kv, HD, 1) * scale, ones).astype(BF16)
    key_t[0] = key_even.T.astype(BF16)
    key_t[1] = pltpu.roll(key_even, HD, 1).T.astype(BF16)
    key_g[...] = jnp.zeros_like(key_g)
    val_g[...] = jnp.zeros_like(val_g)

    def pair_step(j, _):
        cols = pl.ds(pl.multiple_of(j * PAIR, PAIR), PAIR)
        query = query_in[:, 0, :, cols].reshape(length, PAIR)
        grad = grad_in[:, 0, :, cols].reshape(length, PAIR)
        mixed = mixed_in[:, 0, :, cols].reshape(length, PAIR)
        query_t = (query.astype(F32) * scale).T
        grad_t = grad.astype(F32).T
        product = grad_t * mixed.astype(F32).T
        query_g = jnp.zeros((PAIR, length), F32)
        for k in range(2):
            part = slice(k * HD, (k + 1) * HD)
            delta = jnp.sum(product[part], axis=0, keepdims=True) * scale
            scores = dot(key_s[...], with_terms(query_t[part], -lse[0, pl.ds(2 * j + k, 1), :]))
            weight = jnp.exp(scores + bias[...])
            weight_g = dot(val_s[...], with_terms(grad_t[part], -delta))
            val_g[k] += dot(weight.astype(BF16), grad)
            score_g = (weight * weight_g).astype(BF16)
            key_g[k] += dot(score_g, query)
            query_g += dot(key_t[k], score_g)
        value = query_g.T
        value = value * cos[...] - partner(value) * sine[...]
        out[:, 0, :, cols] = value.astype(BF16).reshape(4, length // 4, PAIR)
        return 0

    lax.fori_loop(0, pairs, pair_step, 0)
    keys = key_g[0] + pltpu.roll(key_g[1], HD, 1)
    vals = val_g[1] + pltpu.roll(val_g[0], HD, 1)
    keys = keys * cos[...] - partner(keys) * sine[...]
    out[:, 0, :, pairs * PAIR :] = jnp.where(low, keys, vals).astype(BF16).reshape(4, length // 4, PAIR)


def per_device(
    block_in, span_start, w_query, w_key, w_value, w_out, w_gate, w_up, w_down, gain_attn, gain_mlp, cotangent
):
    z, x, y, c = (lax.axis_index(name) for name in ("fh", "fl", "th", "tl"))
    hi = lax.axis_size("fh")
    batch, rows, width = block_in.shape
    own_rows, half = batch * rows, width // 2
    length = rows * 4
    depth = w_query.shape[0]
    q_cols, kv_cols = w_query.shape[1], w_key.shape[1]
    pairs = q_cols // PAIR
    at = jnp.stack([x]).astype(jnp.int32)

    shard = jnp.concatenate([w_query, w_key, w_value], axis=1)
    gains = jnp.concatenate([gain_attn, gain_mlp])[None]
    gains = jnp.pad(gains, ((0, ROW_PAD - 1), (0, shard.shape[1] - gains.shape[1])))
    shard = jnp.concatenate([shard, gains], axis=0)

    def gather(part):
        return lax.all_gather(part, "fh", axis=0, tiled=True)

    def swap_x(value):
        return swap(value, "fl")

    down_shard = w_down.T
    down_pair = jnp.concatenate([down_shard, swap_x(down_shard)], axis=0)
    attn_own, out_own, gate_own, up_own = gather(shard), gather(w_out.T), gather(w_gate), gather(w_up)
    down_w = gather(down_pair)

    def gather_rows(piece):
        beside = swap(piece, "tl")
        across = swap(piece, "th")
        return piece, across, beside, swap(across, "tl")

    token_parts = gather_rows(block_in.reshape(own_rows, width))
    cot_own = cotangent.reshape(own_rows, width)
    cot_parts = gather_rows(after(101, cot_own, token_parts[1]))

    place = jnp.concatenate(
        [(((y + dy) % 2) * 2 + (c + dc) % 2) * rows + jnp.arange(rows, dtype=jnp.int32) for dc in (0, 1) for dy in (0, 1)]
    )
    frequency = jnp.exp(jnp.arange(HD // 2, dtype=F32) * (-2.0 * math.log(10000.0) / HD))
    angles = place.astype(F32)[:, None] * frequency[None, :]
    cos = jnp.tile(jnp.cos(angles), (1, 4))
    sine = jnp.sin(angles)
    sine = jnp.concatenate([-sine, sine, -sine, sine], axis=1)
    key_at, query_at = place[:, None], place[None, :]
    span = span_start[:, 0]
    tables = [(t, full_spec(t.shape)) for t in (cos, sine, key_at, query_at)]

    quad = (4, batch, rows)
    all_rows = 4 * own_rows
    tile = 256
    steps = all_rows // tile
    hidden = w_gate.shape[1]
    all_cols = q_cols + 2 * kv_cols
    tiles = lambda *values: [(v, row_spec(tile, v.shape[1])) for v in values]
    wholes = lambda *values: [(v, whole_spec(v)) for v in values]
    pieces = lambda parts: [(p, row_spec(rows, width)) for p in parts]
    half_ins = lambda *values: [(v, row_spec(rows, half)) for v in values]
    gain_in = lambda gain: [(g, full_spec((1, half))) for g in gain]
    spread_outs = [(quad + (half,), BF16, quad_spec(rows, half))] * 2
    half_outs = [((own_rows, half), F32, row_spec(rows, half))] * 2
    low_out = [((own_rows, width), BF16, row_spec(rows, width))]
    whole_out = [((own_rows, width), F32, row_spec(rows, width))]
    sum_outs = [((1, half), F32, full_spec((1, half)))]
    hidden_out = ((all_rows, hidden), BF16, row_spec(tile, hidden))

    def tiles_of(size, *values):
        return [(v, row_spec(size, v.shape[1])) for v in values]

    def as_rows(value):
        return value.reshape(all_rows, value.shape[-1])

    def project(step, pair, weights, kind):
        cols = weights[0].shape[1]
        out = ((all_rows, cols), kind, row_spec(tile, cols))
        return call(step, project_kernel, [], steps, tiles(*pair) + wholes(*weights), [out])[0]

    def project_back(step, value, weight):
        outs = two_part_outs(all_rows, weight.shape[0], tile)
        return call(step, project_back_kernel, [], steps, tiles(value) + wholes(weight), outs)

    def weight_grad(step, value, grad, came=None, kind=BF16):
        part, cols = 256, grad.shape[1]
        ins = [(value, pl.BlockSpec((value.shape[0], part), lambda i: (0, i)))] + wholes(grad)
        ins += [] if came is None else [(came, row_spec(part, cols))]
        out = ((value.shape[1], cols), kind, row_spec(part, cols))
        kernel = weight_grad_kernel if came is None else weight_grad_add_kernel
        return call(step, kernel, [], value.shape[1] // part, ins, [out])[0]

    def scatter_rows(step, kept, sent, order=None, *others):
        cols = kept.shape[1]
        came = swap(sent, "tl")
        (passed,) = call(
            step,
            add_kernel,
            [],
            batch,
            [(kept, row_spec(rows, cols, batch)), (came, row_spec(rows, cols, batch))],
            [((own_rows, cols), BF16, row_spec(rows, cols))],
        )
        across = after(order, passed, *others) if others else passed
        return kept, came, swap(across, "th"), passed

    def terms(*scattered):
        return [(t, row_spec(rows, t.shape[1])) for part in scattered for t in part[:3]]

    def stack_rows(step, low, across, order, *others):
        beside, across = swap(low, "tl"), after(order, across, *others)
        parts = (low, across, beside, swap(across, "tl"))
        return tuple(as_rows(v) for v in call(step, stack_kernel, [], batch, pieces(parts), spread_outs))

    attn_own = after(102, attn_own, down_pair)
    attn_pair = tuple(part.reshape(hi, depth + ROW_PAD, -1) for part in (attn_own, swap_x(attn_own)))
    qkv_w = tuple(part[:, :depth].reshape(hi * depth, -1) for part in attn_pair)
    out_w = (out_own, swap_x(after(138, out_own, attn_pair[1])))
    gain_one = tuple(part[:, depth, :depth].reshape(1, half).astype(F32) for part in attn_pair)
    gain_two = tuple(part[:, depth, depth : 2 * depth].reshape(1, half).astype(F32) for part in attn_pair)

    *seq_one, x_own, x_oth = call(
        2,
        functools.partial(norm_in_kernel, hi),
        [at],
        batch,
        pieces(token_parts) + gain_in(gain_one),
        spread_outs + [((own_rows, half), BF16, row_spec(rows, half))] * 2,
    )
    seq_one = tuple(as_rows(v) for v in seq_one)
    gate_near = after(105, after(104, gate_own, out_w[1]), seq_one[0])
    gate_w = (gate_own, swap_x(gate_near))
    up_w = (up_own, swap_x(after(106, up_own, gate_w[1])))

    qkv = project(3, seq_one, qkv_w, F32)
    qkv = after(144, after(107, qkv, out_w[1]), cot_parts[1])
    pair_spec, q_spec = quad_spec(rows, PAIR), quad_spec(rows, q_cols)
    lse_spec = pl.BlockSpec((1, 2 * pairs, length), lambda i, *_: (i, 0, 0))
    query_rot, kv_rot, mixed, lse = call(
        4,
        functools.partial(attend_kernel, pairs),
        [span],
        batch,
        [(qkv.reshape(quad + (all_cols,)), quad_spec(rows, all_cols)), *tables],
        [
            (quad + (q_cols,), BF16, q_spec),
            (quad + (PAIR,), BF16, pair_spec),
            (quad + (q_cols,), BF16, q_spec),
            ((batch, 2 * pairs, length), F32, lse_spec),
        ],
        [
            pltpu.VMEM((length, length), F32),
            pltpu.VMEM((2, length, PAIR), BF16),
            pltpu.VMEM((2, PAIR, length), BF16),
        ],
    )
    mixed = as_rows(mixed)
    attn_oth = scatter_rows(6, *project_back(5, mixed, out_w[1]))
    attn_own = scatter_rows(8, *project_back(7, after(108, mixed, attn_oth[3]), out_w[0]))
    h_own, h_oth, normed_two = call(
        9,
        residual_kernel,
        [],
        batch,
        half_ins(after(109, x_own, gate_own), x_oth) + terms(attn_own, attn_oth) + gain_in(gain_two),
        half_outs + low_out,
    )
    (seq_cot,) = call(
        1,
        functools.partial(pairs_kernel, hi),
        [at],
        batch,
        pieces((after(103, cot_own, normed_two), *cot_parts[1:])),
        [(quad + (width,), BF16, quad_spec(rows, width))],
    )
    seq_cot = as_rows(seq_cot)
    seq_two = stack_rows(10, normed_two, swap(normed_two, "th"), 111, gate_w[1], seq_cot)
    gate_pre = project(38, seq_two, gate_w, F32)
    inner, for_gate, for_up = call(
        11, expand_kernel, [], steps, tiles(*seq_two) + wholes(*up_w) + tiles(gate_pre), [hidden_out] * 3
    )

    def reduce_z(total):
        return lax.psum_scatter(total, "fh", scatter_dimension=0, tiled=True)

    down_part = weight_grad(12, seq_cot, inner)
    grad_down = reduce_z(down_part)
    gate_g, up_g = call(
        13,
        inner_back_kernel,
        [],
        steps,
        tiles(after(112, seq_cot, down_part)) + wholes(down_w) + tiles(for_gate, for_up),
        [hidden_out] * 2,
    )

    def expand_back(step, which, gate_g):
        outs = two_part_outs(all_rows, half, tile)
        ins = tiles(gate_g, up_g) + wholes(gate_w[which], up_w[which])
        return call(step, expand_back_kernel, [], steps, ins, outs)

    gate_sent = weight_grad(16, seq_two[1], gate_g)
    gate_came = swap_x(gate_sent)
    oth_parts = expand_back(14, 1, after(113, gate_g, gate_sent))
    normed_oth = scatter_rows(15, *oth_parts)
    own_parts = expand_back(17, 0, after(116, after(115, gate_g, oth_parts[0]), normed_oth[3]))
    normed_own = scatter_rows(18, *own_parts)
    up_sent = weight_grad(19, seq_two[1], after(117, up_g, normed_own[3]))
    gate_came = after(158, after(147, gate_came, up_sent), oth_parts[0], own_parts[0])
    gate_came = after(149, after(148, gate_came, normed_oth[2]), normed_own[2])
    up_came = swap_x(after(122, up_sent, gate_came))
    gate_total = weight_grad(23, seq_two[0], gate_g, gate_came)
    grad_gate = reduce_z(gate_total)
    r_own, r_oth, attn_low, gain_s_own, gain_s_oth = call(
        20,
        functools.partial(middle_kernel, hi),
        [at],
        batch,
        half_ins(after(120, after(118, h_own, up_sent), gate_total), h_oth)
        + terms(normed_own, normed_oth)
        + gain_in(gain_two)
        + [(cot_own, row_spec(rows, width))],
        half_outs + low_out + sum_outs * 2,
    )
    block_parts = project_back(21, after(150, after(119, inner, attn_low), gate_total), down_w)

    attn_far = swap(attn_low, "th")
    up_came = after(127, after(126, up_came, block_parts[0]), grad_down)
    up_total = weight_grad(28, seq_two[0], up_g, up_came)
    grad_up = reduce_z(up_total)
    seq_attn = stack_rows(24, attn_low, attn_far, 123, up_total)
    block_terms = scatter_rows(22, block_parts[0], after(124, block_parts[1], seq_attn[0]), 160, attn_far)
    grad_mixed = project(25, seq_attn, out_w, BF16)
    out_sent = weight_grad(26, after(125, seq_attn[1], grad_mixed), mixed)
    out_came = swap_x(after(128, out_sent, up_came))
    grad_mixed = after(156, after(139, grad_mixed, out_sent), block_terms[3])
    (qkv_g,) = call(
        27,
        functools.partial(attend_back_kernel, pairs),
        [span],
        batch,
        [
            (query_rot, q_spec),
            (kv_rot, pair_spec),
            (grad_mixed.reshape(quad + (q_cols,)), q_spec),
            (mixed.reshape(quad + (q_cols,)), q_spec),
            (lse, lse_spec),
            *tables,
        ],
        [(quad + (all_cols,), BF16, quad_spec(rows, all_cols))],
        [
            pltpu.VMEM((length, length), F32),
            pltpu.VMEM((length, PAIR), BF16),
            pltpu.VMEM((2, PAIR, length), BF16),
            pltpu.VMEM((length, PAIR), BF16),
            pltpu.VMEM((2, length, PAIR), F32),
            pltpu.VMEM((2, length, PAIR), F32),
        ],
    )
    qkv_g = after(141, after(140, after(129, as_rows(qkv_g), out_came), block_terms[2]), grad_gate)

    def project_gain(step, which, grad):
        outs = two_part_outs(all_rows, half, tile) + sum_outs
        kept, sent, sums = call(
            step, project_gain_kernel, [], steps, tiles(grad) + wholes(qkv_w[which]) + tiles(seq_one[which]), outs
        )
        return (kept, sent), sums / gain_one[which]

    oth_parts, oth_gain = project_gain(29, 1, qkv_g)
    first_oth = scatter_rows(30, *oth_parts)
    qkv_sent = weight_grad(31, seq_one[1], after(167, after(161, after(130, qkv_g, oth_parts[0]), first_oth[3]), block_terms[2]))
    qkv_came = swap_x(after(134, qkv_sent, out_came))
    out_total = weight_grad(34, seq_attn[0], mixed, after(174, after(132, out_came, qkv_sent), first_oth[3]))
    grad_out = reduce_z(out_total)
    own_parts, own_gain = project_gain(32, 0, after(173, after(131, qkv_g, out_total), first_oth[3]))
    first_own = scatter_rows(33, *own_parts)
    qkv_near = weight_grad(35, seq_one[0], after(133, qkv_g, own_parts[0]), kind=F32)

    def gain_pair(one, two):
        return jnp.concatenate([one.reshape(hi, depth), two.reshape(hi, depth)], axis=1)

    gain_own, gain_oth = gain_pair(own_gain, gain_s_own), gain_pair(oth_gain, gain_s_oth)
    gain_both = jnp.stack([gain_own, gain_oth])
    gain_both = gain_both + swap(gain_both, "tl")
    gain_rows = gain_both[0] + swap_x(gain_both[1])
    gain_rows = jnp.pad(gain_rows[:, None], ((0, 0), (0, ROW_PAD - 1), (0, all_cols - 2 * depth))).astype(BF16)
    (qkv_total,) = call(
        39,
        total_kernel,
        [],
        hi,
        tiles_of(depth, qkv_near, after(170, after(152, after(151, after(135, qkv_came, grad_up), first_oth[2]), qkv_near), first_own[3]))
        + tiles_of(ROW_PAD, gain_rows.reshape(hi * ROW_PAD, all_cols)),
        [((hi * (depth + ROW_PAD), all_cols), BF16, row_spec(depth + ROW_PAD, all_cols))],
    )
    grad_qkv = reduce_z(qkv_total).astype(F32)
    gain_sums = grad_qkv[depth, : 2 * depth]
    gain_sums = gain_sums + swap(gain_sums, "th")
    grad_qkv = grad_qkv[:depth]
    (block_out,) = call(
        36,
        functools.partial(block_out_kernel, hi),
        [at],
        batch,
        half_ins(after(137, after(136, h_own, qkv_total), grad_up), h_oth) + terms(block_terms),
        whole_out,
    )

    (grad_in,) = call(
        37,
        functools.partial(grad_in_kernel, hi),
        [at],
        batch,
        half_ins(x_own, x_oth) + terms(first_own, first_oth) + gain_in(gain_one) + half_ins(r_own, r_oth),
        whole_out,
    )
    down_came = swap_x(grad_down[depth:])
    if 171 not in SKIP:
        down_came, block_out, grad_in = lax.optimization_barrier((down_came, block_out, grad_in))
    elif 172 not in SKIP:
        down_came, block_out = lax.optimization_barrier((down_came, block_out))
    grad_down = grad_down[:depth].astype(F32) + down_came.astype(F32)
    return (
        block_out.reshape(block_in.shape),
        grad_in.reshape(block_in.shape),
        grad_qkv[:, :q_cols],
        grad_qkv[:, q_cols : q_cols + kv_cols],
        grad_qkv[:, q_cols + kv_cols :],
        grad_out.astype(F32).T,
        grad_gate.astype(F32),
        grad_up.astype(F32),
        grad_down.T,
        gain_sums[:depth],
        gain_sums[depth:],
    )


def solution(mesh):
    n_fsdp, n_tp = mesh.shape["fsdp"], mesh.shape["tp"]
    fine = Mesh(mesh.devices.reshape(n_fsdp // 2, 2, n_tp // 2, 2), ("fh", "fl", "th", "tl"))
    fsdp, tp = ("fh", "fl"), ("th", "tl")
    rows = P(None, fsdp + tp, None)
    up, across, flat = P(fsdp, tp), P(tp, fsdp), P(fsdp)
    return jax.shard_map(
        per_device,
        mesh=fine,
        in_specs=(rows, P(None, fsdp), up, up, up, across, up, up, across, flat, flat, rows),
        out_specs=(rows, rows, up, up, up, across, up, up, across, flat, flat),
        check_vma=False,
    )
```

```python
import functools
import math

import jax
import jax.numpy as jnp
from jax import lax
from jax.experimental import pallas as pl
from jax.experimental.pallas import tpu as pltpu
from jax.sharding import Mesh, PartitionSpec as P

HD = 64
PAIR = 2 * HD
SPAN = 256
EPS = 1e-05
MASKED = -1e30
F32 = jnp.float32
BF16 = jnp.bfloat16
SWAP = [(0, 1), (1, 0)]
COST = {1: 1702, 2: 2220, 3: 2582, 4: 5630, 5: 1730, 6: 798, 7: 1730, 8: 798, 9: 1498, 10: 1626, 11: 4596, 12: 3950, 13: 4338, 14: 3898, 15: 798, 16: 2348, 17: 3872, 18: 798, 19: 2348, 20: 1986, 21: 3820, 22: 1006, 23: 2556, 24: 1626, 25: 2142, 26: 8118, 27: 127702, 28: 10228, 38: 3898}
SKIP = {136, 137, 139, 140, 142, 150, 158, 159, 161, 103, 170, 107, 174, 116, 120, 122}
ROW_PAD = 16


def dot(a, b):
    return jnp.dot(a, b, preferred_element_type=F32)


def dot_lt(a, b):
    return lax.dot_general(a, b, (((0,), (0,)), ((), ())), preferred_element_type=F32)


def dot_rt(a, b):
    return lax.dot_general(a, b, (((1,), (1,)), ((), ())), preferred_element_type=F32)


def swap(value, axis):
    return lax.ppermute(value, axis, SWAP)


def after(step, value, *others):
    if step in SKIP:
        return value
    return lax.optimization_barrier((value, *others))[0]


def full_spec(shape):
    return pl.BlockSpec(shape, lambda i, *_: (0,) * len(shape))


def row_spec(rows, cols, offset=0):
    return pl.BlockSpec((rows, cols), lambda i, *_: (i + offset, 0))


def quad_spec(rows, cols):
    return pl.BlockSpec((4, 1, rows, cols), lambda i, *_: (0, i, 0, 0))


def two_part_outs(rows, cols, tile):
    half = rows // tile // 2
    first = pl.BlockSpec((tile, cols), lambda i, *_: (jnp.minimum(i, half - 1), 0))
    second = pl.BlockSpec((tile, cols), lambda i, *_: (jnp.maximum(i - half, 0), 0))
    return [((rows // 2, cols), BF16, first), ((rows // 2, cols), BF16, second)]


def whole_spec(array):
    return pl.BlockSpec(array.shape, lambda i, *_: (0, 0), pipeline_mode=pl.Buffered(1))


def call(step, kernel, scalars, grid, ins, outs, scratch=()):
    work = COST.get(step, 0) * 1000
    return pl.pallas_call(
        kernel,
        out_shape=[jax.ShapeDtypeStruct(shape, kind) for shape, kind, _ in outs],
        grid_spec=pltpu.PrefetchScalarGridSpec(
            num_scalar_prefetch=len(scalars),
            grid=(grid,),
            in_specs=[spec for _, spec in ins],
            out_specs=[spec for _, _, spec in outs],
            scratch_shapes=list(scratch),
        ),
        cost_estimate=pl.CostEstimate(flops=work * 300, bytes_accessed=work + step, transcendentals=0),
        compiler_params=pltpu.CompilerParams(vmem_limit_bytes=53 << 20),
    )(*scalars, *[a for a, _ in ins])


def halves_of(value, hi, x):
    width = value.shape[-1] // (2 * hi)
    parts = [value[:, k * width : (k + 1) * width] for k in range(2 * hi)]
    even, odd = parts[0::2], parts[1::2]
    own = [jnp.where(x == 0, a, b) for a, b in zip(even, odd)]
    oth = [jnp.where(x == 0, b, a) for a, b in zip(even, odd)]
    return own, oth


def put_cols(ref, index, parts):
    width = parts[0].shape[-1]
    for k, part in enumerate(parts):
        ref[(*index, slice(None), slice(k * width, (k + 1) * width))] = part.astype(ref.dtype)


def join_to(ref, own, oth, hi, x):
    width = own.shape[-1] // hi
    for k in range(hi):
        a, b = own[:, k * width : (k + 1) * width], oth[:, k * width : (k + 1) * width]
        ref[:, 2 * k * width : (2 * k + 1) * width] = jnp.where(x == 0, a, b)
        ref[:, (2 * k + 1) * width : (2 * k + 2) * width] = jnp.where(x == 0, b, a)


def norm_in_kernel(hi, at, p0, p1, p2, p3, gain_own, gain_oth, n_own, n_oth, x_own, x_oth):
    x = at[0]
    half = n_own.shape[-1]
    for k, piece in enumerate((p0, p1, p2, p3)):
        low = piece[...]
        value = low.astype(F32)
        scale = lax.rsqrt(jnp.mean(value * value, axis=-1, keepdims=True) + EPS)
        own, oth = halves_of(value, hi, x)
        width = half // hi
        for part, gain, ref in ((own, gain_own, n_own), (oth, gain_oth, n_oth)):
            put_cols(
                ref, (k, 0), [v * scale * gain[:, z * width : (z + 1) * width] for z, v in enumerate(part)]
            )
        if k == 0:
            put_cols(x_own, (), own)
            put_cols(x_oth, (), oth)


def spread_kernel(hi, at, p0, p1, p2, p3, o_own, o_oth):
    x = at[0]
    for k, piece in enumerate((p0, p1, p2, p3)):
        own, oth = halves_of(piece[...], hi, x)
        put_cols(o_own, (k, 0), own)
        put_cols(o_oth, (k, 0), oth)


def pairs_kernel(hi, at, p0, p1, p2, p3, out):
    x = at[0]
    for k, piece in enumerate((p0, p1, p2, p3)):
        own, oth = halves_of(piece[...], hi, x)
        put_cols(out, (k, 0), [part for pair in zip(own, oth) for part in pair])


def stack_kernel(p0, p1, p2, p3, o_own, o_oth):
    half = o_own.shape[-1]
    for k, piece in enumerate((p0, p1, p2, p3)):
        o_own[k, 0] = piece[:, :half]
        o_oth[k, 0] = piece[:, half:]


def rows_scale(own, oth):
    total = jnp.sum(own * own, axis=-1, keepdims=True) + jnp.sum(oth * oth, axis=-1, keepdims=True)
    return lax.rsqrt(total / (own.shape[-1] + oth.shape[-1]) + EPS)


def summed(refs):
    return refs[0][...].astype(F32) + refs[1][...].astype(F32) + refs[2][...].astype(F32)


def residual_kernel(x_own, x_oth, a0, a1, a2, b0, b1, b2, gain_own, gain_oth, h_own, h_oth, n_out):
    own = x_own[...].astype(F32) + summed((a0, a1, a2))
    oth = x_oth[...].astype(F32) + summed((b0, b1, b2))
    scale = rows_scale(own, oth)
    half = own.shape[-1]
    h_own[...] = own
    h_oth[...] = oth
    n_out[:, :half] = (own * scale * gain_own[...]).astype(BF16)
    n_out[:, half:] = (oth * scale * gain_oth[...]).astype(BF16)


def block_out_kernel(hi, at, h_own, h_oth, t0, t1, t2, out):
    x = at[0]
    width = h_own.shape[-1] // hi
    for k in range(hi):
        cols = [slice(j * width, (j + 1) * width) for j in (2 * k, 2 * k + 1)]
        own, oth = (sum(t[:, col].astype(F32) for t in (t0, t1, t2)) for col in cols)
        own += h_own[:, k * width : (k + 1) * width]
        oth += h_oth[:, k * width : (k + 1) * width]
        out[:, cols[0]] = jnp.where(x == 0, own, oth)
        out[:, cols[1]] = jnp.where(x == 0, oth, own)


def back_of(own, oth, scale, gain_own, gain_oth, up_own, up_oth):
    w_own, w_oth = up_own * gain_own, up_oth * gain_oth
    total = jnp.sum(w_own * own, axis=-1, keepdims=True) + jnp.sum(w_oth * oth, axis=-1, keepdims=True)
    cube = scale * scale * scale * (total / (own.shape[-1] + oth.shape[-1]))
    return scale * w_own - own * cube, scale * w_oth - oth * cube


def middle_kernel(
    hi, at, h_own, h_oth, a0, a1, a2, b0, b1, b2, gain_own, gain_oth, upstream, r_own, r_oth, low_out, s_own, s_oth
):
    own, oth = h_own[...], h_oth[...]
    up_own, up_oth = summed((a0, a1, a2)), summed((b0, b1, b2))
    scale = rows_scale(own, oth)
    back_own, back_oth = back_of(own, oth, scale, gain_own[...], gain_oth[...], up_own, up_oth)
    u_own, u_oth = (jnp.concatenate(part, axis=1) for part in halves_of(upstream[...].astype(F32), hi, at[0]))
    back_own = u_own + back_own
    back_oth = u_oth + back_oth
    half = own.shape[-1]
    r_own[...] = back_own
    r_oth[...] = back_oth
    low_out[:, :half] = back_own.astype(BF16)
    low_out[:, half:] = back_oth.astype(BF16)

    @pl.when(pl.program_id(0) == 0)
    def _():
        s_own[...] = jnp.zeros_like(s_own)
        s_oth[...] = jnp.zeros_like(s_oth)

    s_own[...] += jnp.sum(up_own * own * scale, axis=0, keepdims=True)
    s_oth[...] += jnp.sum(up_oth * oth * scale, axis=0, keepdims=True)


def grad_in_kernel(hi, at, x_own, x_oth, a0, a1, a2, b0, b1, b2, gain_own, gain_oth, r_own, r_oth, out):
    own, oth = x_own[...].astype(F32), x_oth[...].astype(F32)
    scale = rows_scale(own, oth)
    back_own, back_oth = back_of(
        own, oth, scale, gain_own[...], gain_oth[...], summed((a0, a1, a2)), summed((b0, b1, b2))
    )
    join_to(out, r_own[...] + back_own, r_oth[...] + back_oth, hi, at[0])


def project_kernel(n_own, n_oth, w_own, w_oth, out):
    out[...] = (dot(n_own[...], w_own[...]) + dot(n_oth[...], w_oth[...])).astype(out.dtype)


def put_rows(kept, sent, value):
    stay = pl.program_id(0) < pl.num_programs(0) // 2

    @pl.when(stay)
    def _():
        kept[...] = value

    @pl.when(jnp.logical_not(stay))
    def _():
        sent[...] = value


def project_back_kernel(rows, weight, kept, sent):
    put_rows(kept, sent, dot_rt(rows[...], weight[...]).astype(BF16))


def project_gain_kernel(grad, weight, normed, kept, sent, sums):
    part = dot_rt(grad[...], weight[...])
    put_rows(kept, sent, part.astype(BF16))

    @pl.when(pl.program_id(0) == 0)
    def _():
        sums[...] = jnp.zeros_like(sums)

    sums[...] += jnp.sum(part * normed[...].astype(F32), axis=0, keepdims=True)


def weight_grad_kernel(rows, grad, out):
    out[...] = dot_lt(rows[...], grad[...]).astype(out.dtype)


def weight_grad_add_kernel(rows, grad, came, out):
    out[...] = (dot_lt(rows[...], grad[...]) + came[...].astype(F32)).astype(BF16)


def add_kernel(first, second, out):
    out[...] = (first[...].astype(F32) + second[...].astype(F32)).astype(BF16)


def total_kernel(near, came, gains, out):
    depth = near.shape[0]
    out[:depth] = (near[...] + came[...].astype(F32)).astype(BF16)
    out[depth:] = gains[...]


def expand_kernel(n_own, n_oth, u_own, u_oth, gate_in, inner, for_gate, for_up):
    gate = gate_in[...]
    up = dot(n_own[...], u_own[...]) + dot(n_oth[...], u_oth[...])
    sigmoid = jax.nn.sigmoid(gate)
    active = gate * sigmoid
    inner[...] = (active * up).astype(BF16)
    for_gate[...] = (up * sigmoid * (1.0 + gate * (1.0 - sigmoid))).astype(BF16)
    for_up[...] = active.astype(BF16)


def inner_back_kernel(grad, weight, for_gate, for_up, gate_g, up_g):
    inner_g = dot(grad[...], weight[...])
    gate_g[...] = (inner_g * for_gate[...].astype(F32)).astype(BF16)
    up_g[...] = (inner_g * for_up[...].astype(F32)).astype(BF16)


def expand_back_kernel(gate_g, up_g, gate_w, up_w, kept, sent):
    put_rows(kept, sent, (dot_rt(gate_g[...], gate_w[...]) + dot_rt(up_g[...], up_w[...])).astype(BF16))


def partner(value):
    lane = lax.broadcasted_iota(jnp.int32, value.shape, 1)
    return jnp.where(lane % HD < HD // 2, pltpu.roll(value, PAIR - HD // 2, 1), pltpu.roll(value, HD // 2, 1))


def low_lanes(shape):
    return lax.broadcasted_iota(jnp.int32, shape, 1) < HD


def set_bias(bias, key_at, query_at, first):
    keys, queries = key_at[...], query_at[...]
    key_in = ((keys >= first) & (keys < first + SPAN)).astype(jnp.int32)
    query_in = ((queries >= first) & (queries < first + SPAN)).astype(jnp.int32)
    seen = (keys <= queries).astype(jnp.int32) + key_in * query_in
    bias[...] = jnp.where(seen > 0, 0.0, MASKED)


def attend_kernel(pairs, span, qkv, cos, sine, key_at, query_at, q_out, kv_out, o_out, lse_out, bias, key_s, val_s):
    length = cos.shape[0]
    set_bias(bias, key_at, query_at, span[pl.program_id(0)])
    kv = qkv[:, 0, :, pairs * PAIR :].reshape(length, PAIR)
    low = low_lanes(kv.shape)
    turned = kv * cos[...] + partner(kv) * sine[...]
    kv = jnp.where(low, turned, kv).astype(BF16)
    kv_out[:, 0] = kv.reshape(4, length // 4, PAIR)
    wide = kv.astype(F32)
    key_even = jnp.where(low, wide, 0.0)
    val_odd = jnp.where(low, 0.0, wide)
    key_s[0] = key_even.astype(BF16)
    key_s[1] = pltpu.roll(key_even, HD, 1).astype(BF16)
    val_s[0] = pltpu.roll(val_odd, HD, 1).T.astype(BF16)
    val_s[1] = val_odd.T.astype(BF16)

    def pair_step(j, _):
        cols = pl.ds(pl.multiple_of(j * PAIR, PAIR), PAIR)
        raw = qkv[:, 0, :, cols].reshape(length, PAIR)
        query = (raw * cos[...] + partner(raw) * sine[...]).astype(BF16)
        q_out[:, 0, :, cols] = query.reshape(4, length // 4, PAIR)
        query_t = (query.astype(F32) * HD**-0.5).T.astype(BF16)
        mixed = jnp.zeros((PAIR, length), F32)
        for k in range(2):
            scores = dot(key_s[k], query_t) + bias[...]
            top = jnp.max(scores, axis=0, keepdims=True)
            raised = jnp.exp(scores - top)
            total = jnp.sum(raised, axis=0, keepdims=True)
            lse_out[0, pl.ds(2 * j + k, 1), :] = top + jnp.log(total)
            mixed += dot(val_s[k], (raised * (1.0 / total)).astype(BF16))
        o_out[:, 0, :, cols] = mixed.T.astype(BF16).reshape(4, length // 4, PAIR)
        return 0

    lax.fori_loop(0, pairs, pair_step, 0)


def with_terms(rows, number):
    high = number.astype(BF16).astype(F32)
    middle = (number - high).astype(BF16).astype(F32)
    low = number - high - middle
    line = lax.broadcasted_iota(jnp.int32, (16, number.shape[1]), 0)
    terms = jnp.where(line == 0, high, jnp.where(line == 1, middle, jnp.where(line == 2, low, 0.0)))
    rest = jnp.zeros((HD - 16, number.shape[1]), BF16)
    return jnp.concatenate([rows.astype(BF16), terms.astype(BF16), rest], axis=0)


def attend_back_kernel(
    pairs, span, query_in, kv_in, grad_in, mixed_in, lse, cos, sine, key_at, query_at, out, bias, key_s, key_t, val_s, key_g, val_g
):
    length = cos.shape[0]
    scale = HD**-0.5
    set_bias(bias, key_at, query_at, span[pl.program_id(0)])
    kv = kv_in[:, 0].reshape(length, PAIR).astype(F32)
    low = low_lanes(kv.shape)
    lane = lax.broadcasted_iota(jnp.int32, kv.shape, 1)
    ones = jnp.where(lane < HD + 3, 1.0, 0.0)
    key_even = jnp.where(low, kv, 0.0)
    key_s[...] = jnp.where(low, kv, ones).astype(BF16)
    val_s[...] = jnp.where(low, pltpu.roll(kv, HD, 1) * scale, ones).astype(BF16)
    key_t[0] = key_even.T.astype(BF16)
    key_t[1] = pltpu.roll(key_even, HD, 1).T.astype(BF16)
    key_g[...] = jnp.zeros_like(key_g)
    val_g[...] = jnp.zeros_like(val_g)

    def pair_step(j, _):
        cols = pl.ds(pl.multiple_of(j * PAIR, PAIR), PAIR)
        query = query_in[:, 0, :, cols].reshape(length, PAIR)
        grad = grad_in[:, 0, :, cols].reshape(length, PAIR)
        mixed = mixed_in[:, 0, :, cols].reshape(length, PAIR)
        query_t = (query.astype(F32) * scale).T
        grad_t = grad.astype(F32).T
        product = grad_t * mixed.astype(F32).T
        query_g = jnp.zeros((PAIR, length), F32)
        for k in range(2):
            part = slice(k * HD, (k + 1) * HD)
            delta = jnp.sum(product[part], axis=0, keepdims=True) * scale
            scores = dot(key_s[...], with_terms(query_t[part], -lse[0, pl.ds(2 * j + k, 1), :]))
            weight = jnp.exp(scores + bias[...])
            weight_g = dot(val_s[...], with_terms(grad_t[part], -delta))
            val_g[k] += dot(weight.astype(BF16), grad)
            score_g = (weight * weight_g).astype(BF16)
            key_g[k] += dot(score_g, query)
            query_g += dot(key_t[k], score_g)
        value = query_g.T
        value = value * cos[...] - partner(value) * sine[...]
        out[:, 0, :, cols] = value.astype(BF16).reshape(4, length // 4, PAIR)
        return 0

    lax.fori_loop(0, pairs, pair_step, 0)
    keys = key_g[0] + pltpu.roll(key_g[1], HD, 1)
    vals = val_g[1] + pltpu.roll(val_g[0], HD, 1)
    keys = keys * cos[...] - partner(keys) * sine[...]
    out[:, 0, :, pairs * PAIR :] = jnp.where(low, keys, vals).astype(BF16).reshape(4, length // 4, PAIR)


def per_device(
    block_in, span_start, w_query, w_key, w_value, w_out, w_gate, w_up, w_down, gain_attn, gain_mlp, cotangent
):
    z, x, y, c = (lax.axis_index(name) for name in ("fh", "fl", "th", "tl"))
    hi = lax.axis_size("fh")
    batch, rows, width = block_in.shape
    own_rows, half = batch * rows, width // 2
    length = rows * 4
    depth = w_query.shape[0]
    q_cols, kv_cols = w_query.shape[1], w_key.shape[1]
    pairs = q_cols // PAIR
    at = jnp.stack([x]).astype(jnp.int32)

    shard = jnp.concatenate([w_query, w_key, w_value], axis=1)
    gains = jnp.concatenate([gain_attn, gain_mlp])[None]
    gains = jnp.pad(gains, ((0, ROW_PAD - 1), (0, shard.shape[1] - gains.shape[1])))
    shard = jnp.concatenate([shard, gains], axis=0)

    def gather(part):
        return lax.all_gather(part, "fh", axis=0, tiled=True)

    def swap_x(value):
        return swap(value, "fl")

    down_shard = w_down.T
    down_pair = jnp.concatenate([down_shard, swap_x(down_shard)], axis=0)
    attn_own, out_own, gate_own, up_own = gather(shard), gather(w_out.T), gather(w_gate), gather(w_up)
    down_w = gather(down_pair)

    def gather_rows(piece):
        beside = swap(piece, "tl")
        across = swap(piece, "th")
        return piece, across, beside, swap(across, "tl")

    token_parts = gather_rows(block_in.reshape(own_rows, width))
    cot_own = cotangent.reshape(own_rows, width)
    cot_parts = gather_rows(after(101, cot_own, token_parts[1]))

    place = jnp.concatenate(
        [(((y + dy) % 2) * 2 + (c + dc) % 2) * rows + jnp.arange(rows, dtype=jnp.int32) for dc in (0, 1) for dy in (0, 1)]
    )
    frequency = jnp.exp(jnp.arange(HD // 2, dtype=F32) * (-2.0 * math.log(10000.0) / HD))
    angles = place.astype(F32)[:, None] * frequency[None, :]
    cos = jnp.tile(jnp.cos(angles), (1, 4))
    sine = jnp.sin(angles)
    sine = jnp.concatenate([-sine, sine, -sine, sine], axis=1)
    key_at, query_at = place[:, None], place[None, :]
    span = span_start[:, 0]
    tables = [(t, full_spec(t.shape)) for t in (cos, sine, key_at, query_at)]

    quad = (4, batch, rows)
    all_rows = 4 * own_rows
    tile = 256
    steps = all_rows // tile
    hidden = w_gate.shape[1]
    all_cols = q_cols + 2 * kv_cols
    tiles = lambda *values: [(v, row_spec(tile, v.shape[1])) for v in values]
    wholes = lambda *values: [(v, whole_spec(v)) for v in values]
    pieces = lambda parts: [(p, row_spec(rows, width)) for p in parts]
    half_ins = lambda *values: [(v, row_spec(rows, half)) for v in values]
    gain_in = lambda gain: [(g, full_spec((1, half))) for g in gain]
    spread_outs = [(quad + (half,), BF16, quad_spec(rows, half))] * 2
    half_outs = [((own_rows, half), F32, row_spec(rows, half))] * 2
    low_out = [((own_rows, width), BF16, row_spec(rows, width))]
    whole_out = [((own_rows, width), F32, row_spec(rows, width))]
    sum_outs = [((1, half), F32, full_spec((1, half)))]
    hidden_out = ((all_rows, hidden), BF16, row_spec(tile, hidden))

    def tiles_of(size, *values):
        return [(v, row_spec(size, v.shape[1])) for v in values]

    def as_rows(value):
        return value.reshape(all_rows, value.shape[-1])

    def project(step, pair, weights, kind):
        cols = weights[0].shape[1]
        out = ((all_rows, cols), kind, row_spec(tile, cols))
        return call(step, project_kernel, [], steps, tiles(*pair) + wholes(*weights), [out])[0]

    def project_back(step, value, weight):
        outs = two_part_outs(all_rows, weight.shape[0], tile)
        return call(step, project_back_kernel, [], steps, tiles(value) + wholes(weight), outs)

    def weight_grad(step, value, grad, came=None, kind=BF16):
        part, cols = 256, grad.shape[1]
        ins = [(value, pl.BlockSpec((value.shape[0], part), lambda i: (0, i)))] + wholes(grad)
        ins += [] if came is None else [(came, row_spec(part, cols))]
        out = ((value.shape[1], cols), kind, row_spec(part, cols))
        kernel = weight_grad_kernel if came is None else weight_grad_add_kernel
        return call(step, kernel, [], value.shape[1] // part, ins, [out])[0]

    def scatter_rows(step, kept, sent, order=None, *others):
        cols = kept.shape[1]
        came = swap(sent, "tl")
        (passed,) = call(
            step,
            add_kernel,
            [],
            batch,
            [(kept, row_spec(rows, cols, batch)), (came, row_spec(rows, cols, batch))],
            [((own_rows, cols), BF16, row_spec(rows, cols))],
        )
        across = after(order, passed, *others) if others else passed
        return kept, came, swap(across, "th"), passed

    def terms(*scattered):
        return [(t, row_spec(rows, t.shape[1])) for part in scattered for t in part[:3]]

    def stack_rows(step, low, across, order, *others):
        beside, across = swap(low, "tl"), after(order, across, *others)
        parts = (low, across, beside, swap(across, "tl"))
        return tuple(as_rows(v) for v in call(step, stack_kernel, [], batch, pieces(parts), spread_outs))

    attn_own = after(102, attn_own, down_pair)
    attn_pair = tuple(part.reshape(hi, depth + ROW_PAD, -1) for part in (attn_own, swap_x(attn_own)))
    qkv_w = tuple(part[:, :depth].reshape(hi * depth, -1) for part in attn_pair)
    out_w = (out_own, swap_x(after(138, out_own, attn_pair[1])))
    gain_one = tuple(part[:, depth, :depth].reshape(1, half).astype(F32) for part in attn_pair)
    gain_two = tuple(part[:, depth, depth : 2 * depth].reshape(1, half).astype(F32) for part in attn_pair)

    *seq_one, x_own, x_oth = call(
        2,
        functools.partial(norm_in_kernel, hi),
        [at],
        batch,
        pieces(token_parts) + gain_in(gain_one),
        spread_outs + [((own_rows, half), BF16, row_spec(rows, half))] * 2,
    )
    seq_one = tuple(as_rows(v) for v in seq_one)
    gate_near = after(105, after(104, gate_own, out_w[1]), seq_one[0])
    gate_w = (gate_own, swap_x(gate_near))
    up_w = (up_own, swap_x(after(106, up_own, gate_w[1])))

    qkv = project(3, seq_one, qkv_w, F32)
    qkv = after(144, after(107, qkv, out_w[1]), cot_parts[1])
    pair_spec, q_spec = quad_spec(rows, PAIR), quad_spec(rows, q_cols)
    lse_spec = pl.BlockSpec((1, 2 * pairs, length), lambda i, *_: (i, 0, 0))
    query_rot, kv_rot, mixed, lse = call(
        4,
        functools.partial(attend_kernel, pairs),
        [span],
        batch,
        [(qkv.reshape(quad + (all_cols,)), quad_spec(rows, all_cols)), *tables],
        [
            (quad + (q_cols,), BF16, q_spec),
            (quad + (PAIR,), BF16, pair_spec),
            (quad + (q_cols,), BF16, q_spec),
            ((batch, 2 * pairs, length), F32, lse_spec),
        ],
        [
            pltpu.VMEM((length, length), F32),
            pltpu.VMEM((2, length, PAIR), BF16),
            pltpu.VMEM((2, PAIR, length), BF16),
        ],
    )
    mixed = as_rows(mixed)
    attn_oth = scatter_rows(6, *project_back(5, mixed, out_w[1]))
    attn_own = scatter_rows(8, *project_back(7, after(108, mixed, attn_oth[3]), out_w[0]))
    h_own, h_oth, normed_two = call(
        9,
        residual_kernel,
        [],
        batch,
        half_ins(after(109, x_own, gate_own), x_oth) + terms(attn_own, attn_oth) + gain_in(gain_two),
        half_outs + low_out,
    )
    (seq_cot,) = call(
        1,
        functools.partial(pairs_kernel, hi),
        [at],
        batch,
        pieces((after(103, cot_own, normed_two), *cot_parts[1:])),
        [(quad + (width,), BF16, quad_spec(rows, width))],
    )
    seq_cot = as_rows(seq_cot)
    seq_two = stack_rows(10, normed_two, swap(normed_two, "th"), 111, gate_w[1], seq_cot)
    gate_pre = project(38, seq_two, gate_w, F32)
    inner, for_gate, for_up = call(
        11, expand_kernel, [], steps, tiles(*seq_two) + wholes(*up_w) + tiles(gate_pre), [hidden_out] * 3
    )

    def reduce_z(total):
        return lax.psum_scatter(total, "fh", scatter_dimension=0, tiled=True)

    down_part = weight_grad(12, seq_cot, inner)
    grad_down = reduce_z(down_part)
    gate_g, up_g = call(
        13,
        inner_back_kernel,
        [],
        steps,
        tiles(after(112, seq_cot, down_part)) + wholes(down_w) + tiles(for_gate, for_up),
        [hidden_out] * 2,
    )

    def expand_back(step, which, gate_g):
        outs = two_part_outs(all_rows, half, tile)
        ins = tiles(gate_g, up_g) + wholes(gate_w[which], up_w[which])
        return call(step, expand_back_kernel, [], steps, ins, outs)

    gate_sent = weight_grad(16, seq_two[1], gate_g)
    gate_came = swap_x(gate_sent)
    oth_parts = expand_back(14, 1, after(113, gate_g, gate_sent))
    normed_oth = scatter_rows(15, *oth_parts)
    own_parts = expand_back(17, 0, after(116, after(115, gate_g, oth_parts[0]), normed_oth[3]))
    normed_own = scatter_rows(18, *own_parts)
    up_sent = weight_grad(19, seq_two[1], after(117, up_g, normed_own[3]))
    gate_came = after(158, after(147, gate_came, up_sent), oth_parts[0], own_parts[0])
    gate_came = after(149, after(148, gate_came, normed_oth[2]), normed_own[2])
    up_came = swap_x(after(122, up_sent, gate_came))
    gate_total = weight_grad(23, seq_two[0], gate_g, gate_came)
    grad_gate = reduce_z(gate_total)
    r_own, r_oth, attn_low, gain_s_own, gain_s_oth = call(
        20,
        functools.partial(middle_kernel, hi),
        [at],
        batch,
        half_ins(after(120, after(118, h_own, up_sent), gate_total), h_oth)
        + terms(normed_own, normed_oth)
        + gain_in(gain_two)
        + [(cot_own, row_spec(rows, width))],
        half_outs + low_out + sum_outs * 2,
    )
    block_parts = project_back(21, after(150, after(119, inner, attn_low), gate_total), down_w)

    attn_far = swap(attn_low, "th")
    up_came = after(127, after(126, up_came, block_parts[0]), grad_down)
    up_total = weight_grad(28, seq_two[0], up_g, up_came)
    grad_up = reduce_z(up_total)
    seq_attn = stack_rows(24, attn_low, attn_far, 123, up_total)
    block_terms = scatter_rows(22, block_parts[0], after(124, block_parts[1], seq_attn[0]), 160, attn_far)
    grad_mixed = project(25, seq_attn, out_w, BF16)
    out_sent = weight_grad(26, after(125, seq_attn[1], grad_mixed), mixed)
    out_came = swap_x(after(128, out_sent, up_came))
    grad_mixed = after(156, after(139, grad_mixed, out_sent), block_terms[3])
    (qkv_g,) = call(
        27,
        functools.partial(attend_back_kernel, pairs),
        [span],
        batch,
        [
            (query_rot, q_spec),
            (kv_rot, pair_spec),
            (grad_mixed.reshape(quad + (q_cols,)), q_spec),
            (mixed.reshape(quad + (q_cols,)), q_spec),
            (lse, lse_spec),
            *tables,
        ],
        [(quad + (all_cols,), BF16, quad_spec(rows, all_cols))],
        [
            pltpu.VMEM((length, length), F32),
            pltpu.VMEM((length, PAIR), BF16),
            pltpu.VMEM((2, PAIR, length), BF16),
            pltpu.VMEM((length, PAIR), BF16),
            pltpu.VMEM((2, length, PAIR), F32),
            pltpu.VMEM((2, length, PAIR), F32),
        ],
    )
    qkv_g = after(141, after(140, after(129, as_rows(qkv_g), out_came), block_terms[2]), grad_gate)

    def project_gain(step, which, grad):
        outs = two_part_outs(all_rows, half, tile) + sum_outs
        kept, sent, sums = call(
            step, project_gain_kernel, [], steps, tiles(grad) + wholes(qkv_w[which]) + tiles(seq_one[which]), outs
        )
        return (kept, sent), sums / gain_one[which]

    oth_parts, oth_gain = project_gain(29, 1, qkv_g)
    first_oth = scatter_rows(30, *oth_parts)
    qkv_sent = weight_grad(31, seq_one[1], after(167, after(161, after(130, qkv_g, oth_parts[0]), first_oth[3]), block_terms[2]))
    qkv_came = swap_x(after(134, qkv_sent, out_came))
    out_total = weight_grad(34, seq_attn[0], mixed, after(174, after(132, out_came, qkv_sent), first_oth[3]))
    grad_out = reduce_z(out_total)
    own_parts, own_gain = project_gain(32, 0, after(173, after(131, qkv_g, out_total), first_oth[3]))
    first_own = scatter_rows(33, *own_parts)
    qkv_near = weight_grad(35, seq_one[0], after(133, qkv_g, own_parts[0]), kind=F32)

    def gain_pair(one, two):
        return jnp.concatenate([one.reshape(hi, depth), two.reshape(hi, depth)], axis=1)

    gain_own, gain_oth = gain_pair(own_gain, gain_s_own), gain_pair(oth_gain, gain_s_oth)
    gain_both = jnp.stack([gain_own, gain_oth])
    gain_both = gain_both + swap(gain_both, "tl")
    gain_rows = gain_both[0] + swap_x(gain_both[1])
    gain_rows = jnp.pad(gain_rows[:, None], ((0, 0), (0, ROW_PAD - 1), (0, all_cols - 2 * depth))).astype(BF16)
    (qkv_total,) = call(
        39,
        total_kernel,
        [],
        hi,
        tiles_of(depth, qkv_near, after(170, after(152, after(151, after(135, qkv_came, grad_up), first_oth[2]), qkv_near), first_own[3]))
        + tiles_of(ROW_PAD, gain_rows.reshape(hi * ROW_PAD, all_cols)),
        [((hi * (depth + ROW_PAD), all_cols), BF16, row_spec(depth + ROW_PAD, all_cols))],
    )
    grad_qkv = reduce_z(qkv_total).astype(F32)
    gain_sums = grad_qkv[depth, : 2 * depth]
    gain_sums = gain_sums + swap(gain_sums, "th")
    grad_qkv = grad_qkv[:depth]
    (block_out,) = call(
        36,
        functools.partial(block_out_kernel, hi),
        [at],
        batch,
        half_ins(after(137, after(136, h_own, qkv_total), grad_up), h_oth) + terms(block_terms),
        whole_out,
    )

    (grad_in,) = call(
        37,
        functools.partial(grad_in_kernel, hi),
        [at],
        batch,
        half_ins(x_own, x_oth) + terms(first_own, first_oth) + gain_in(gain_one) + half_ins(r_own, r_oth),
        whole_out,
    )
    down_came = swap_x(grad_down[depth:])
    if 171 not in SKIP:
        down_came, block_out, grad_in = lax.optimization_barrier((down_came, block_out, grad_in))
    elif 172 not in SKIP:
        down_came, block_out = lax.optimization_barrier((down_came, block_out))
    grad_down = grad_down[:depth].astype(F32) + down_came.astype(F32)
    return (
        block_out.reshape(block_in.shape),
        grad_in.reshape(block_in.shape),
        grad_qkv[:, :q_cols],
        grad_qkv[:, q_cols : q_cols + kv_cols],
        grad_qkv[:, q_cols + kv_cols :],
        grad_out.astype(F32).T,
        grad_gate.astype(F32),
        grad_up.astype(F32),
        grad_down.T,
        gain_sums[:depth],
        gain_sums[depth:],
    )


def solution(mesh):
    n_fsdp, n_tp = mesh.shape["fsdp"], mesh.shape["tp"]
    fine = Mesh(mesh.devices.reshape(n_fsdp // 2, 2, n_tp // 2, 2), ("fh", "fl", "th", "tl"))
    fsdp, tp = ("fh", "fl"), ("th", "tl")
    rows = P(None, fsdp + tp, None)
    up, across, flat = P(fsdp, tp), P(tp, fsdp), P(fsdp)
    return jax.shard_map(
        per_device,
        mesh=fine,
        in_specs=(rows, P(None, fsdp), up, up, up, across, up, up, across, flat, flat, rows),
        out_specs=(rows, rows, up, up, up, across, up, up, across, flat, flat),
        check_vma=False,
    )
```
